32 devices in a mesh: depth: 4 (over y, x), lat: 8 (over z, core).
Axes of the slice: x: 2, y: 2, z: 4, core: 2. Of those that a mesh axis runs over, the one named last changes fastest.
Arguments:
- operator: float32 [4, 40, 9, 256, 128], P('depth', 'lat'), may hold values from -0.125 to 0.125
- band_shift: int32 [4, 40], P('depth', 'lat'), may hold values from -1 to 1, as said below
- reflectivity: float32 [4, 5120], P('depth', 'lat'), may hold values from -0.4 to 0.4
- up_stored: float32 [4, 5120, 128], P('depth', 'lat'), may hold values from -6 to 6
- down_stored: float32 [4, 5120, 128], P('depth', 'lat'), may hold values from -6 to 6
- sources: float32 [5120, 128], P('lat'), may hold values from -6 to 6
- assignment: int32 [64], replicated, may hold values from 0 to 63, each once
Outputs:
- down_fields: float32 [4, 5120, 128], P('depth', 'lat')
- up_fields: float32 [4, 5120, 128], P('depth', 'lat')
The draws below stay inside these ranges and needn't reach their ends.
Inputs may be any that keep to these rules, and one draw needn't show every extreme that they name: `band_shift`: in every section some tile row has -1 and some has +1.
All inputs are finite; a program needn't handle non-finite values.
Results may differ from the reference program's by a relative error of at most 0.00013.
Values sent between devices are 32-bit elements; how exact they have to be, the bound alone decides.
No kernel may reach another device: no remote copies, remote signals or barrier semaphores. Data moves between devices by JAX's collectives and lax.ppermute only.
A program may use at most 64 MiB of HBM per device.

```python
import jax
import jax.numpy as jnp
from jax import lax

TILE = 128
SHOTS = 32
SECTIONS = 4
LAT_TILES = 40
LAT = 5120
COLS = 128


def draw_band_shift(key, part):
    base = jax.random.fold_in(key, 11)
    key_a, key_b, key_c = jax.random.split(base, 3)
    values = jax.random.randint(key_a, (SECTIONS, LAT_TILES), -1, 2)
    low_at = jax.random.randint(key_b, (SECTIONS,), 0, LAT_TILES)
    high_at = (low_at + 1 + jax.random.randint(key_c, (SECTIONS,), 0, LAT_TILES - 1)) % LAT_TILES
    column_ids = jnp.arange(LAT_TILES)[None, :]
    values = jnp.where(column_ids == low_at[:, None], -1, values)
    values = jnp.where(column_ids == high_at[:, None], 1, values)
    return values.astype(jnp.int32)


def shard_levels(stream_key, dims, cuts, least, high):
    level = 1.0
    for dim, parts in cuts:
        heights = jax.random.uniform(jax.random.fold_in(jax.random.fold_in(stream_key, 6), dim), (parts,), jnp.float32, least / len(cuts), high / len(cuts))
        level = level * jnp.repeat(jnp.exp(heights), dims[dim] // parts).reshape((-1,) + (1,) * (len(dims) - 1 - dim))
    return level


def noise(own_key, shape, scale, most, shards=(), kind=jnp.bfloat16):
    loudness = shard_levels(own_key, shape, shards, -0.22, 0.18) if shards else 1.0
    array = jax.random.normal(own_key, shape, jnp.float32) * scale * loudness
    return jnp.minimum(jnp.maximum(array, -most), most).astype(kind)


def setup_inputs(seed: int = 0) -> dict:
    key_of = jax.random.split(jax.random.key(seed), 8)
    operator = noise(key_of[0], (SECTIONS, LAT_TILES, 9, 2 * TILE, TILE), (2 * 9 * TILE) ** -0.5, 0.125, ((0, 4), (1, 8)), jnp.float32)
    band_shift = draw_band_shift(jax.random.fold_in(key_of[7], 71), 0)
    reflectivity = jnp.clip(jax.random.uniform(key_of[2], (SECTIONS, LAT), jnp.float32, -0.4, 0.4) * shard_levels(key_of[2], (SECTIONS, LAT), ((0, 4), (1, 8)), -0.4, 0.0), -0.4, 0.4)
    up_stored = noise(key_of[3], (SECTIONS, LAT, COLS), 1.0, 6.0, ((0, 4), (1, 8)), jnp.float32)
    down_stored = noise(key_of[4], (SECTIONS, LAT, COLS), 1.0, 6.0, ((0, 4), (1, 8)), jnp.float32)
    sources = noise(key_of[5], (LAT, COLS), 1.0, 6.0, ((0, 8),), jnp.float32)
    assignment = jax.random.permutation(key_of[6], 2 * SHOTS).astype(jnp.int32)
    return {"operator": operator, "band_shift": band_shift, "reflectivity": reflectivity, "up_stored": up_stored, "down_stored": down_stored, "sources": sources, "assignment": assignment}


def combine_parts(real_rows, imag_rows):
    col_count = real_rows.shape[-1]
    shape_in = real_rows.shape[:-1] + (col_count // (2 * SHOTS), 2, SHOTS)
    real_terms = real_rows.reshape(shape_in)
    imag_terms = imag_rows.reshape(shape_in)
    real_part = real_terms[..., 0, :] - imag_terms[..., 1, :]
    imag_part = real_terms[..., 1, :] + imag_terms[..., 0, :]
    return jnp.stack([real_part, imag_part], axis=-2).reshape(real_rows.shape)


def propagate(extrapolator, offsets, wavefield):
    tile_count = extrapolator.shape[0]
    col_count = wavefield.shape[1]
    padded = jnp.pad(wavefield, ((5 * TILE, 5 * TILE), (0, 0)))
    blocks = padded.reshape(tile_count + 10, TILE, col_count)
    starts = jnp.arange(tile_count, dtype=jnp.int32) + 1 + offsets.astype(jnp.int32)
    banded = jax.vmap(lambda begin_at: lax.dynamic_slice_in_dim(blocks, begin_at, 9, 0))(starts)
    product = jnp.einsum("gkab,gkbc->gac", extrapolator, banded, precision=lax.Precision.HIGHEST)
    real_rows = product[:, :TILE].reshape(tile_count * TILE, col_count)
    imag_rows = product[:, TILE:].reshape(tile_count * TILE, col_count)
    return combine_parts(real_rows, imag_rows)


def reference(operator, band_shift, reflectivity, up_stored, down_stored, sources, assignment):
    lateral = sources.shape[0]
    real_src = jnp.take(sources[:, :2 * SHOTS], assignment, axis=1)
    imag_src = jnp.take(sources[:, 2 * SHOTS:], assignment, axis=1)
    entering = jnp.stack([real_src.reshape(lateral, 2, SHOTS), imag_src.reshape(lateral, 2, SHOTS)], axis=2).reshape(lateral, 4 * SHOTS)
    down_list = []
    for section in range(SECTIONS):
        reflect_col = reflectivity[section][:, None]
        joined = (1.0 + reflect_col) * entering - reflect_col * up_stored[section]
        entering = propagate(operator[section], band_shift[section], joined)
        down_list.append(entering)
    rising = jnp.zeros_like(sources)
    up_list = [None] * SECTIONS
    for section in reversed(range(SECTIONS)):
        reflect_col = reflectivity[section][:, None]
        joined = (1.0 - reflect_col) * rising + reflect_col * down_stored[section]
        rising = propagate(operator[section], band_shift[section], joined)
        up_list[section] = rising
    return jnp.stack(down_list), jnp.stack(up_list)
```

```python
import functools

import jax
import jax.numpy as jnp
from jax import lax
from jax.experimental import pallas as pl
from jax.experimental.pallas import tpu as pltpu
from jax.sharding import PartitionSpec as P

TILE = 128
CHUNKS = (5,)
VMEM = pltpu.VMEM
LIMIT = 24 * 1024 * 1024


def spec(space):
    return pl.BlockSpec(memory_space=space)


def spans():
    out, at = [], 0
    for count in CHUNKS:
        out.append((at, count))
        at += count
    return out


def f32(*shape):
    return jax.ShapeDtypeStruct(shape, jnp.float32)


def params():
    return pltpu.CompilerParams(vmem_limit_bytes=LIMIT)


def cost(flops, read):
    return pl.CostEstimate(flops=flops, bytes_accessed=read, transcendentals=0)


def down_column(row):
    return jnp.transpose(jnp.broadcast_to(row, (TILE, TILE)))


def split(value):
    high = value.astype(jnp.bfloat16)
    low = (value - high.astype(jnp.float32)).astype(jnp.bfloat16)
    return high, low


def prep_kernel(tiles, shots, sections, assign, refl, up, down, src, *outs):
    info_a, info_b = outs[-2:]
    firsts = outs[:-2]
    depth = lax.axis_index("depth")
    rows = tiles * TILE

    def rows_of(j):
        return pl.ds(j * TILE, TILE)

    @pl.when(depth == 0)
    def _():
        lane = lax.broadcasted_iota(jnp.int32, (8, TILE), 1)
        wanted = jnp.zeros((8, TILE), jnp.int32)
        for b in range(TILE // (2 * shots)):
            for i in range(shots):
                shot = assign[b * shots + i]
                at = b * 2 * shots + i
                wanted = jnp.where(lane == at, shot, wanted)
                wanted = jnp.where(lane == at + shots, shot + TILE // 2, wanted)
        source = lax.broadcasted_iota(jnp.int32, (TILE, TILE), 0)
        pick = (source == jnp.broadcast_to(wanted[0:1], (TILE, TILE))).astype(jnp.float32).astype(jnp.bfloat16)
        for (at, count), first in zip(spans(), firsts):
            for j in range(at, at + count):
                x = src[rows_of(j)]
                high = x.astype(jnp.bfloat16)
                rest = x - high.astype(jnp.float32)
                mid, low = split(rest)
                entering = jnp.dot(low, pick, preferred_element_type=jnp.float32)
                entering += jnp.dot(mid, pick, preferred_element_type=jnp.float32)
                entering += jnp.dot(high, pick, preferred_element_type=jnp.float32)
                r = down_column(refl[0:1, j * TILE : (j + 1) * TILE])
                first[(j - at) * TILE : (j - at + 1) * TILE] = (1.0 + r) * entering - r * up[0, rows_of(j)]

    @pl.when(depth == sections - 1)
    def _():
        for (at, count), first in zip(spans(), firsts):
            for j in range(at, at + count):
                r = down_column(refl[0:1, j * TILE : (j + 1) * TILE])
                first[(j - at) * TILE : (j - at + 1) * TILE] = r * down[0, rows_of(j)]

    def tell(upward, downward):
        for j in range(tiles):
            row = refl[0:1, j * TILE : (j + 1) * TILE]
            r = down_column(row)
            upward[rows_of(j)] = -r * down[0, rows_of(j)]
            downward[rows_of(j)] = r * up[0, rows_of(j)]
            upward[rows + j : rows + j + 1] = -row
            downward[rows + j : rows + j + 1] = row

    @pl.when(lax.rem(depth, 2) == 0)
    def _():
        tell(info_a, info_b)

    @pl.when(lax.rem(depth, 2) == 1)
    def _():
        tell(info_b, info_a)


def pack_kernel(band, shift, tile_in, out):
    j = pl.program_id(0)
    move = shift[0, j]
    for k in range(band):
        high, low = split(tile_in[0, 0, k])
        slot = k + 1 + move
        out[0, slot, :, :TILE] = high
        out[0, slot, :, TILE:] = low
    zero = jnp.zeros(out.shape[2:], jnp.bfloat16)
    out[0, jnp.where(move >= 0, 0, band)] = zero
    out[0, jnp.where(move <= 0, band + 1, 1)] = zero


def doubled(tile):
    high, low = split(tile)
    line = jnp.concatenate([high, low], axis=1)
    return jnp.concatenate([line, line], axis=0)


def folded(product):
    return product[:, :TILE] + product[:, TILE:]


def is_active(step, sections):
    depth = lax.axis_index("depth")
    return (depth == step) | (depth == sections - 1 - step)


def tile_of(chunks, t):
    for (at, count), chunk in zip(spans(), chunks):
        if at <= t < at + count:
            return chunk[(t - at) * TILE : (t - at + 1) * TILE]


def spread(chunks, tiles, mirrored, held):
    for t in range(tiles):
        slot = jnp.where(mirrored, tiles - 1 - t, t)
        held[slot] = doubled(tile_of(chunks, t))


def side_product(packed, held, tiles, band, low_side, jj):
    j = jnp.where(low_side, tiles - 1 - jj, jj)
    lhs, rhs = [], []
    for tt in range(jj + 1):
        slot = jnp.where(low_side, jj - tt, band + 1 + tt - jj)
        lhs.append(packed[j, slot])
        rhs.append(held[tt])
    return j, folded(
        jnp.dot(
            jnp.concatenate(lhs, axis=1),
            jnp.concatenate(rhs, axis=0),
            preferred_element_type=jnp.float32,
        )
    )


def inner_kernel(step, sections, tiles, band, packed, *refs):
    n = len(CHUNKS)
    own, near, total, held_own, held_near = refs[:n], refs[n : 2 * n], *refs[2 * n :]

    @pl.when(is_active(step, sections))
    def _():
        for t in range(tiles):
            held_own[t * 2 * TILE : (t + 1) * 2 * TILE] = doubled(tile_of(own, t))
        low_side = lax.rem(lax.axis_index("lat"), 2) == 1
        spread(near, tiles, low_side, held_near)
        for j in range(tiles):
            lhs = jnp.concatenate([packed[j, tiles - j + t] for t in range(tiles)], axis=1)
            total[j] = folded(jnp.dot(lhs, held_own[...], preferred_element_type=jnp.float32))
        for jj in range(tiles):
            j, more = side_product(packed, held_near, tiles, band, low_side, jj)
            total[j] = total[j] + more


def outer_kernel(step, sections, lats, tiles, band, shots, last, chained, packed, total, info, *refs):
    n = len(CHUNKS)
    far, refs = refs[:n], refs[n:]
    if chained:
        refs = refs[2:]
    result_down, result_up, refs = refs[0], refs[1], refs[2:]
    nexts, refs = ((), refs) if last else (refs[:n], refs[n:])
    held, leaving, sems = refs
    rows = tiles * TILE
    lat = lax.axis_index("lat")
    depth = lax.axis_index("depth")
    low_side = lax.rem(lat, 2) == 0

    @pl.when(is_active(step, sections))
    def _():
        lane = lax.broadcasted_iota(jnp.int32, (TILE, TILE), 1)
        real_lane = lax.rem(lane, 2 * shots) < shots

        def finish(j, product):
            by_imag = product[TILE:]
            ahead = pltpu.roll(by_imag, TILE - shots, 1)
            behind = pltpu.roll(by_imag, shots, 1)
            leaving[j] = product[:TILE] + jnp.where(real_lane, -ahead, behind)

        has_far = (lat > 0) & (lat < lats - 1)

        @pl.when(has_far)
        def _():
            spread(far, tiles, low_side, held)
            for jj in range(tiles):
                j, more = side_product(packed, held, tiles, band, low_side, jj)
                finish(j, total[j] + more)

        @pl.when(jnp.logical_not(has_far))
        def _():
            for j in range(tiles):
                finish(j, total[j])

        def leave(result):
            copy = pltpu.make_async_copy(leaving, result.at[0], sems)
            copy.start()
            for (at, count), nxt in zip(spans(), nexts):
                for j in range(at, at + count):
                    rho = down_column(info[rows + j : rows + j + 1])
                    nxt[(j - at) * TILE : (j - at + 1) * TILE] = (1.0 + rho) * leaving[j] - info[
                        j * TILE : (j + 1) * TILE
                    ]
            copy.wait()

        @pl.when(depth == step)
        def _():
            leave(result_down)

        @pl.when(depth != step)
        def _():
            leave(result_up)


def shards(sections, lats, operator, band_shift, reflectivity, up_stored, down_stored, sources, assignment):
    tiles, band = operator.shape[1], operator.shape[2]
    lateral, columns = sources.shape
    shots = columns // 4
    rows = tiles * TILE
    info_rows = rows + 8
    if sections % 2 or lats % 2 or tiles != band // 2 + 1 or tiles != sum(CHUNKS):
        raise ValueError("unsupported sizes")

    def pairs(partner):
        out = []
        for d in range(sections):
            for l in range(lats):
                e, m = partner(d, l)
                out.append((d * lats + l, e * lats + m))
        return out

    def near_of(d, l):
        return d, l ^ 1

    def far_of(d, l):
        m = l + 1 if l % 2 else l - 1
        return (d, m) if 0 <= m < lats else (d ^ 1, l)

    def across(lower):
        def partner(d, l):
            for low in lower:
                if d == low:
                    return low + 1, l
                if d == low + 1:
                    return low, l
            return near_of(d, l)

        return partner

    def move(x, partner):
        return lax.ppermute(x, ("depth", "lat"), pairs(partner))

    chunk_rows = [count * TILE for count in CHUNKS]
    prep = pl.pallas_call(
        functools.partial(prep_kernel, tiles, shots, sections),
        out_shape=[f32(c, columns) for c in chunk_rows] + [f32(info_rows, columns)] * 2,
        in_specs=[spec(pltpu.SMEM)] + [spec(VMEM)] * 4,
        out_specs=[spec(VMEM)] * (len(CHUNKS) + 2),
        compiler_params=params(),
        cost_estimate=cost(10**7, 5 * rows * columns * 4),
        name="prep",
    )
    *field, info_a, info_b = prep(assignment, reflectivity, up_stored, down_stored, sources)

    def halo(field):
        far = [move(f, far_of) for f in field]
        near = [move(f, near_of) for f in field]
        return near, far

    near, far = halo(field)
    info_a = move(info_a, across(range(0, sections, 2)))
    packed = pl.pallas_call(
        functools.partial(pack_kernel, band),
        out_shape=jax.ShapeDtypeStruct((tiles, band + 2, 2 * TILE, 2 * TILE), jnp.bfloat16),
        grid=(tiles,),
        in_specs=[
            spec(pltpu.SMEM),
            pl.BlockSpec((1, 1, band, 2 * TILE, TILE), lambda j: (0, j, 0, 0, 0)),
        ],
        out_specs=pl.BlockSpec((1, band + 2, 2 * TILE, 2 * TILE), lambda j: (j, 0, 0, 0)),
        compiler_params=params(),
        cost_estimate=cost(10**7, 2 * operator.size * 4),
        name="pack",
    )(band_shift, operator)
    info_b = move(info_b, across(range(1, sections - 1, 2)))

    results = None
    for step in range(sections):
        last = step == sections - 1
        total = pl.pallas_call(
            functools.partial(inner_kernel, step, sections, tiles, band),
            out_shape=f32(tiles, 2 * TILE, columns),
            in_specs=[spec(VMEM)] * (1 + 2 * len(CHUNKS)),
            out_specs=spec(VMEM),
            scratch_shapes=[
                VMEM((tiles * 2 * TILE, 2 * TILE), jnp.bfloat16),
                VMEM((tiles, 2 * TILE, 2 * TILE), jnp.bfloat16),
            ],
            compiler_params=params(),
            cost_estimate=cost(2 * 40 * 256**3, 8 * 2**20),
            name=f"inner_{step}",
        )(packed, *field, *near)
        n = len(CHUNKS)
        chained = results is not None
        result_shape = f32(1, tiles, TILE, columns)
        outs = pl.pallas_call(
            functools.partial(outer_kernel, step, sections, lats, tiles, band, shots, last, chained),
            out_shape=[result_shape] * 2 + ([] if last else [f32(c, columns) for c in chunk_rows]),
            in_specs=[spec(VMEM)] * (3 + n) + [spec(pl.ANY)] * (2 if chained else 0),
            out_specs=[spec(pl.ANY)] * 2 + [spec(VMEM)] * (0 if last else n),
            scratch_shapes=[
                VMEM((tiles, 2 * TILE, 2 * TILE), jnp.bfloat16),
                VMEM((tiles, TILE, columns), jnp.float32),
                pltpu.SemaphoreType.DMA(()),
            ],
            input_output_aliases={3 + n: 0, 4 + n: 1} if chained else {},
            compiler_params=params(),
            cost_estimate=cost(2 * 15 * 256**3, 4 * 2**20),
            name=f"outer_{step}",
        )(packed, total, info_a if step % 2 == 0 else info_b, *far, *(results or ()))
        results = outs[:2]
        if not last:
            lower = sorted({step, sections - 2 - step})
            field = [move(f, across(lower)) for f in outs[2:]]
            near, far = halo(field)
    return tuple(r.reshape(1, lateral, columns) for r in results)


def solution(mesh):
    return jax.shard_map(
        functools.partial(shards, mesh.shape["depth"], mesh.shape["lat"]),
        mesh=mesh,
        in_specs=(
            P("depth", "lat", None, None, None),
            P("depth", "lat"),
            P("depth", "lat"),
            P("depth", "lat", None),
            P("depth", "lat", None),
            P("lat", None),
            P(),
        ),
        out_specs=(P("depth", "lat", None), P("depth", "lat", None)),
        check_vma=False,
    )
```

```python
import functools

import jax
import jax.numpy as jnp
from jax import lax
from jax.experimental import pallas as pl
from jax.experimental.pallas import tpu as pltpu
from jax.sharding import PartitionSpec as P

TILE = 128
VMEM = pltpu.VMEM
LIMIT = 16 * 2**20


def spec(space):
    return pl.BlockSpec(memory_space=space)


def f32(*shape):
    return jax.ShapeDtypeStruct(shape, jnp.float32)


def params(limit=LIMIT):
    return pltpu.CompilerParams(vmem_limit_bytes=limit)


def cost(flops, read):
    return pl.CostEstimate(flops=flops, bytes_accessed=read, transcendentals=0)


def rows_of(t):
    return slice(t * TILE, (t + 1) * TILE)


def down_column(row):
    return jnp.transpose(jnp.broadcast_to(row, (TILE, TILE)))


def split(value):
    high = value.astype(jnp.bfloat16)
    low = (value - high.astype(jnp.float32)).astype(jnp.bfloat16)
    return high, low


def prep_kernel(tiles, shots, sections, assign_at, refl_at, up_at, down_at, src_at, first, second, assign, refl, up, down, src, sems):
    depth = lax.axis_index("depth")
    loads = [
        pltpu.make_async_copy(assign_at, assign, sems.at[0]),
        pltpu.make_async_copy(refl_at, refl, sems.at[1]),
        pltpu.make_async_copy(up_at, up, sems.at[2]),
        pltpu.make_async_copy(down_at, down, sems.at[3]),
        pltpu.make_async_copy(src_at, src, sems.at[4]),
    ]
    for load in loads:
        load.start()
    for load in loads:
        load.wait()
    descends = depth < sections // 2

    def write(of_up, of_down):
        for j in range(tiles):
            row = refl[0:1, rows_of(j)]
            r = down_column(row)
            of_up[rows_of(j)] = -(r * up[0, rows_of(j)])
            of_down[rows_of(j)] = r * down[0, rows_of(j)]
            first[tiles * TILE + j : tiles * TILE + j + 1] = row

    @pl.when(descends)
    def _():
        write(first, second)

    @pl.when(jnp.logical_not(descends))
    def _():
        write(second, first)

    @pl.when(depth == 0)
    def _():
        lane = lax.broadcasted_iota(jnp.int32, (8, TILE), 1)
        wanted = jnp.zeros((8, TILE), jnp.int32)
        for b in range(TILE // (2 * shots)):
            for i in range(shots):
                shot = assign[b * shots + i]
                at = b * 2 * shots + i
                wanted = jnp.where(lane == at, shot, wanted)
                wanted = jnp.where(lane == at + shots, shot + TILE // 2, wanted)
        source = lax.broadcasted_iota(jnp.int32, (TILE, TILE), 0)
        pick = (source == jnp.broadcast_to(wanted[0:1], (TILE, TILE))).astype(jnp.float32).astype(jnp.bfloat16)
        for j in range(tiles):
            x = src[rows_of(j)]
            high = x.astype(jnp.bfloat16)
            mid, low = split(x - high.astype(jnp.float32))
            entering = jnp.dot(low, pick, preferred_element_type=jnp.float32)
            entering += jnp.dot(mid, pick, preferred_element_type=jnp.float32)
            entering += jnp.dot(high, pick, preferred_element_type=jnp.float32)
            r = down_column(refl[0:1, rows_of(j)])
            first[rows_of(j)] = (1.0 + r) * entering + first[rows_of(j)]


def pack_kernel(tiles, band, shift_at, tiles_at, out, shift, held, sems):
    loads = [pltpu.make_async_copy(shift_at, shift, sems.at[tiles])]
    loads += [pltpu.make_async_copy(tiles_at.at[0, j], held.at[j], sems.at[j]) for j in range(tiles)]
    for load in loads:
        load.start()
    loads[0].wait()
    for j in range(tiles):
        loads[1 + j].wait()
        move = shift[0, j]
        for k in range(band):
            high, low = split(held[j, k])
            slot = k + 1 + move
            out[j, slot, :, :TILE] = high
            out[j, slot, :, TILE:] = low
        zero = jnp.zeros(out.shape[2:], jnp.bfloat16)
        out[j, jnp.where(move >= 0, 0, band)] = zero
        out[j, jnp.where(move <= 0, band + 1, 1)] = zero


def doubled(tile):
    high, low = split(tile)
    line = jnp.concatenate([high, low], axis=1)
    return jnp.concatenate([line, line], axis=0)


def folded(product):
    return product[:, :TILE] + product[:, TILE:]


def scaled(field, t, scale, sign):
    tile = field[rows_of(t)]
    return tile if scale is None else tile * (1.0 + sign * scale[t])


def spread(field, scale, sign, tiles, mirrored, held):
    for t in range(tiles):
        slot = jnp.where(mirrored, tiles - 1 - t, t)
        held[slot] = doubled(scaled(field, t, scale, sign))


def side_product(packed, held, tiles, band, low_side, jj):
    j = jnp.where(low_side, tiles - 1 - jj, jj)
    lhs, rhs = [], []
    for tt in range(jj + 1):
        slot = jnp.where(low_side, jj - tt, band + 1 + tt - jj)
        lhs.append(packed[j, slot])
        rhs.append(held[tt])
    return j, folded(
        jnp.dot(
            jnp.concatenate(lhs, axis=1),
            jnp.concatenate(rhs, axis=0),
            preferred_element_type=jnp.float32,
        )
    )


def when_active(step, sections, body):
    depth = lax.axis_index("depth")
    if step is None or step == 0:
        body()
    else:
        pl.when((depth == step) | (depth == sections - 1 - step))(body)


def inner_kernel(step, sections, tiles, band, packed, own, near, *refs):
    scales = [None, None]
    if step is None:
        own_rows, near_rows, total, own_scale, near_scale, held_own, held_near = refs
    elif step == 0:
        total, held_own, held_near = refs
    else:
        *scales, total, held_own, held_near = refs

    def body():
        sign = jnp.where(lax.axis_index("depth") == (step or 0), 1.0, -1.0)
        for t in range(tiles):
            held_own[t * 2 * TILE : (t + 1) * 2 * TILE] = doubled(scaled(own, t, scales[0], sign))
        low_side = lax.rem(lax.axis_index("lat"), 2) == 1
        spread(near, scales[1], sign, tiles, low_side, held_near)
        for j in range(tiles):
            lhs = jnp.concatenate([packed[j, tiles - j + t] for t in range(tiles)], axis=1)
            total[j] = folded(jnp.dot(lhs, held_own[...], preferred_element_type=jnp.float32))
        for jj in range(tiles):
            j, more = side_product(packed, held_near, tiles, band, low_side, jj)
            total[j] = total[j] + more
        if step is None:
            for t in range(tiles):
                at = tiles * TILE + t
                own_scale[t] = down_column(own_rows[at : at + 1])
                near_scale[t] = down_column(near_rows[at : at + 1])

    when_active(step, sections, body)


def outer_kernel(step, sections, lats, tiles, band, shots, packed, total, far, *refs):
    scale, base = None, None
    if step is None:
        far_rows, out, far_scale, held = refs
    elif step == 0:
        out, held = refs
    elif step < sections - 1:
        scale, base, out, held = refs
    else:
        scale, base, _, _, result_down, result_up, held, out, sem = refs
    lat = lax.axis_index("lat")
    depth = lax.axis_index("depth")
    low_side = lax.rem(lat, 2) == 0
    has_far = (lat > 0) & (lat < lats - 1)

    def body():
        sign = jnp.where(depth == (step or 0), 1.0, -1.0)
        lane = lax.broadcasted_iota(jnp.int32, (TILE, TILE), 1)
        real_lane = lax.rem(lane, 2 * shots) < shots

        def finish(j, product):
            by_imag = product[TILE:]
            ahead = pltpu.roll(by_imag, TILE - shots, 1)
            behind = pltpu.roll(by_imag, shots, 1)
            value = product[:TILE] + jnp.where(real_lane, -ahead, behind)
            at = pl.ds(pl.multiple_of(j * TILE, TILE), TILE)
            out[at] = value if base is None else value + base[at]

        @pl.when(has_far)
        def _():
            spread(far, scale, sign, tiles, low_side, held)
            for jj in range(tiles):
                j, more = side_product(packed, held, tiles, band, low_side, jj)
                finish(j, total[j] + more)

        @pl.when(jnp.logical_not(has_far))
        def _():
            for j in range(tiles):
                finish(j, total[j])

        if step is None:
            for t in range(tiles):
                at = tiles * TILE + t
                far_scale[t] = down_column(far_rows[at : at + 1])

        if step == sections - 1:

            def leave(result):
                copy = pltpu.make_async_copy(out, result.at[0], sem)
                copy.start()
                copy.wait()

            pl.when(depth == step)(lambda: leave(result_down))
            pl.when(depth != step)(lambda: leave(result_up))

    when_active(step, sections, body)


def keep_kernel(sections, *refs):
    fields, (result_down, result_up, sem) = refs[: sections - 1], refs[sections - 1 :]
    depth = lax.axis_index("depth")

    def put(field, result):
        copy = pltpu.make_async_copy(field, result.at[0], sem)
        copy.start()
        copy.wait()

    for step, field in enumerate(fields):
        pl.when(depth == step)(functools.partial(put, field, result_down))
        pl.when(depth == sections - 1 - step)(functools.partial(put, field, result_up))


def shards(sections, lats, operator, band_shift, reflectivity, up_stored, down_stored, sources, assignment):
    tiles, band = operator.shape[1], operator.shape[2]
    lateral, columns = sources.shape
    shots = columns // 4
    rows = tiles * TILE
    if sections % 2 or lats % 2 or tiles != band // 2 + 1:
        raise ValueError("unsupported sizes")

    def move(x, partner):
        pairs = []
        for d in range(sections):
            for l in range(lats):
                e, m = partner(d, l)
                pairs.append((d * lats + l, e * lats + m))
        return lax.ppermute(x, ("depth", "lat"), pairs)

    def near_of(d, l):
        return d, l ^ 1

    def far_of(spare, d, l):
        m = l + 1 if l % 2 else l - 1
        return (d, m) if 0 <= m < lats else (spare(d), l)

    def across(step, d, l):
        for low in (step, sections - 2 - step):
            if d == low:
                return low + 1, l
            if d == low + 1:
                return low, l
        return near_of(d, l)

    def halo(field, spare):
        return move(field, functools.partial(far_of, spare)), move(field, near_of)

    first, second = pl.pallas_call(
        functools.partial(prep_kernel, tiles, shots, sections),
        out_shape=[f32(rows + 8, columns), f32(rows, columns)],
        in_specs=[spec(pltpu.HBM)] * 5,
        out_specs=[spec(VMEM)] * 2,
        scratch_shapes=[
            pltpu.SMEM(assignment.shape, jnp.int32),
            VMEM(reflectivity.shape, jnp.float32),
            VMEM(up_stored.shape, jnp.float32),
            VMEM(down_stored.shape, jnp.float32),
            VMEM(sources.shape, jnp.float32),
            pltpu.SemaphoreType.DMA((5,)),
        ],
        compiler_params=params(),
        cost_estimate=cost(10**7, 5 * rows * columns * 4),
        name="prep",
    )(assignment, reflectivity, up_stored, down_stored, sources)

    packed = pl.pallas_call(
        functools.partial(pack_kernel, tiles, band),
        out_shape=jax.ShapeDtypeStruct((tiles, band + 2, 2 * TILE, 2 * TILE), jnp.bfloat16),
        in_specs=[spec(pltpu.HBM)] * 2,
        out_specs=spec(VMEM),
        scratch_shapes=[
            pltpu.SMEM(band_shift.shape, jnp.int32),
            VMEM(operator.shape[1:], jnp.float32),
            pltpu.SemaphoreType.DMA((tiles + 1,)),
        ],
        compiler_params=params(),
        cost_estimate=cost(10**7, 2 * operator.size * 4),
        name="pack",
    )(band_shift, operator)

    square = f32(tiles, TILE, columns)
    held = VMEM((tiles, 2 * TILE, 2 * TILE), jnp.bfloat16)

    def inner(step, own, near, more, extra):
        return pl.pallas_call(
            functools.partial(inner_kernel, step, sections, tiles, band),
            out_shape=[f32(tiles, 2 * TILE, columns)] + extra,
            in_specs=[spec(VMEM)] * (3 + len(more)),
            out_specs=[spec(VMEM)] * (1 + len(extra)),
            scratch_shapes=[VMEM((tiles * 2 * TILE, 2 * TILE), jnp.bfloat16), held],
            compiler_params=params(),
            cost_estimate=cost(2 * 40 * 256**3, 8 * 2**20),
            name=f"inner_{'base' if step is None else step}",
        )(packed, own, near, *more)

    def outer(step, total, far, more, extra):
        return pl.pallas_call(
            functools.partial(outer_kernel, step, sections, lats, tiles, band, shots),
            out_shape=[f32(rows, columns)] + extra,
            in_specs=[spec(VMEM)] * (3 + len(more)),
            out_specs=[spec(VMEM)] * (1 + len(extra)),
            scratch_shapes=[held],
            compiler_params=params(),
            cost_estimate=cost(2 * 15 * 256**3, 4 * 2**20),
            name=f"outer_{'base' if step is None else step}",
        )(packed, total, far, *more)

    first_far, first_near = halo(first, lambda d: d ^ 1)
    (total,) = inner(0, first, first_near, (), [])
    (field,) = outer(0, total, first_far, (), [])
    fields = [field]
    arrived = move(field, functools.partial(across, 0))

    second, _ = lax.optimization_barrier((second, field))
    far, near = halo(second, lambda d: (d + sections // 2) % sections)
    total, own_scale, near_scale = inner(None, second, near, (first, first_near), [square, square])
    second_base, far_scale = outer(None, total, far, (first_far,), [square])

    for step in range(1, sections):
        far, near = halo(arrived, lambda d: d ^ 1)
        (total,) = inner(step, arrived, near, (own_scale, near_scale), [])
        base = fields[0] if step < sections // 2 else second_base
        if step < sections - 1:
            (field,) = outer(step, total, far, (far_scale, base), [])
            fields.append(field)
            arrived = move(field, functools.partial(across, step))
            continue
        shape = f32(1, rows, columns)
        results = pl.pallas_call(
            functools.partial(keep_kernel, sections),
            out_shape=[shape] * 2,
            in_specs=[spec(VMEM)] * len(fields),
            out_specs=[spec(pl.ANY)] * 2,
            scratch_shapes=[pltpu.SemaphoreType.DMA(())],
            compiler_params=params(),
            cost_estimate=cost(0, 4 * rows * columns * 4),
            name="keep",
        )(*fields)
        results = pl.pallas_call(
            functools.partial(outer_kernel, step, sections, lats, tiles, band, shots),
            out_shape=[shape] * 2,
            in_specs=[spec(VMEM)] * 5 + [spec(pl.ANY)] * 2,
            out_specs=[spec(pl.ANY)] * 2,
            scratch_shapes=[held, VMEM((rows, columns), jnp.float32), pltpu.SemaphoreType.DMA(())],
            input_output_aliases={5: 0, 6: 1},
            compiler_params=params(),
            cost_estimate=cost(2 * 15 * 256**3, 4 * 2**20),
            name=f"outer_{step}",
        )(packed, total, far, far_scale, base, *results)
    return tuple(results)


def solution(mesh):
    return jax.shard_map(
        functools.partial(shards, mesh.shape["depth"], mesh.shape["lat"]),
        mesh=mesh,
        in_specs=(
            P("depth", "lat", None, None, None),
            P("depth", "lat"),
            P("depth", "lat"),
            P("depth", "lat", None),
            P("depth", "lat", None),
            P("lat", None),
            P(),
        ),
        out_specs=(P("depth", "lat", None), P("depth", "lat", None)),
        check_vma=False,
    )
```

```python
import functools

import jax
import jax.numpy as jnp
from jax import lax
from jax.experimental import pallas as pl
from jax.experimental.pallas import tpu as pltpu
from jax.sharding import PartitionSpec as P

TILE = 128
VMEM = pltpu.VMEM
LIMIT = 16 * 2**20
CHUNKS = (3, 2)


def spec(space):
    return pl.BlockSpec(memory_space=space)


def f32(*shape):
    return jax.ShapeDtypeStruct(shape, jnp.float32)


def params(limit=LIMIT):
    return pltpu.CompilerParams(vmem_limit_bytes=limit)


def cost(flops, read):
    return pl.CostEstimate(flops=flops, bytes_accessed=read, transcendentals=0)


def in_hbm(x):
    return pltpu.with_memory_space_constraint(x, pltpu.HBM)


def rows_of(t):
    return slice(t * TILE, (t + 1) * TILE)


def down_column(row):
    return jnp.transpose(jnp.broadcast_to(row, (TILE, TILE)))


def split(value):
    high = value.astype(jnp.bfloat16)
    low = (value - high.astype(jnp.float32)).astype(jnp.bfloat16)
    return high, low


def prep_kernel(tiles, shots, sections, assign_at, refl_at, up_at, down_at, src_at, first, second, assign, refl, up, down, src, sems):
    depth = lax.axis_index("depth")
    loads = [
        pltpu.make_async_copy(assign_at, assign, sems.at[0]),
        pltpu.make_async_copy(refl_at, refl, sems.at[1]),
        pltpu.make_async_copy(up_at, up, sems.at[2]),
        pltpu.make_async_copy(down_at, down, sems.at[3]),
        pltpu.make_async_copy(src_at, src, sems.at[4]),
    ]
    for load in loads:
        load.start()
    for load in loads:
        load.wait()
    descends = depth < sections // 2

    def write(of_up, of_down):
        for j in range(tiles):
            row = refl[0:1, rows_of(j)]
            r = down_column(row)
            of_up[rows_of(j)] = -(r * up[0, rows_of(j)])
            of_down[rows_of(j)] = r * down[0, rows_of(j)]
            first[tiles * TILE + j : tiles * TILE + j + 1] = row

    @pl.when(descends)
    def _():
        write(first, second)

    @pl.when(jnp.logical_not(descends))
    def _():
        write(second, first)

    @pl.when(depth == 0)
    def _():
        lane = lax.broadcasted_iota(jnp.int32, (8, TILE), 1)
        wanted = jnp.zeros((8, TILE), jnp.int32)
        for b in range(TILE // (2 * shots)):
            for i in range(shots):
                shot = assign[b * shots + i]
                at = b * 2 * shots + i
                wanted = jnp.where(lane == at, shot, wanted)
                wanted = jnp.where(lane == at + shots, shot + TILE // 2, wanted)
        source = lax.broadcasted_iota(jnp.int32, (TILE, TILE), 0)
        pick = (source == jnp.broadcast_to(wanted[0:1], (TILE, TILE))).astype(jnp.float32).astype(jnp.bfloat16)
        for j in range(tiles):
            x = src[rows_of(j)]
            high = x.astype(jnp.bfloat16)
            mid, low = split(x - high.astype(jnp.float32))
            entering = jnp.dot(low, pick, preferred_element_type=jnp.float32)
            entering += jnp.dot(mid, pick, preferred_element_type=jnp.float32)
            entering += jnp.dot(high, pick, preferred_element_type=jnp.float32)
            r = down_column(refl[0:1, rows_of(j)])
            first[rows_of(j)] = (1.0 + r) * entering + first[rows_of(j)]


def pack_kernel(tiles, band, shift_at, tiles_at, out, shift, held, sems):
    loads = [pltpu.make_async_copy(shift_at, shift, sems.at[tiles])]
    loads += [pltpu.make_async_copy(tiles_at.at[0, j], held.at[j], sems.at[j]) for j in range(tiles)]
    for load in loads:
        load.start()
    loads[0].wait()
    for j in range(tiles):
        loads[1 + j].wait()
        move = shift[0, j]
        for k in range(band):
            high, low = split(held[j, k])
            slot = k + 1 + move
            out[j, slot, :, :TILE] = high
            out[j, slot, :, TILE:] = low
        zero = jnp.zeros(out.shape[2:], jnp.bfloat16)
        out[j, jnp.where(move >= 0, 0, band)] = zero
        out[j, jnp.where(move <= 0, band + 1, 1)] = zero


def doubled(tile):
    high, low = split(tile)
    line = jnp.concatenate([high, low], axis=1)
    return jnp.concatenate([line, line], axis=0)


def folded(product):
    return product[:, :TILE] + product[:, TILE:]


def tile_of(chunks, t):
    for chunk in chunks:
        count = chunk.shape[0] // TILE
        if t < count:
            return chunk, rows_of(t)
        t -= count


def read(chunks, t):
    chunk, at = tile_of(chunks, t)
    return chunk[at]


def spread(field, scale, sign, tiles, held):
    for t in range(tiles):
        tile = read(field, t)
        held[2 * t * TILE : 2 * (t + 1) * TILE] = doubled(tile if scale is None else tile * (1.0 + sign * scale[t]))


def product(packed, held, tiles, j, side):
    if side == "low":
        slots, first, last = range(tiles - j), j, tiles
    elif side == "own":
        slots, first, last = range(tiles - j, 2 * tiles - j), 0, tiles
    else:
        slots, first, last = range(2 * tiles - j, 2 * tiles + 1), 0, j + 1
    return folded(
        jnp.dot(
            jnp.concatenate([packed[j, slot] for slot in slots], axis=1),
            held[2 * first * TILE : 2 * last * TILE],
            preferred_element_type=jnp.float32,
        )
    )


def when_active(step, sections, body):
    depth = lax.axis_index("depth")
    if step is None or step == 0:
        body()
    else:
        pl.when((depth == step) | (depth == sections - 1 - step))(body)


def inner_kernel(step, sections, tiles, n, packed, *refs):
    own, near, refs = refs[:n], refs[n : 2 * n], refs[2 * n :]
    scales = [None, None]
    if step is None:
        rows_at, (total, *scales_out, held_own, held_near) = refs[:3], refs[3:]
    elif step == 0:
        total, held_own, held_near = refs
    else:
        *scales, total, held_own, held_near = refs

    def body():
        sign = jnp.where(lax.axis_index("depth") == (step or 0), 1.0, -1.0)
        spread(own, scales[0], sign, tiles, held_own)
        spread(near, scales[1], sign, tiles, held_near)
        for j in range(tiles):
            total[j] = product(packed, held_own, tiles, j, "own")
        low_side = lax.rem(lax.axis_index("lat"), 2) == 1

        def add(side):
            for j in range(tiles):
                total[j] = total[j] + product(packed, held_near, tiles, j, side)

        pl.when(low_side)(lambda: add("low"))
        pl.when(jnp.logical_not(low_side))(lambda: add("high"))
        if step is None:
            for source, out in zip(rows_at, scales_out):
                for t in range(tiles):
                    at = tiles * TILE + t
                    out[t] = down_column(source[at : at + 1])

    when_active(step, sections, body)


def outer_kernel(step, sections, lats, tiles, shots, n, bases, packed, total, *refs):
    far, refs = refs[:n], refs[n:]
    scale, base, sems = None, None, None
    if step:
        scale, refs = refs[0], refs[1:]
        base, refs = refs[:bases], refs[bases:]
    if step == sections - 1:
        _, _, result_down, result_up, held, leaving, sems = refs
        outs = (leaving,)
    else:
        outs, held = refs[:-1], refs[-1]
    lat = lax.axis_index("lat")
    depth = lax.axis_index("depth")
    low_side = lax.rem(lat, 2) == 0
    has_far = (lat > 0) & (lat < lats - 1)

    def body():
        sign = jnp.where(depth == (step or 0), 1.0, -1.0)
        lane = lax.broadcasted_iota(jnp.int32, (TILE, TILE), 1)
        real_lane = lax.rem(lane, 2 * shots) < shots

        def finish(j, value):
            by_imag = value[TILE:]
            ahead = pltpu.roll(by_imag, TILE - shots, 1)
            behind = pltpu.roll(by_imag, shots, 1)
            value = value[:TILE] + jnp.where(real_lane, -ahead, behind)
            out, at = tile_of(outs, j)
            out[at] = value if base is None else value + read(base, j)

        def with_far(side):
            spread(far, scale, sign, tiles, held)
            for j in range(tiles):
                finish(j, total[j] + product(packed, held, tiles, j, side))

        pl.when(has_far & low_side)(lambda: with_far("low"))
        pl.when(has_far & jnp.logical_not(low_side))(lambda: with_far("high"))

        @pl.when(jnp.logical_not(has_far))
        def _():
            for j in range(tiles):
                finish(j, total[j])

        if sems is not None:

            def leave(result):
                copy = pltpu.make_async_copy(leaving, result.at[0], sems)
                copy.start()
                copy.wait()

            pl.when(depth == step)(lambda: leave(result_down))
            pl.when(depth != step)(lambda: leave(result_up))

    when_active(step, sections, body)


def keep_kernel(sections, counts, *refs):
    result_down, result_up, sems = refs[-3:]
    depth = lax.axis_index("depth")

    def put(field, result):
        copies, at = [], 0
        for i, chunk in enumerate(field):
            span = pl.ds(at, chunk.shape[0])
            copies.append(pltpu.make_async_copy(chunk, result.at[0, span], sems.at[i]))
            at += chunk.shape[0]
        for copy in copies:
            copy.start()
        for copy in copies:
            copy.wait()

    at = 0
    for step, count in enumerate(counts):
        field = refs[at : at + count]
        at += count
        pl.when(depth == step)(functools.partial(put, field, result_down))
        pl.when(depth == sections - 1 - step)(functools.partial(put, field, result_up))


def shards(sections, lats, operator, band_shift, reflectivity, up_stored, down_stored, sources, assignment):
    tiles, band = operator.shape[1], operator.shape[2]
    lateral, columns = sources.shape
    shots = columns // 4
    rows = tiles * TILE
    if sections % 2 or lats % 2 or tiles != band // 2 + 1 or tiles != sum(CHUNKS):
        raise ValueError("unsupported sizes")

    def move(x, partner):
        pairs = []
        for d in range(sections):
            for l in range(lats):
                e, m = partner(d, l)
                pairs.append((d * lats + l, e * lats + m))
        return lax.ppermute(x, ("depth", "lat"), pairs)

    def near_of(d, l):
        return d, l ^ 1

    def far_of(spare, d, l):
        m = l + 1 if l % 2 else l - 1
        return (d, m) if 0 <= m < lats else (spare(d), l)

    def across(step, d, l):
        for low in (step, sections - 2 - step):
            if d == low:
                return low + 1, l
            if d == low + 1:
                return low, l
        return near_of(d, l)

    def halo(field, spare):
        far, near = [], []
        for chunk in field:
            far.append(move(chunk, functools.partial(far_of, spare)))
            near.append(move(chunk, near_of))
        return far, near

    first, second = pl.pallas_call(
        functools.partial(prep_kernel, tiles, shots, sections),
        out_shape=[f32(rows + 8, columns), f32(rows, columns)],
        in_specs=[spec(pltpu.HBM)] * 5,
        out_specs=[spec(VMEM)] * 2,
        scratch_shapes=[
            pltpu.SMEM(assignment.shape, jnp.int32),
            VMEM(reflectivity.shape, jnp.float32),
            VMEM(up_stored.shape, jnp.float32),
            VMEM(down_stored.shape, jnp.float32),
            VMEM(sources.shape, jnp.float32),
            pltpu.SemaphoreType.DMA((5,)),
        ],
        compiler_params=params(),
        cost_estimate=cost(10**7, 5 * rows * columns * 4),
        name="prep",
    )(*map(in_hbm, (assignment, reflectivity, up_stored, down_stored, sources)))

    packed = pl.pallas_call(
        functools.partial(pack_kernel, tiles, band),
        out_shape=jax.ShapeDtypeStruct((tiles, band + 2, 2 * TILE, 2 * TILE), jnp.bfloat16),
        in_specs=[spec(pltpu.HBM)] * 2,
        out_specs=spec(VMEM),
        scratch_shapes=[
            pltpu.SMEM(band_shift.shape, jnp.int32),
            VMEM(operator.shape[1:], jnp.float32),
            pltpu.SemaphoreType.DMA((tiles + 1,)),
        ],
        compiler_params=params(),
        cost_estimate=cost(10**7, 2 * operator.size * 4),
        name="pack",
    )(in_hbm(band_shift), in_hbm(operator))

    square = f32(tiles, TILE, columns)
    held = VMEM((tiles * 2 * TILE, 2 * TILE), jnp.bfloat16)
    chunked = [f32(count * TILE, columns) for count in CHUNKS]
    whole = [f32(rows, columns)]

    def inner(step, own, near, more, extra):
        return pl.pallas_call(
            functools.partial(inner_kernel, step, sections, tiles, len(own)),
            out_shape=[f32(tiles, 2 * TILE, columns)] + extra,
            in_specs=[spec(VMEM)] * (1 + 2 * len(own) + len(more)),
            out_specs=[spec(VMEM)] * (1 + len(extra)),
            scratch_shapes=[held, held],
            compiler_params=params(),
            cost_estimate=cost(2 * 40 * 256**3, 8 * 2**20),
            name=f"inner_{'base' if step is None else step}",
        )(packed, *own, *near, *more)

    def outer(step, total, far, scale, base, shapes):
        last = step == sections - 1
        args = [packed, total, *far, *scale, *base]
        specs = [spec(VMEM)] * len(args)
        scratch, out_specs, aliases = [held], [spec(VMEM)] * len(shapes), {}
        if last:
            aliases = {len(args): 0, len(args) + 1: 1}
            args += keep()
            specs += [spec(pl.ANY)] * 2
            out_specs = [spec(pl.ANY)] * 2
            scratch += [VMEM((rows, columns), jnp.float32), pltpu.SemaphoreType.DMA(())]
        return pl.pallas_call(
            functools.partial(outer_kernel, step, sections, lats, tiles, shots, len(far), len(base)),
            out_shape=shapes,
            in_specs=specs,
            out_specs=out_specs,
            scratch_shapes=scratch,
            input_output_aliases=aliases,
            compiler_params=params(),
            cost_estimate=cost(2 * 15 * 256**3, 4 * 2**20),
            name=f"outer_{'base' if step is None else step}",
        )(*args)

    def keep():
        return pl.pallas_call(
            functools.partial(keep_kernel, sections, [len(field) for field in fields]),
            out_shape=result,
            in_specs=[spec(VMEM)] * sum(len(field) for field in fields),
            out_specs=[spec(pl.ANY)] * 2,
            scratch_shapes=[pltpu.SemaphoreType.DMA((len(CHUNKS),))],
            compiler_params=params(),
            cost_estimate=cost(0, 4 * rows * columns * 4),
            name="keep",
        )(*[chunk for field in fields for chunk in field])

    def cross(step, field):
        return [move(chunk, functools.partial(across, step)) for chunk in field]

    result = [f32(1, rows, columns)] * 2
    first_far, first_near = halo([first], lambda d: d ^ 1)
    (total,) = inner(0, [first], first_near, (), [])
    fields = [outer(0, total, first_far, (), (), chunked)]
    arrived = cross(0, fields[0])

    second, *_ = lax.optimization_barrier((second, *fields[0]))
    far, near = halo([second], lambda d: (d + sections // 2) % sections)
    total, own_scale, near_scale, far_scale = inner(None, [second], near, (first, *first_near, *first_far), [square] * 3)
    second_base = outer(None, total, far, (), (), whole)

    for step in range(1, sections):
        far, near = halo(arrived, lambda d: d ^ 1)
        (total,) = inner(step, arrived, near, (own_scale, near_scale), [])
        base = fields[0] if step < sections // 2 else second_base
        shapes = result if step == sections - 1 else chunked
        fields.append(outer(step, total, far, (far_scale,), base, shapes))
        if step < sections - 1:
            arrived = cross(step, fields[step])
    return tuple(fields[-1])


def solution(mesh):
    return jax.shard_map(
        functools.partial(shards, mesh.shape["depth"], mesh.shape["lat"]),
        mesh=mesh,
        in_specs=(
            P("depth", "lat", None, None, None),
            P("depth", "lat"),
            P("depth", "lat"),
            P("depth", "lat", None),
            P("depth", "lat", None),
            P("lat", None),
            P(),
        ),
        out_specs=(P("depth", "lat", None), P("depth", "lat", None)),
        check_vma=False,
    )
```

```python
import functools

import jax
import jax.numpy as jnp
from jax import lax
from jax.experimental import pallas as pl
from jax.experimental.pallas import tpu as pltpu
from jax.sharding import PartitionSpec as P


TILE = 128
VMEM = pltpu.VMEM
LIMIT = 16 * 2**20
CHUNKS = (3, 2)


def spec(space):
    return pl.BlockSpec(memory_space=space)


def f32(*shape):
    return jax.ShapeDtypeStruct(shape, jnp.float32)


def call(kernel, **kwargs):
    return pl.pallas_call(kernel, **kwargs)


def params(limit=LIMIT):
    return pltpu.CompilerParams(vmem_limit_bytes=limit)


def cost(flops, read):
    return pl.CostEstimate(flops=flops, bytes_accessed=read, transcendentals=0)


def in_hbm(x):
    return pltpu.with_memory_space_constraint(x, pltpu.HBM)


def rows_of(t):
    return slice(t * TILE, (t + 1) * TILE)


def down_column(row):
    return jnp.transpose(jnp.broadcast_to(row, (TILE, TILE)))


def split(value):
    high = value.astype(jnp.bfloat16)
    low = (value - high.astype(jnp.float32)).astype(jnp.bfloat16)
    return high, low


def prep_kernel(tiles, shots, sections, assign_at, refl_at, up_at, down_at, src_at, first, second, assign, refl, up, down, src, sems):
    depth = lax.axis_index("depth")
    loads = [
        pltpu.make_async_copy(assign_at, assign, sems.at[0]),
        pltpu.make_async_copy(refl_at, refl, sems.at[1]),
        pltpu.make_async_copy(up_at, up, sems.at[2]),
        pltpu.make_async_copy(down_at, down, sems.at[3]),
        pltpu.make_async_copy(src_at, src, sems.at[4]),
    ]
    for load in loads:
        load.start()
    for load in loads:
        load.wait()
    descends = depth < sections // 2

    def write(of_up, of_down):
        for j in range(tiles):
            row = refl[0:1, rows_of(j)]
            r = down_column(row)
            of_up[rows_of(j)] = -(r * up[0, rows_of(j)])
            of_down[rows_of(j)] = r * down[0, rows_of(j)]
            first[tiles * TILE + j : tiles * TILE + j + 1] = row

    @pl.when(descends)
    def _():
        write(first, second)

    @pl.when(jnp.logical_not(descends))
    def _():
        write(second, first)

    @pl.when(depth == 0)
    def _():
        lane = lax.broadcasted_iota(jnp.int32, (8, TILE), 1)
        wanted = jnp.zeros((8, TILE), jnp.int32)
        for b in range(TILE // (2 * shots)):
            for i in range(shots):
                shot = assign[b * shots + i]
                at = b * 2 * shots + i
                wanted = jnp.where(lane == at, shot, wanted)
                wanted = jnp.where(lane == at + shots, shot + TILE // 2, wanted)
        source = lax.broadcasted_iota(jnp.int32, (TILE, TILE), 0)
        pick = (source == jnp.broadcast_to(wanted[0:1], (TILE, TILE))).astype(jnp.float32).astype(jnp.bfloat16)
        for j in range(tiles):
            x = src[rows_of(j)]
            high = x.astype(jnp.bfloat16)
            mid, low = split(x - high.astype(jnp.float32))
            entering = jnp.dot(low, pick, preferred_element_type=jnp.float32)
            entering += jnp.dot(mid, pick, preferred_element_type=jnp.float32)
            entering += jnp.dot(high, pick, preferred_element_type=jnp.float32)
            r = down_column(refl[0:1, rows_of(j)])
            first[rows_of(j)] = (1.0 + r) * entering + first[rows_of(j)]


def pack_kernel(tiles, band, shift_at, tiles_at, out, shift, held, sems):
    loads = [pltpu.make_async_copy(shift_at, shift, sems.at[tiles])]
    loads += [pltpu.make_async_copy(tiles_at.at[0, j], held.at[j], sems.at[j]) for j in range(tiles)]
    for load in loads:
        load.start()
    loads[0].wait()
    for j in range(tiles):
        loads[1 + j].wait()
        move = shift[0, j]
        for k in range(band):
            high, low = split(held[j, k])
            slot = k + 1 + move
            out[j, slot, :, :TILE] = high
            out[j, slot, :, TILE:] = low
        zero = jnp.zeros(out.shape[2:], jnp.bfloat16)
        out[j, jnp.where(move >= 0, 0, band)] = zero
        out[j, jnp.where(move <= 0, band + 1, 1)] = zero


def doubled(tile):
    high, low = split(tile)
    line = jnp.concatenate([high, low], axis=1)
    return jnp.concatenate([line, line], axis=0)


def folded(product):
    return product[:, :TILE] + product[:, TILE:]


def tile_of(chunks, t):
    for chunk in chunks:
        count = chunk.shape[0] // TILE
        if t < count:
            return chunk, rows_of(t)
        t -= count


def read(chunks, t):
    chunk, at = tile_of(chunks, t)
    return chunk[at]


def spread(field, scale, sign, span, held):
    for t in span:
        tile = read(field, t - span.start)
        held[2 * t * TILE : 2 * (t + 1) * TILE] = doubled(tile if scale is None else tile * (1.0 + sign * scale[t]))


def product(packed, held, j, slots, at):
    return folded(
        jnp.dot(
            jnp.concatenate([packed[j, slot] for slot in slots], axis=1),
            held[2 * at * TILE : 2 * (at + len(slots)) * TILE],
            preferred_element_type=jnp.float32,
        )
    )


def side_product(packed, held, tiles, j, low_side):
    if low_side:
        return product(packed, held, j, range(tiles - j), j)
    return product(packed, held, j, range(2 * tiles - j, 2 * tiles + 1), 0)


def when_active(step, sections, body):
    depth = lax.axis_index("depth")
    if step is None or step == 0:
        body()
    else:
        pl.when((depth == step) | (depth == sections - 1 - step))(body)


def scale_kernel(tiles, *refs):
    for source, out in zip(refs[:3], refs[3:]):
        for t in range(tiles):
            at = tiles * TILE + t
            out[t] = down_column(source[at : at + 1])


def inner_kernel(step, sections, tiles, span, n_own, n_near, packed, *refs):
    own, near, refs = refs[:n_own], refs[n_own : n_own + n_near], refs[n_own + n_near :]
    scale, near_scale, before = None, None, None
    if step:
        scale, refs = refs[0], refs[1:]
        if near:
            near_scale, refs = refs[0], refs[1:]
    if span.start:
        before, refs = refs[0], refs[1:]
    total, held_own, held_near = refs

    def body():
        sign = jnp.where(lax.axis_index("depth") == (step or 0), 1.0, -1.0)
        spread(own, scale, sign, span, held_own)
        for j in range(tiles):
            value = product(packed, held_own, j, range(tiles - j + span.start, tiles - j + span.stop), span.start)
            total[j] = value if before is None else before[j] + value
        if near:
            spread(near, near_scale, sign, range(tiles), held_near)
            low_side = lax.rem(lax.axis_index("lat"), 2) == 1

            def add(low):
                for j in range(tiles):
                    total[j] = total[j] + side_product(packed, held_near, tiles, j, low)

            pl.when(low_side)(lambda: add(True))
            pl.when(jnp.logical_not(low_side))(lambda: add(False))

    when_active(step, sections, body)


def outer_kernel(step, sections, lats, tiles, shots, n, bases, packed, total, *refs):
    far, refs = refs[:n], refs[n:]
    scale, base, sems = None, None, None
    if step:
        scale, refs = refs[0], refs[1:]
        base, refs = refs[:bases], refs[bases:]
    if step == sections - 1:
        _, _, result_down, result_up, held, leaving, sems = refs
        outs = (leaving,)
    else:
        outs, held = refs[:-1], refs[-1]
    lat = lax.axis_index("lat")
    depth = lax.axis_index("depth")
    low_side = lax.rem(lat, 2) == 0
    has_far = (lat > 0) & (lat < lats - 1)

    def body():
        sign = jnp.where(depth == (step or 0), 1.0, -1.0)
        lane = lax.broadcasted_iota(jnp.int32, (TILE, TILE), 1)
        real_lane = lax.rem(lane, 2 * shots) < shots

        def finish(j, value):
            by_imag = value[TILE:]
            ahead = pltpu.roll(by_imag, TILE - shots, 1)
            behind = pltpu.roll(by_imag, shots, 1)
            value = value[:TILE] + jnp.where(real_lane, -ahead, behind)
            out, at = tile_of(outs, j)
            out[at] = value if base is None else value + read(base, j)

        def with_far(side):
            spread(far, scale, sign, range(tiles), held)
            for j in range(tiles):
                finish(j, total[j] + side_product(packed, held, tiles, j, side))

        pl.when(has_far & low_side)(lambda: with_far(True))
        pl.when(has_far & jnp.logical_not(low_side))(lambda: with_far(False))

        @pl.when(jnp.logical_not(has_far))
        def _():
            for j in range(tiles):
                finish(j, total[j])

        if sems is not None:

            def leave(result):
                copy = pltpu.make_async_copy(leaving, result.at[0], sems)
                copy.start()
                copy.wait()

            pl.when(depth == step)(lambda: leave(result_down))
            pl.when(depth != step)(lambda: leave(result_up))

    when_active(step, sections, body)


def keep_kernel(sections, counts, *refs):
    result_down, result_up, sems = refs[-3:]
    depth = lax.axis_index("depth")

    def put(field, result):
        copies, at = [], 0
        for i, chunk in enumerate(field):
            span = pl.ds(at, chunk.shape[0])
            copies.append(pltpu.make_async_copy(chunk, result.at[0, span], sems.at[i]))
            at += chunk.shape[0]
        for copy in copies:
            copy.start()
        for copy in copies:
            copy.wait()

    at = 0
    for step, count in enumerate(counts):
        field = refs[at : at + count]
        at += count
        pl.when(depth == step)(functools.partial(put, field, result_down))
        pl.when(depth == sections - 1 - step)(functools.partial(put, field, result_up))


def shards(sections, lats, operator, band_shift, reflectivity, up_stored, down_stored, sources, assignment):
    tiles, band = operator.shape[1], operator.shape[2]
    _, columns = sources.shape
    shots = columns // 4
    rows = tiles * TILE
    if sections % 2 or lats % 2 or tiles != band // 2 + 1 or tiles != sum(CHUNKS):
        raise ValueError("unsupported sizes")

    def move(x, partner):
        pairs = []
        for d in range(sections):
            for l in range(lats):
                e, m = partner(d, l)
                pairs.append((d * lats + l, e * lats + m))
        return lax.ppermute(x, ("depth", "lat"), pairs)

    def near_of(d, l):
        return d, l ^ 1

    def far_of(spare, d, l):
        m = l + 1 if l % 2 else l - 1
        return (d, m) if 0 <= m < lats else (spare(d), l)

    def across(step, d, l):
        for low in (step, sections - 2 - step):
            if d == low:
                return low + 1, l
            if d == low + 1:
                return low, l
        return near_of(d, l)

    def halo(field, spare):
        far, near = [], []
        for chunk in field:
            far.append(move(chunk, functools.partial(far_of, spare)))
            near.append(move(chunk, near_of))
        return far, near

    first, second = call(
        functools.partial(prep_kernel, tiles, shots, sections),
        out_shape=[f32(rows + 8, columns), f32(rows, columns)],
        in_specs=[spec(pltpu.HBM)] * 5,
        out_specs=[spec(VMEM)] * 2,
        scratch_shapes=[
            pltpu.SMEM(assignment.shape, jnp.int32),
            VMEM(reflectivity.shape, jnp.float32),
            VMEM(up_stored.shape, jnp.float32),
            VMEM(down_stored.shape, jnp.float32),
            VMEM(sources.shape, jnp.float32),
            pltpu.SemaphoreType.DMA((5,)),
        ],
        compiler_params=params(),
        cost_estimate=cost(10**7, 5 * rows * columns * 4),
    )(*map(in_hbm, (assignment, reflectivity, up_stored, down_stored, sources)))

    packed = call(
        functools.partial(pack_kernel, tiles, band),
        out_shape=jax.ShapeDtypeStruct((tiles, band + 2, 2 * TILE, 2 * TILE), jnp.bfloat16),
        in_specs=[spec(pltpu.HBM)] * 2,
        out_specs=spec(VMEM),
        scratch_shapes=[
            pltpu.SMEM(band_shift.shape, jnp.int32),
            VMEM(operator.shape[1:], jnp.float32),
            pltpu.SemaphoreType.DMA((tiles + 1,)),
        ],
        compiler_params=params(),
        cost_estimate=cost(10**7, 2 * operator.size * 4),
    )(in_hbm(band_shift), in_hbm(operator))

    square = f32(tiles, TILE, columns)
    held = VMEM((tiles * 2 * TILE, 2 * TILE), jnp.bfloat16)
    chunked = [f32(count * TILE, columns) for count in CHUNKS]
    whole = [f32(rows, columns)]

    def inner(step, own, near, more, at=0):
        count = sum(chunk.shape[0] for chunk in own) // TILE
        args = [packed, *own, *near, *more]
        return call(
            functools.partial(
                inner_kernel, step, sections, tiles, range(at, at + count), len(own), len(near)
            ),
            out_shape=f32(tiles, 2 * TILE, columns),
            in_specs=[spec(VMEM)] * len(args),
            out_specs=spec(VMEM),
            scratch_shapes=[held, held],
            compiler_params=params(),
            cost_estimate=cost(2 * 40 * 256**3, 8 * 2**20),
        )(*args)

    def outer(step, total, far, scale, base, shapes):
        last = step == sections - 1
        args = [packed, total, *far, *scale, *base]
        specs = [spec(VMEM)] * len(args)
        scratch, out_specs, aliases = [held], [spec(VMEM)] * len(shapes), {}
        if last:
            aliases = {len(args): 0, len(args) + 1: 1}
            args += keep()
            specs += [spec(pl.ANY)] * 2
            out_specs = [spec(pl.ANY)] * 2
            scratch += [VMEM((rows, columns), jnp.float32), pltpu.SemaphoreType.DMA(())]
        return call(
            functools.partial(outer_kernel, step, sections, lats, tiles, shots, len(far), len(base)),
            out_shape=shapes,
            in_specs=specs,
            out_specs=out_specs,
            scratch_shapes=scratch,
            input_output_aliases=aliases,
            compiler_params=params(),
            cost_estimate=cost(2 * 15 * 256**3, 4 * 2**20),
        )(*args)

    def keep():
        return call(
            functools.partial(keep_kernel, sections, [len(field) for field in fields]),
            out_shape=result,
            in_specs=[spec(VMEM)] * sum(len(field) for field in fields),
            out_specs=[spec(pl.ANY)] * 2,
            scratch_shapes=[pltpu.SemaphoreType.DMA((len(CHUNKS),))],
            compiler_params=params(),
            cost_estimate=cost(0, 4 * rows * columns * 4),
        )(*[chunk for field in fields for chunk in field])

    def cross(step, field):
        return [move(chunk, functools.partial(across, step)) for chunk in field]

    result = [f32(1, rows, columns)] * 2
    first_far, first_near = halo([first], lambda d: d ^ 1)
    total = inner(0, [first], first_near, ())
    fields = [outer(0, total, first_far, (), (), chunked)]
    arrived = cross(0, fields[0])

    second, *_ = lax.optimization_barrier((second, *fields[0]))
    far, near = halo([second], lambda d: (d + sections // 2) % sections)
    own_scale, near_scale, far_scale = call(
        functools.partial(scale_kernel, tiles),
        out_shape=[square] * 3,
        in_specs=[spec(VMEM)] * 3,
        out_specs=[spec(VMEM)] * 3,
        compiler_params=params(),
        cost_estimate=cost(10**6, 4 * rows * columns * 4),
    )(first, *first_near, *first_far)
    total = inner(None, [second], near, ())
    second_base = outer(None, total, far, (), (), whole)

    for step in range(1, sections):
        far, near = halo(arrived, lambda d: d ^ 1)
        total, at = None, 0
        for chunk in arrived[:-1]:
            before = () if total is None else (total,)
            total = inner(step, [chunk], [], (own_scale, *before), at)
            at += chunk.shape[0] // TILE
        before = () if total is None else (total,)
        total = inner(step, arrived[-1:], near, (own_scale, near_scale, *before), at=at)
        base = fields[0] if step < sections // 2 else second_base
        shapes = result if step == sections - 1 else chunked
        fields.append(outer(step, total, far, (far_scale,), base, shapes))
        if step < sections - 1:
            arrived = cross(step, fields[step])
    return tuple(fields[-1])


def solution(mesh):
    return jax.shard_map(
        functools.partial(shards, mesh.shape["depth"], mesh.shape["lat"]),
        mesh=mesh,
        in_specs=(
            P("depth", "lat", None, None, None),
            P("depth", "lat"),
            P("depth", "lat"),
            P("depth", "lat", None),
            P("depth", "lat", None),
            P("lat", None),
            P(),
        ),
        out_specs=(P("depth", "lat", None), P("depth", "lat", None)),
        check_vma=False,
    )
```

```python
import functools

import jax
import jax.numpy as jnp
from jax import lax
from jax.experimental import pallas as pl
from jax.experimental.pallas import tpu as pltpu
from jax.sharding import PartitionSpec as P


TILE = 128
HALF = TILE // 2
VMEM = pltpu.VMEM
LIMIT = 16 * 2**20
STREAMS = 2


def spec(space):
    return pl.BlockSpec(memory_space=space)


def f32(*shape):
    return jax.ShapeDtypeStruct(shape, jnp.float32)


def call(kernel, **kwargs):
    return pl.pallas_call(kernel, **kwargs)


def params(limit=LIMIT):
    return pltpu.CompilerParams(vmem_limit_bytes=limit)


def cost(flops, read):
    return pl.CostEstimate(flops=flops, bytes_accessed=read, transcendentals=0)


def in_hbm(x):
    return pltpu.with_memory_space_constraint(x, pltpu.HBM)


def rows_of(t):
    return slice(t * TILE, (t + 1) * TILE)


def down_column(row):
    return jnp.transpose(jnp.broadcast_to(row, (TILE, TILE)))


def split(value):
    high = value.astype(jnp.bfloat16)
    low = (value - high.astype(jnp.float32)).astype(jnp.bfloat16)
    return high, low


def prep_kernel(tiles, shots, sections, assign_at, refl_at, up_at, down_at, src_at, first, second, assign, refl, up, down, src, sems):
    depth = lax.axis_index("depth")
    loads = [
        pltpu.make_async_copy(assign_at, assign, sems.at[0]),
        pltpu.make_async_copy(refl_at, refl, sems.at[1]),
        pltpu.make_async_copy(up_at, up, sems.at[2]),
        pltpu.make_async_copy(down_at, down, sems.at[3]),
        pltpu.make_async_copy(src_at, src, sems.at[4]),
    ]
    for load in loads:
        load.start()
    for load in loads:
        load.wait()
    descends = depth < sections // 2

    def write(of_up, of_down):
        for j in range(tiles):
            row = refl[0:1, rows_of(j)]
            r = down_column(row)
            of_up[rows_of(j)] = -(r * up[0, rows_of(j)])
            of_down[rows_of(j)] = r * down[0, rows_of(j)]
            first[tiles * TILE + j : tiles * TILE + j + 1] = row

    @pl.when(descends)
    def _():
        write(first, second)

    @pl.when(jnp.logical_not(descends))
    def _():
        write(second, first)

    @pl.when(depth == 0)
    def _():
        lane = lax.broadcasted_iota(jnp.int32, (8, TILE), 1)
        wanted = jnp.zeros((8, TILE), jnp.int32)
        for b in range(TILE // (2 * shots)):
            for i in range(shots):
                shot = assign[b * shots + i]
                at = b * 2 * shots + i
                wanted = jnp.where(lane == at, shot, wanted)
                wanted = jnp.where(lane == at + shots, shot + TILE // 2, wanted)
        source = lax.broadcasted_iota(jnp.int32, (TILE, TILE), 0)
        pick = (source == jnp.broadcast_to(wanted[0:1], (TILE, TILE))).astype(jnp.float32).astype(jnp.bfloat16)
        for j in range(tiles):
            x = src[rows_of(j)]
            high = x.astype(jnp.bfloat16)
            mid, low = split(x - high.astype(jnp.float32))
            entering = jnp.dot(low, pick, preferred_element_type=jnp.float32)
            entering += jnp.dot(mid, pick, preferred_element_type=jnp.float32)
            entering += jnp.dot(high, pick, preferred_element_type=jnp.float32)
            r = down_column(refl[0:1, rows_of(j)])
            first[rows_of(j)] = (1.0 + r) * entering + first[rows_of(j)]


def pack_kernel(tiles, band, shift_at, tiles_at, out, shift, held, sems):
    loads = [pltpu.make_async_copy(shift_at, shift, sems.at[tiles])]
    loads += [pltpu.make_async_copy(tiles_at.at[0, j], held.at[j], sems.at[j]) for j in range(tiles)]
    for load in loads:
        load.start()
    loads[0].wait()
    for j in range(tiles):
        loads[1 + j].wait()
        move = shift[0, j]
        for k in range(band):
            high, low = split(held[j, k])
            slot = k + 1 + move
            out[j, slot, :, :TILE] = high
            out[j, slot, :, TILE:] = low
        zero = jnp.zeros(out.shape[2:], jnp.bfloat16)
        out[j, jnp.where(move >= 0, 0, band)] = zero
        out[j, jnp.where(move <= 0, band + 1, 1)] = zero


def doubled(tile):
    high, low = split(tile)
    line = jnp.concatenate([high, low], axis=1)
    return jnp.concatenate([line, line], axis=0)


def folded(value):
    return value[:, :TILE] + value[:, TILE:]


def lanes(rows):
    return lax.broadcasted_iota(jnp.int32, (rows, TILE), 1)


def turned(value):
    return pltpu.roll(value, HALF, 1)


def left_half(rows):
    return lanes(rows) < HALF


def halves_of(t):
    return slice(t * HALF, (t + 1) * HALF)


def unpack_tile(chunk, t):
    part = chunk[halves_of(t)]
    return jnp.concatenate([part, turned(part)], axis=0)


def stream_line(tile):
    rest = tile - tile.astype(jnp.bfloat16).astype(jnp.float32)
    line = jnp.where(left_half(TILE), tile, turned(rest)).astype(jnp.bfloat16)
    return jnp.concatenate([line, line], axis=0)


def merged(first, second):
    left = left_half(HALF)
    upper = jnp.where(left, first, turned(second))
    lower = jnp.where(left, turned(first), second)
    return jnp.concatenate([upper, lower], axis=0)


def parted(value):
    upper, lower = value[:HALF], value[HALF:]
    left = left_half(HALF)
    return jnp.where(left, upper, turned(lower)), jnp.where(left, turned(upper), lower)


def spread(field, scale, sign, tiles, narrow, mirrored, held):
    for t in range(tiles):
        tile = unpack_tile(field, t) if narrow else field[rows_of(t)]
        if scale is not None:
            tile = tile * (1.0 + sign * scale[t])
        at = 2 * t * TILE
        if mirrored is not None:
            at = pl.multiple_of(jnp.where(mirrored, 2 * (tiles - 1 - t) * TILE, at), 2 * TILE)
        held[pl.ds(at, 2 * TILE)] = stream_line(tile) if narrow else doubled(tile)


def product(packed, held, j, slots, narrow):
    value = jnp.dot(
        jnp.concatenate([packed[j, slot] for slot in slots], axis=1),
        held[: 2 * len(slots) * TILE],
        preferred_element_type=jnp.float32,
    )
    return value if narrow else folded(value)


def side_product(packed, held, tiles, jj, low_side, narrow):
    j = jnp.where(low_side, tiles - 1 - jj, jj)
    slots = [jnp.where(low_side, jj - t, 2 * tiles + t - jj) for t in range(jj + 1)]
    return j, product(packed, held, j, slots, narrow)


def when_active(step, sections, body):
    depth = lax.axis_index("depth")
    if step:
        pl.when((depth == step) | (depth == sections - 1 - step))(body)
    else:
        body()


def combined(value, shots):
    by_imag = value[TILE:]
    ahead = pltpu.roll(by_imag, TILE - shots, 1)
    behind = pltpu.roll(by_imag, shots, 1)
    return value[:TILE] + jnp.where(lax.rem(lanes(TILE), 2 * shots) < shots, -ahead, behind)


def scale_kernel(tiles, *refs):
    for source, out in zip(refs[:3], refs[3:]):
        for t in range(tiles):
            at = tiles * TILE + t
            out[t] = down_column(source[at : at + 1])


def inner_kernel(step, sections, tiles, packed, own, near, *refs):
    narrow = bool(step)
    scale, near_scale = refs[:2] if narrow else (None, None)
    total, held_own, held_near = refs[-3:]

    def body():
        sign = jnp.where(lax.axis_index("depth") == (step or 0), 1.0, -1.0)
        low_side = lax.rem(lax.axis_index("lat"), 2) == 1
        spread(own, scale, sign, tiles, narrow, None, held_own)
        spread(near, near_scale, sign, tiles, narrow, low_side, held_near)
        for j in range(tiles):
            total[j] = product(packed, held_own, j, range(tiles - j, 2 * tiles - j), narrow)
        for jj in range(tiles):
            j, value = side_product(packed, held_near, tiles, jj, low_side, narrow)
            total[j] = total[j] + value

    when_active(step, sections, body)


def outer_kernel(step, sections, lats, tiles, shots, ends, packed, total, far, *refs):
    narrow = bool(step)
    scale, base, other = None, None, None
    if narrow:
        (scale, base), refs = refs[:2], refs[2:]
    if ends:
        other, _, _, result_down, result_up, held, leaving, sems = refs
    else:
        outs, held = refs[:-1], refs[-1]
    lat = lax.axis_index("lat")
    depth = lax.axis_index("depth")
    low_side = lax.rem(lat, 2) == 0
    has_far = (lat > 0) & (lat < lats - 1)

    def body():
        sign = jnp.where(depth == (step or 0), 1.0, -1.0)

        def finish(j, value):
            at = pl.ds(pl.multiple_of(j * HALF, HALF), HALF)
            if not narrow:
                for out, part in zip(outs, parted(combined(value, shots))):
                    out[at] = part
                return
            value = combined(value + turned(value), shots)
            part = jnp.where(left_half(HALF), value[:HALF], value[HALF:]) + base[at]
            if ends:
                leaving[pl.ds(pl.multiple_of(j * TILE, TILE), TILE)] = merged(other[at], part)
            else:
                outs[0][at] = part

        @pl.when(has_far)
        def _():
            spread(far, scale, sign, tiles, narrow, low_side, held)
            for jj in range(tiles):
                j, value = side_product(packed, held, tiles, jj, low_side, narrow)
                finish(j, total[j] + value)

        @pl.when(jnp.logical_not(has_far))
        def _():
            for j in range(tiles):
                finish(j, total[j])

        if ends:

            def leave(result):
                copy = pltpu.make_async_copy(leaving, result.at[0], sems)
                copy.start()
                copy.wait()

            pl.when(depth == step)(lambda: leave(result_down))
            pl.when(depth != step)(lambda: leave(result_up))

    when_active(step, sections, body)


def keep_kernel(sections, tiles, *refs):
    fields, (result_down, result_up, whole, sems) = refs[:-4], refs[-4:]
    depth = lax.axis_index("depth")

    def put(first, second, result):
        for j in range(tiles):
            whole[rows_of(j)] = merged(first[halves_of(j)], second[halves_of(j)])
        copy = pltpu.make_async_copy(whole, result.at[0], sems)
        copy.start()
        copy.wait()

    for step in range(sections - 1):
        first, second = fields[2 * step : 2 * step + 2]
        pl.when(depth == step)(functools.partial(put, first, second, result_down))
        pl.when(depth == sections - 1 - step)(functools.partial(put, first, second, result_up))


def shards(sections, lats, operator, band_shift, reflectivity, up_stored, down_stored, sources, assignment):
    tiles, band = operator.shape[1], operator.shape[2]
    _, columns = sources.shape
    shots = columns // 4
    rows = tiles * TILE
    if sections % 2 or lats % 2 or tiles != band // 2 + 1 or columns != TILE:
        raise ValueError("unsupported sizes")

    def move(x, partner):
        pairs = []
        for d in range(sections):
            for l in range(lats):
                e, m = partner(d, l)
                pairs.append((d * lats + l, e * lats + m))
        return lax.ppermute(x, ("depth", "lat"), pairs)

    def near_of(d, l):
        return d, l ^ 1

    def far_of(spare, d, l):
        m = l + 1 if l % 2 else l - 1
        return (d, m) if 0 <= m < lats else (spare(d), l)

    def across(step, d, l):
        for low in (step, sections - 2 - step):
            if d == low:
                return low + 1, l
            if d == low + 1:
                return low, l
        return near_of(d, l)

    def halo(field, spare):
        near = move(field, near_of)
        return near, move(field, functools.partial(far_of, spare))

    def next_door(d):
        return d ^ 1

    first, second = call(
        functools.partial(prep_kernel, tiles, shots, sections),
        out_shape=[f32(rows + 8, columns), f32(rows, columns)],
        in_specs=[spec(pltpu.HBM)] * 5,
        out_specs=[spec(VMEM)] * 2,
        scratch_shapes=[
            pltpu.SMEM(assignment.shape, jnp.int32),
            VMEM(reflectivity.shape, jnp.float32),
            VMEM(up_stored.shape, jnp.float32),
            VMEM(down_stored.shape, jnp.float32),
            VMEM(sources.shape, jnp.float32),
            pltpu.SemaphoreType.DMA((5,)),
        ],
        compiler_params=params(),
        cost_estimate=cost(10**7, 5 * rows * columns * 4),
    )(*map(in_hbm, (assignment, reflectivity, up_stored, down_stored, sources)))

    packed = call(
        functools.partial(pack_kernel, tiles, band),
        out_shape=jax.ShapeDtypeStruct((tiles, band + 2, 2 * TILE, 2 * TILE), jnp.bfloat16),
        in_specs=[spec(pltpu.HBM)] * 2,
        out_specs=spec(VMEM),
        scratch_shapes=[
            pltpu.SMEM(band_shift.shape, jnp.int32),
            VMEM(operator.shape[1:], jnp.float32),
            pltpu.SemaphoreType.DMA((tiles + 1,)),
        ],
        compiler_params=params(),
        cost_estimate=cost(10**7, 2 * operator.size * 4),
    )(in_hbm(band_shift), in_hbm(operator))

    square = f32(tiles, TILE, columns)
    half = f32(rows // STREAMS, columns)
    result = [f32(1, rows, columns)] * 2

    def held(step):
        return VMEM((tiles * 2 * TILE, TILE if step else 2 * TILE), jnp.bfloat16)

    def inner(step, own, near, *scales):
        args = [packed, own, near, *scales]
        return call(
            functools.partial(inner_kernel, step, sections, tiles),
            out_shape=f32(tiles, 2 * TILE, columns),
            in_specs=[spec(VMEM)] * len(args),
            out_specs=spec(VMEM),
            scratch_shapes=[held(step)] * 2,
            compiler_params=params(),
            cost_estimate=cost(2 * 40 * 256**3, 8 * 2**20),
        )(*args)

    def outer(step, *args, shapes, kept=()):
        count = len(args) + 1
        ends = bool(kept)
        scratch = [held(step)]
        if ends:
            scratch += [VMEM((rows, columns), jnp.float32), pltpu.SemaphoreType.DMA(())]
        return call(
            functools.partial(outer_kernel, step, sections, lats, tiles, shots, ends),
            out_shape=shapes,
            in_specs=[spec(VMEM)] * count + [spec(pl.ANY)] * len(kept),
            out_specs=[spec(pl.ANY if ends else VMEM)] * len(shapes),
            scratch_shapes=scratch,
            input_output_aliases={count: 0, count + 1: 1} if ends else {},
            compiler_params=params(),
            cost_estimate=cost(2 * 15 * 256**3, 4 * 2**20),
        )(packed, *args, *kept)

    def cross(step, field):
        return [move(part, functools.partial(across, step)) for part in field]

    first_near, first_far = halo(first, next_door)
    total = inner(0, first, first_near)
    fields = [outer(0, total, first_far, shapes=[half] * STREAMS)]
    arrived = cross(0, fields[0])

    second, *_ = lax.optimization_barrier((second, *fields[0]))
    near, far = halo(second, lambda d: (d + sections // 2) % sections)
    own_scale, near_scale, far_scale = call(
        functools.partial(scale_kernel, tiles),
        out_shape=[square] * 3,
        in_specs=[spec(VMEM)] * 3,
        out_specs=[spec(VMEM)] * 3,
        compiler_params=params(),
        cost_estimate=cost(10**6, 4 * rows * columns * 4),
    )(first, first_near, first_far)
    total = inner(None, second, near)
    second_base = outer(None, total, far, shapes=[half] * STREAMS)

    for step in range(1, sections):
        bases = fields[0] if step < sections // 2 else second_base
        field = []
        for q in range(STREAMS):
            near, far = halo(arrived[q], next_door)
            total = inner(step, arrived[q], near, own_scale, near_scale)
            if step == sections - 1 and q == STREAMS - 1:
                kept = call(
                    functools.partial(keep_kernel, sections, tiles),
                    out_shape=result,
                    in_specs=[spec(VMEM)] * (len(fields) * STREAMS),
                    out_specs=[spec(pl.ANY)] * 2,
                    scratch_shapes=[VMEM((rows, columns), jnp.float32), pltpu.SemaphoreType.DMA(())],
                    compiler_params=params(),
                    cost_estimate=cost(0, 4 * rows * columns * 4),
                )(*[part for field_ in fields for part in field_])
                ended = outer(
                    step, total, far, far_scale, bases[q], field[0], shapes=result, kept=kept
                )
                return tuple(ended)
            (part,) = outer(step, total, far, far_scale, bases[q], shapes=[half])
            field.append(part)
        fields.append(field)
        arrived = cross(step, field)


def solution(mesh):
    return jax.shard_map(
        functools.partial(shards, mesh.shape["depth"], mesh.shape["lat"]),
        mesh=mesh,
        in_specs=(
            P("depth", "lat", None, None, None),
            P("depth", "lat"),
            P("depth", "lat"),
            P("depth", "lat", None),
            P("depth", "lat", None),
            P("lat", None),
            P(),
        ),
        out_specs=(P("depth", "lat", None), P("depth", "lat", None)),
        check_vma=False,
    )
```

```python
import functools

import jax
import jax.numpy as jnp
from jax import lax
from jax.experimental import pallas as pl
from jax.experimental.pallas import tpu as pltpu
from jax.sharding import PartitionSpec as P


TILE = 128
HALF = TILE // 2
VMEM = pltpu.VMEM
LIMIT = 16 * 2**20
STREAMS = 2


def spec(space):
    return pl.BlockSpec(memory_space=space)


def f32(*shape):
    return jax.ShapeDtypeStruct(shape, jnp.float32)


def call(kernel, **kwargs):
    return pl.pallas_call(kernel, **kwargs)


def params(limit=LIMIT):
    return pltpu.CompilerParams(vmem_limit_bytes=limit)


def cost(flops, read):
    return pl.CostEstimate(flops=flops, bytes_accessed=read, transcendentals=0)


def in_hbm(x):
    return pltpu.with_memory_space_constraint(x, pltpu.HBM)


def rows_of(t):
    return slice(t * TILE, (t + 1) * TILE)


def down_column(row):
    return jnp.transpose(jnp.broadcast_to(row, (TILE, TILE)))


def split(value):
    high = value.astype(jnp.bfloat16)
    low = (value - high.astype(jnp.float32)).astype(jnp.bfloat16)
    return high, low


def prep_kernel(tiles, shots, sections, assign_at, refl_at, up_at, down_at, src_at, first, second, assign, refl, up, down, src, sems):
    depth = lax.axis_index("depth")
    loads = [
        pltpu.make_async_copy(assign_at, assign, sems.at[0]),
        pltpu.make_async_copy(refl_at, refl, sems.at[1]),
        pltpu.make_async_copy(up_at, up, sems.at[2]),
        pltpu.make_async_copy(down_at, down, sems.at[3]),
        pltpu.make_async_copy(src_at, src, sems.at[4]),
    ]
    for load in loads:
        load.start()
    for load in loads:
        load.wait()
    descends = depth < sections // 2

    def write(of_up, of_down):
        for j in range(tiles):
            row = refl[0:1, rows_of(j)]
            r = down_column(row)
            of_up[rows_of(j)] = -(r * up[0, rows_of(j)])
            of_down[rows_of(j)] = r * down[0, rows_of(j)]
            first[tiles * TILE + j : tiles * TILE + j + 1] = row

    @pl.when(descends)
    def _():
        write(first, second)

    @pl.when(jnp.logical_not(descends))
    def _():
        write(second, first)

    @pl.when(depth == 0)
    def _():
        lane = lax.broadcasted_iota(jnp.int32, (8, TILE), 1)
        wanted = jnp.zeros((8, TILE), jnp.int32)
        for b in range(TILE // (2 * shots)):
            for i in range(shots):
                shot = assign[b * shots + i]
                at = b * 2 * shots + i
                wanted = jnp.where(lane == at, shot, wanted)
                wanted = jnp.where(lane == at + shots, shot + TILE // 2, wanted)
        source = lax.broadcasted_iota(jnp.int32, (TILE, TILE), 0)
        pick = (source == jnp.broadcast_to(wanted[0:1], (TILE, TILE))).astype(jnp.float32).astype(jnp.bfloat16)
        for j in range(tiles):
            x = src[rows_of(j)]
            high = x.astype(jnp.bfloat16)
            mid, low = split(x - high.astype(jnp.float32))
            entering = jnp.dot(low, pick, preferred_element_type=jnp.float32)
            entering += jnp.dot(mid, pick, preferred_element_type=jnp.float32)
            entering += jnp.dot(high, pick, preferred_element_type=jnp.float32)
            r = down_column(refl[0:1, rows_of(j)])
            first[rows_of(j)] = (1.0 + r) * entering + first[rows_of(j)]


def pack_kernel(tiles, band, shift_at, tiles_at, out, shift, held, sems):
    loads = [pltpu.make_async_copy(shift_at, shift, sems.at[tiles])]
    loads += [pltpu.make_async_copy(tiles_at.at[0, j], held.at[j], sems.at[j]) for j in range(tiles)]
    for load in loads:
        load.start()
    loads[0].wait()
    for j in range(tiles):
        loads[1 + j].wait()
        move = shift[0, j]
        for k in range(band):
            high, low = split(held[j, k])
            slot = k + 1 + move
            out[j, slot, :, :TILE] = high
            out[j, slot, :, TILE:] = low
        zero = jnp.zeros(out.shape[2:], jnp.bfloat16)
        out[j, jnp.where(move >= 0, 0, band)] = zero
        out[j, jnp.where(move <= 0, band + 1, 1)] = zero


def doubled(tile):
    high, low = split(tile)
    line = jnp.concatenate([high, low], axis=1)
    return jnp.concatenate([line, line], axis=0)


def folded(value):
    return value[:, :TILE] + value[:, TILE:]


def lanes(rows):
    return lax.broadcasted_iota(jnp.int32, (rows, TILE), 1)


def turned(value):
    return pltpu.roll(value, HALF, 1)


def left_half(rows):
    return lanes(rows) < HALF


def halves_of(t):
    return slice(t * HALF, (t + 1) * HALF)


def unpack_tile(chunk, t):
    part = chunk[halves_of(t)]
    return jnp.concatenate([part, turned(part)], axis=0)


def stream_line(tile):
    rest = tile - tile.astype(jnp.bfloat16).astype(jnp.float32)
    line = jnp.where(left_half(TILE), tile, turned(rest)).astype(jnp.bfloat16)
    return jnp.concatenate([line, line], axis=0)


def merged(first, second):
    left = left_half(HALF)
    upper = jnp.where(left, first, turned(second))
    lower = jnp.where(left, turned(first), second)
    return jnp.concatenate([upper, lower], axis=0)


def parted(value):
    upper, lower = value[:HALF], value[HALF:]
    left = left_half(HALF)
    return jnp.where(left, upper, turned(lower)), jnp.where(left, turned(upper), lower)


def spread(field, scale, sign, tiles, narrow, mirrored, held):
    for t in range(tiles):
        tile = unpack_tile(field, t) if narrow else field[rows_of(t)]
        if scale is not None:
            tile = tile * (1.0 + sign * scale[t])
        at = 2 * t * TILE
        if mirrored is not None:
            at = pl.multiple_of(jnp.where(mirrored, 2 * (tiles - 1 - t) * TILE, at), 2 * TILE)
        held[pl.ds(at, 2 * TILE)] = stream_line(tile) if narrow else doubled(tile)


def product(packed, held, j, slots, narrow):
    value = jnp.dot(
        jnp.concatenate([packed[j, slot] for slot in slots], axis=1),
        held[: 2 * len(slots) * TILE],
        preferred_element_type=jnp.float32,
    )
    return value if narrow else folded(value)


def side_product(packed, held, tiles, jj, low_side, narrow):
    j = jnp.where(low_side, tiles - 1 - jj, jj)
    slots = [jnp.where(low_side, jj - t, 2 * tiles + t - jj) for t in range(jj + 1)]
    return j, product(packed, held, j, slots, narrow)


def when_active(step, sections, body):
    depth = lax.axis_index("depth")
    if step is None:
        body()
    else:
        pl.when((depth == step) | (depth == sections - 1 - step))(body)


def combined(value, shots):
    by_imag = value[TILE:]
    ahead = pltpu.roll(by_imag, TILE - shots, 1)
    behind = pltpu.roll(by_imag, shots, 1)
    return value[:TILE] + jnp.where(lax.rem(lanes(TILE), 2 * shots) < shots, -ahead, behind)


def scale_kernel(tiles, *refs):
    for source, out in zip(refs[:3], refs[3:]):
        for t in range(tiles):
            at = tiles * TILE + t
            out[t] = down_column(source[at : at + 1])


def inner_kernel(step, sections, tiles, packed, own, near, *refs):
    narrow = bool(step)
    scale, near_scale = refs[:2] if narrow else (None, None)
    total, held_own, held_near = refs[-3:]

    def body():
        sign = jnp.where(lax.axis_index("depth") == (step or 0), 1.0, -1.0)
        low_side = lax.rem(lax.axis_index("lat"), 2) == 1
        spread(own, scale, sign, tiles, narrow, None, held_own)
        spread(near, near_scale, sign, tiles, narrow, low_side, held_near)
        for j in range(tiles):
            total[j] = product(packed, held_own, j, range(tiles - j, 2 * tiles - j), narrow)
        for jj in range(tiles):
            j, value = side_product(packed, held_near, tiles, jj, low_side, narrow)
            total[j] = total[j] + value

    when_active(step or None, sections, body)


def outer_kernel(step, sections, lats, tiles, shots, ends, late, packed, total, far, *refs):
    narrow = bool(step)
    scale, base, other = None, None, None
    if narrow:
        (scale, base), refs = refs[:2], refs[2:]
    if ends:
        other, _, _, result_down, result_up, held, leaving, sems = refs
    else:
        outs, held = refs[:-1], refs[-1]
    lat = lax.axis_index("lat")
    depth = lax.axis_index("depth")
    low_side = lax.rem(lat, 2) == 0
    has_far = (lat > 0) & (lat < lats - 1)

    def body():
        sign = jnp.where(depth == (step or 0), 1.0, -1.0)

        def copy_of(j, result):
            at = pl.ds(pl.multiple_of(j * TILE, TILE), TILE)
            return pltpu.make_async_copy(leaving.at[at], result.at[0, at], sems.at[j])

        def finish(j, value):
            at = pl.ds(pl.multiple_of(j * HALF, HALF), HALF)
            if not narrow:
                for out, part in zip(outs, parted(combined(value, shots))):
                    out[at] = part
                return
            value = combined(value + turned(value), shots)
            part = jnp.where(left_half(HALF), value[:HALF], value[HALF:]) + base[at]
            if ends:
                leaving[pl.ds(pl.multiple_of(j * TILE, TILE), TILE)] = merged(other[at], part)
                pl.when(depth == step)(lambda: copy_of(j, result_down).start())
                pl.when(depth != step)(lambda: copy_of(j, result_up).start())
            else:
                outs[0][at] = part

        @pl.when(has_far)
        def _():
            spread(far, scale, sign, tiles, narrow, low_side, held)
            for jj in range(tiles):
                j, value = side_product(packed, held, tiles, jj, low_side, narrow)
                finish(j, total[j] + value)

        @pl.when(jnp.logical_not(has_far))
        def _():
            for j in range(tiles):
                finish(j, total[j])

        if ends:

            def wait_all(result):
                for j in range(tiles):
                    copy_of(j, result).wait()

            pl.when(depth == step)(lambda: wait_all(result_down))
            pl.when(depth != step)(lambda: wait_all(result_up))

    if late:
        pl.when((depth > 0) & (depth < sections - 1))(body)
    else:
        when_active(step, sections, body)


def keep_kernel(sections, tiles, *refs):
    fields, (result_down, result_up, whole, sems) = refs[:-4], refs[-4:]
    depth = lax.axis_index("depth")

    def put(first, second, result):
        for j in range(tiles):
            whole[rows_of(j)] = merged(first[halves_of(j)], second[halves_of(j)])
        copy = pltpu.make_async_copy(whole, result.at[0], sems)
        copy.start()
        copy.wait()

    for step in range(sections - 1):
        first, second = fields[2 * step : 2 * step + 2]
        pl.when(depth == step)(functools.partial(put, first, second, result_down))
        pl.when(depth == sections - 1 - step)(functools.partial(put, first, second, result_up))


def shards(sections, lats, operator, band_shift, reflectivity, up_stored, down_stored, sources, assignment):
    tiles, band = operator.shape[1], operator.shape[2]
    _, columns = sources.shape
    shots = columns // 4
    rows = tiles * TILE
    if sections % 2 or lats % 2 or tiles != band // 2 + 1 or columns != TILE:
        raise ValueError("unsupported sizes")

    def move(x, partner):
        pairs = []
        for d in range(sections):
            for l in range(lats):
                e, m = partner(d, l)
                pairs.append((d * lats + l, e * lats + m))
        return lax.ppermute(x, ("depth", "lat"), pairs)

    def near_of(d, l):
        return d, l ^ 1

    def far_of(spare, d, l):
        m = l + 1 if l % 2 else l - 1
        return (d, m) if 0 <= m < lats else (spare(d), l)

    def across(step, d, l):
        for low in (step, sections - 2 - step):
            if d == low:
                return low + 1, l
            if d == low + 1:
                return low, l
        return near_of(d, l)

    def halo(field, spare):
        near = move(field, near_of)
        return near, move(field, functools.partial(far_of, spare))

    def next_door(d):
        return d ^ 1

    first, second = call(
        functools.partial(prep_kernel, tiles, shots, sections),
        out_shape=[f32(rows + 8, columns), f32(rows, columns)],
        in_specs=[spec(pltpu.HBM)] * 5,
        out_specs=[spec(VMEM)] * 2,
        scratch_shapes=[
            pltpu.SMEM(assignment.shape, jnp.int32),
            VMEM(reflectivity.shape, jnp.float32),
            VMEM(up_stored.shape, jnp.float32),
            VMEM(down_stored.shape, jnp.float32),
            VMEM(sources.shape, jnp.float32),
            pltpu.SemaphoreType.DMA((5,)),
        ],
        compiler_params=params(),
        cost_estimate=cost(10**7, 5 * rows * columns * 4),
    )(*map(in_hbm, (assignment, reflectivity, up_stored, down_stored, sources)))

    packed = call(
        functools.partial(pack_kernel, tiles, band),
        out_shape=jax.ShapeDtypeStruct((tiles, band + 2, 2 * TILE, 2 * TILE), jnp.bfloat16),
        in_specs=[spec(pltpu.HBM)] * 2,
        out_specs=spec(VMEM),
        scratch_shapes=[
            pltpu.SMEM(band_shift.shape, jnp.int32),
            VMEM(operator.shape[1:], jnp.float32),
            pltpu.SemaphoreType.DMA((tiles + 1,)),
        ],
        compiler_params=params(),
        cost_estimate=cost(10**7, 2 * operator.size * 4),
    )(in_hbm(band_shift), in_hbm(operator))

    square = f32(tiles, TILE, columns)
    half = f32(rows // STREAMS, columns)
    result = [f32(1, rows, columns)] * 2

    def held(step):
        return VMEM((tiles * 2 * TILE, TILE if step else 2 * TILE), jnp.bfloat16)

    def inner(step, own, near, *scales):
        args = [packed, own, near, *scales]
        return call(
            functools.partial(inner_kernel, step, sections, tiles),
            out_shape=f32(tiles, 2 * TILE, columns),
            in_specs=[spec(VMEM)] * len(args),
            out_specs=spec(VMEM),
            scratch_shapes=[held(step)] * 2,
            compiler_params=params(),
            cost_estimate=cost(2 * 40 * 256**3, 8 * 2**20),
        )(*args)

    def outer(step, *args, shapes, kept=(), late=False):
        count = len(args) + 1
        ends = bool(kept)
        scratch = [held(step)]
        if ends:
            scratch += [VMEM((rows, columns), jnp.float32), pltpu.SemaphoreType.DMA((tiles,))]
        return call(
            functools.partial(outer_kernel, step, sections, lats, tiles, shots, ends, late),
            out_shape=shapes,
            in_specs=[spec(VMEM)] * count + [spec(pl.ANY)] * len(kept),
            out_specs=[spec(pl.ANY if ends else VMEM)] * len(shapes),
            scratch_shapes=scratch,
            input_output_aliases={count: 0, count + 1: 1} if ends else {},
            compiler_params=params(),
            cost_estimate=cost(2 * 15 * 256**3, 4 * 2**20),
        )(packed, *args, *kept)

    def cross(step, field):
        return [move(part, functools.partial(across, step)) for part in field]

    first_near, first_far = halo(first, next_door)
    total = inner(0, first, first_near)
    fields = [outer(0, total, first_far, shapes=[half] * STREAMS)]
    first_base = outer(0, total, first_far, shapes=[half] * STREAMS, late=True)
    arrived = cross(0, fields[0])

    second, *_ = lax.optimization_barrier((second, *fields[0]))
    near, far = halo(second, lambda d: (d + sections // 2) % sections)
    own_scale, near_scale, far_scale = call(
        functools.partial(scale_kernel, tiles),
        out_shape=[square] * 3,
        in_specs=[spec(VMEM)] * 3,
        out_specs=[spec(VMEM)] * 3,
        compiler_params=params(),
        cost_estimate=cost(10**6, 4 * rows * columns * 4),
    )(first, first_near, first_far)
    total = inner(None, second, near)
    second_base = outer(None, total, far, shapes=[half] * STREAMS)

    for step in range(1, sections):
        bases = first_base if step < sections // 2 else second_base
        field = []
        for q in range(STREAMS):
            near, far = halo(arrived[q], next_door)
            total = inner(step, arrived[q], near, own_scale, near_scale)
            if step == sections - 1 and q == STREAMS - 1:
                kept = call(
                    functools.partial(keep_kernel, sections, tiles),
                    out_shape=result,
                    in_specs=[spec(VMEM)] * (len(fields) * STREAMS),
                    out_specs=[spec(pl.ANY)] * 2,
                    scratch_shapes=[VMEM((rows, columns), jnp.float32), pltpu.SemaphoreType.DMA(())],
                    compiler_params=params(),
                    cost_estimate=cost(0, 4 * rows * columns * 4),
                )(*[part for field_ in fields for part in field_])
                ended = outer(
                    step, total, far, far_scale, bases[q], field[0], shapes=result, kept=kept
                )
                return tuple(ended)
            (part,) = outer(step, total, far, far_scale, bases[q], shapes=[half])
            field.append(part)
        fields.append(field)
        arrived = cross(step, field)


def solution(mesh):
    return jax.shard_map(
        functools.partial(shards, mesh.shape["depth"], mesh.shape["lat"]),
        mesh=mesh,
        in_specs=(
            P("depth", "lat", None, None, None),
            P("depth", "lat"),
            P("depth", "lat"),
            P("depth", "lat", None),
            P("depth", "lat", None),
            P("lat", None),
            P(),
        ),
        out_specs=(P("depth", "lat", None), P("depth", "lat", None)),
        check_vma=False,
    )
```

```python
import functools

import jax
import jax.numpy as jnp
from jax import lax
from jax.experimental import pallas as pl
from jax.experimental.pallas import tpu as pltpu
from jax.sharding import PartitionSpec as P


TILE = 128
HALF = TILE // 2
VMEM = pltpu.VMEM
LIMIT = 16 * 2**20
STREAMS = 2


def spec(space):
    return pl.BlockSpec(memory_space=space)


def f32(*shape):
    return jax.ShapeDtypeStruct(shape, jnp.float32)


def call(kernel, **kwargs):
    return pl.pallas_call(kernel, **kwargs)


def params(limit=LIMIT):
    return pltpu.CompilerParams(vmem_limit_bytes=limit)


def cost(flops, read):
    return pl.CostEstimate(flops=flops, bytes_accessed=read, transcendentals=0)


def in_hbm(x):
    return pltpu.with_memory_space_constraint(x, pltpu.HBM)


def rows_of(t):
    return slice(t * TILE, (t + 1) * TILE)


def down_column(row):
    return jnp.transpose(jnp.broadcast_to(row, (TILE, TILE)))


def split(value):
    high = value.astype(jnp.bfloat16)
    low = (value - high.astype(jnp.float32)).astype(jnp.bfloat16)
    return high, low


def prep_kernel(tiles, shots, sections, assign_at, refl_at, up_at, down_at, src_at, first, second, assign, refl, up, down, src, sems):
    depth = lax.axis_index("depth")
    loads = [
        pltpu.make_async_copy(assign_at, assign, sems.at[0]),
        pltpu.make_async_copy(refl_at, refl, sems.at[1]),
        pltpu.make_async_copy(up_at, up, sems.at[2]),
        pltpu.make_async_copy(down_at, down, sems.at[3]),
        pltpu.make_async_copy(src_at, src, sems.at[4]),
    ]
    for load in loads:
        load.start()
    for load in loads:
        load.wait()
    descends = depth < sections // 2

    def write(of_up, of_down):
        for j in range(tiles):
            row = refl[0:1, rows_of(j)]
            r = down_column(row)
            of_up[rows_of(j)] = -(r * up[0, rows_of(j)])
            of_down[rows_of(j)] = r * down[0, rows_of(j)]
            first[tiles * TILE + j : tiles * TILE + j + 1] = row

    @pl.when(descends)
    def _():
        write(first, second)

    @pl.when(jnp.logical_not(descends))
    def _():
        write(second, first)

    @pl.when(depth == 0)
    def _():
        lane = lax.broadcasted_iota(jnp.int32, (8, TILE), 1)
        wanted = jnp.zeros((8, TILE), jnp.int32)
        for b in range(TILE // (2 * shots)):
            for i in range(shots):
                shot = assign[b * shots + i]
                at = b * 2 * shots + i
                wanted = jnp.where(lane == at, shot, wanted)
                wanted = jnp.where(lane == at + shots, shot + TILE // 2, wanted)
        source = lax.broadcasted_iota(jnp.int32, (TILE, TILE), 0)
        pick = (source == jnp.broadcast_to(wanted[0:1], (TILE, TILE))).astype(jnp.float32).astype(jnp.bfloat16)
        for j in range(tiles):
            x = src[rows_of(j)]
            high = x.astype(jnp.bfloat16)
            mid, low = split(x - high.astype(jnp.float32))
            entering = jnp.dot(low, pick, preferred_element_type=jnp.float32)
            entering += jnp.dot(mid, pick, preferred_element_type=jnp.float32)
            entering += jnp.dot(high, pick, preferred_element_type=jnp.float32)
            r = down_column(refl[0:1, rows_of(j)])
            first[rows_of(j)] = (1.0 + r) * entering + first[rows_of(j)]


def pack_kernel(tiles, band, shift_at, tiles_at, out, shift, held, sems):
    loads = [pltpu.make_async_copy(shift_at, shift, sems.at[tiles])]
    loads += [pltpu.make_async_copy(tiles_at.at[0, j], held.at[j], sems.at[j]) for j in range(tiles)]
    for load in loads:
        load.start()
    loads[0].wait()
    for j in range(tiles):
        loads[1 + j].wait()
        move = shift[0, j]
        for k in range(band):
            high, low = split(held[j, k])
            slot = k + 1 + move
            out[j, slot, :, :TILE] = high
            out[j, slot, :, TILE:] = low
        zero = jnp.zeros(out.shape[2:], jnp.bfloat16)
        out[j, jnp.where(move >= 0, 0, band)] = zero
        out[j, jnp.where(move <= 0, band + 1, 1)] = zero


def doubled(tile):
    high, low = split(tile)
    line = jnp.concatenate([high, low], axis=1)
    return jnp.concatenate([line, line], axis=0)


def folded(value):
    return value[:, :TILE] + value[:, TILE:]


def lanes(rows):
    return lax.broadcasted_iota(jnp.int32, (rows, TILE), 1)


def turned(value):
    return pltpu.roll(value, HALF, 1)


def left_half(rows):
    return lanes(rows) < HALF


def halves_of(t):
    return slice(t * HALF, (t + 1) * HALF)


def unpack_tile(chunk, t):
    part = chunk[halves_of(t)]
    return jnp.concatenate([part, turned(part)], axis=0)


def stream_line(tile):
    rest = tile - tile.astype(jnp.bfloat16).astype(jnp.float32)
    line = jnp.where(left_half(TILE), tile, turned(rest)).astype(jnp.bfloat16)
    return jnp.concatenate([line, line], axis=0)


def merged(first, second):
    left = left_half(HALF)
    upper = jnp.where(left, first, turned(second))
    lower = jnp.where(left, turned(first), second)
    return jnp.concatenate([upper, lower], axis=0)


def parted(value):
    upper, lower = value[:HALF], value[HALF:]
    left = left_half(HALF)
    return jnp.where(left, upper, turned(lower)), jnp.where(left, turned(upper), lower)


def full_tile(field, t):
    if len(field) == 1:
        return field[0][rows_of(t)]
    return merged(*[part[halves_of(t)] for part in field])


def spread(field, scale, sign, tiles, narrow, mirrored, held):
    for t in range(tiles):
        tile = unpack_tile(field[0], t) if narrow else full_tile(field, t)
        if scale is not None:
            tile = tile * (1.0 + sign * scale[t])
        at = 2 * t * TILE
        if mirrored is not None:
            at = pl.multiple_of(jnp.where(mirrored, 2 * (tiles - 1 - t) * TILE, at), 2 * TILE)
        held[pl.ds(at, 2 * TILE)] = stream_line(tile) if narrow else doubled(tile)


def product(packed, held, j, slots, narrow):
    value = jnp.dot(
        jnp.concatenate([packed[j, slot] for slot in slots], axis=1),
        held[: 2 * len(slots) * TILE],
        preferred_element_type=jnp.float32,
    )
    return value if narrow else folded(value)


def side_product(packed, held, tiles, jj, low_side, narrow):
    j = jnp.where(low_side, tiles - 1 - jj, jj)
    slots = [jnp.where(low_side, jj - t, 2 * tiles + t - jj) for t in range(jj + 1)]
    return j, product(packed, held, j, slots, narrow)


def when_active(step, sections, body):
    depth = lax.axis_index("depth")
    if step is None:
        body()
    else:
        pl.when((depth == step) | (depth == sections - 1 - step))(body)


def combined(value, shots):
    by_imag = value[TILE:]
    ahead = pltpu.roll(by_imag, TILE - shots, 1)
    behind = pltpu.roll(by_imag, shots, 1)
    return value[:TILE] + jnp.where(lax.rem(lanes(TILE), 2 * shots) < shots, -ahead, behind)


def scale_kernel(tiles, *refs):
    for source, out in zip(refs[:3], refs[3:]):
        for t in range(tiles):
            at = tiles * TILE + t
            out[t] = down_column(source[at : at + 1])


def inner_kernel(step, sections, tiles, parts, packed, *refs):
    narrow = bool(step) and parts == 1
    own, near, refs = refs[:parts], refs[parts : 2 * parts], refs[2 * parts :]
    scale, near_scale = refs[:2] if step else (None, None)
    total, held_own, held_near = refs[-3:]

    def body():
        sign = jnp.where(lax.axis_index("depth") == (step or 0), 1.0, -1.0)
        low_side = lax.rem(lax.axis_index("lat"), 2) == 1
        spread(own, scale, sign, tiles, narrow, None, held_own)
        spread(near, near_scale, sign, tiles, narrow, low_side, held_near)
        for j in range(tiles):
            total[j] = product(packed, held_own, j, range(tiles - j, 2 * tiles - j), narrow)
        for jj in range(tiles):
            j, value = side_product(packed, held_near, tiles, jj, low_side, narrow)
            total[j] = total[j] + value

    when_active(step or None, sections, body)


def outer_kernel(step, sections, lats, tiles, shots, parts, ends, late, packed, total, *refs):
    narrow = bool(step) and not ends
    far, refs = refs[:parts], refs[parts:]
    scale, base = None, None
    if step:
        scale, base, refs = refs[0], refs[1 : 1 + parts], refs[1 + parts :]
    if ends:
        _, _, result_down, result_up, held, leaving, sems = refs
    else:
        outs, held = refs[:-1], refs[-1]
    lat = lax.axis_index("lat")
    depth = lax.axis_index("depth")
    low_side = lax.rem(lat, 2) == 0
    has_far = (lat > 0) & (lat < lats - 1)

    def body():
        sign = jnp.where(depth == (step or 0), 1.0, -1.0)

        def copy_of(j, result):
            at = pl.ds(pl.multiple_of(j * TILE, TILE), TILE)
            return pltpu.make_async_copy(leaving.at[at], result.at[0, at], sems.at[j])

        def finish(j, value):
            at = pl.ds(pl.multiple_of(j * HALF, HALF), HALF)
            if narrow:
                value = combined(value + turned(value), shots)
                outs[0][at] = jnp.where(left_half(HALF), value[:HALF], value[HALF:]) + base[0][at]
                return
            value = combined(value, shots)
            if ends:
                value = value + merged(*[part[at] for part in base])
                leaving[pl.ds(pl.multiple_of(j * TILE, TILE), TILE)] = value
                pl.when(depth == step)(lambda: copy_of(j, result_down).start())
                pl.when(depth != step)(lambda: copy_of(j, result_up).start())
                return
            for out, part in zip(outs, parted(value)):
                out[at] = part

        @pl.when(has_far)
        def _():
            spread(far, scale, sign, tiles, narrow, low_side, held)
            for jj in range(tiles):
                j, value = side_product(packed, held, tiles, jj, low_side, narrow)
                finish(j, total[j] + value)

        @pl.when(jnp.logical_not(has_far))
        def _():
            for j in range(tiles):
                finish(j, total[j])

        if ends:

            def wait_all(result):
                for j in range(tiles):
                    copy_of(j, result).wait()

            pl.when(depth == step)(lambda: wait_all(result_down))
            pl.when(depth != step)(lambda: wait_all(result_up))

    if late:
        pl.when((depth > 0) & (depth < sections - 1))(body)
    else:
        when_active(step, sections, body)


def keep_kernel(sections, tiles, steps, *refs):
    fields, (result_down, result_up, whole, sems) = refs[: 2 * len(steps)], refs[-4:]
    depth = lax.axis_index("depth")

    def put(first, second, result):
        for j in range(tiles):
            whole[rows_of(j)] = merged(first[halves_of(j)], second[halves_of(j)])
        copy = pltpu.make_async_copy(whole, result.at[0], sems)
        copy.start()
        copy.wait()

    for i, step in enumerate(steps):
        first, second = fields[2 * i : 2 * i + 2]
        pl.when(depth == step)(functools.partial(put, first, second, result_down))
        pl.when(depth == sections - 1 - step)(functools.partial(put, first, second, result_up))


def shards(sections, lats, operator, band_shift, reflectivity, up_stored, down_stored, sources, assignment):
    tiles, band = operator.shape[1], operator.shape[2]
    _, columns = sources.shape
    shots = columns // 4
    rows = tiles * TILE
    if sections % 2 or lats % 2 or tiles != band // 2 + 1 or columns != TILE:
        raise ValueError("unsupported sizes")

    def move(x, partner):
        pairs = []
        for d in range(sections):
            for l in range(lats):
                e, m = partner(d, l)
                pairs.append((d * lats + l, e * lats + m))
        return lax.ppermute(x, ("depth", "lat"), pairs)

    def near_of(d, l):
        return d, l ^ 1

    def far_of(spare, d, l):
        m = l + 1 if l % 2 else l - 1
        return (d, m) if 0 <= m < lats else (spare(d), l)

    def across(step, d, l):
        for low in (step, sections - 2 - step):
            if d == low:
                return low + 1, l
            if d == low + 1:
                return low, l
        return near_of(d, l)

    def halo(field, spare):
        near = move(field, near_of)
        return near, move(field, functools.partial(far_of, spare))

    def next_door(d):
        return (d + sections // 2) % sections

    first, second = call(
        functools.partial(prep_kernel, tiles, shots, sections),
        out_shape=[f32(rows + 8, columns), f32(rows, columns)],
        in_specs=[spec(pltpu.HBM)] * 5,
        out_specs=[spec(VMEM)] * 2,
        scratch_shapes=[
            pltpu.SMEM(assignment.shape, jnp.int32),
            VMEM(reflectivity.shape, jnp.float32),
            VMEM(up_stored.shape, jnp.float32),
            VMEM(down_stored.shape, jnp.float32),
            VMEM(sources.shape, jnp.float32),
            pltpu.SemaphoreType.DMA((5,)),
        ],
        compiler_params=params(),
        cost_estimate=cost(10**7, 5 * rows * columns * 4),
    )(*map(in_hbm, (assignment, reflectivity, up_stored, down_stored, sources)))

    packed = call(
        functools.partial(pack_kernel, tiles, band),
        out_shape=jax.ShapeDtypeStruct((tiles, band + 2, 2 * TILE, 2 * TILE), jnp.bfloat16),
        in_specs=[spec(pltpu.HBM)] * 2,
        out_specs=spec(VMEM),
        scratch_shapes=[
            pltpu.SMEM(band_shift.shape, jnp.int32),
            VMEM(operator.shape[1:], jnp.float32),
            pltpu.SemaphoreType.DMA((tiles + 1,)),
        ],
        compiler_params=params(),
        cost_estimate=cost(10**7, 2 * operator.size * 4),
    )(in_hbm(band_shift), in_hbm(operator))

    square = f32(tiles, TILE, columns)
    half = f32(rows // STREAMS, columns)
    result = [f32(1, rows, columns)] * 2

    def held(narrow):
        return VMEM((tiles * 2 * TILE, TILE if narrow else 2 * TILE), jnp.bfloat16)

    def inner(step, own, near, *scales):
        args = [packed, *own, *near, *scales]
        return call(
            functools.partial(inner_kernel, step, sections, tiles, len(own)),
            out_shape=f32(tiles, 2 * TILE, columns),
            in_specs=[spec(VMEM)] * len(args),
            out_specs=spec(VMEM),
            scratch_shapes=[held(step and len(own) == 1)] * 2,
            compiler_params=params(),
            cost_estimate=cost(2 * 40 * 256**3, 8 * 2**20),
        )(*args)

    def outer(step, total, far, *more, shapes, kept=(), late=False):
        ends = bool(kept)
        args = [packed, total, *far, *more]
        count = len(args)
        scratch = [held(step and not ends)]
        if ends:
            scratch += [VMEM((rows, columns), jnp.float32), pltpu.SemaphoreType.DMA((tiles,))]
        return call(
            functools.partial(outer_kernel, step, sections, lats, tiles, shots, len(far), ends, late),
            out_shape=shapes,
            in_specs=[spec(VMEM)] * count + [spec(pl.ANY)] * len(kept),
            out_specs=[spec(pl.ANY if ends else VMEM)] * len(shapes),
            scratch_shapes=scratch,
            input_output_aliases={count: 0, count + 1: 1} if ends else {},
            compiler_params=params(),
            cost_estimate=cost(2 * 15 * 256**3, 4 * 2**20),
        )(*args, *kept)

    def keep(steps, kept=()):
        args = [part for step in steps for part in fields[step]]
        count = len(args)
        return call(
            functools.partial(keep_kernel, sections, tiles, steps),
            out_shape=result,
            in_specs=[spec(VMEM)] * count + [spec(pl.ANY)] * len(kept),
            out_specs=[spec(pl.ANY)] * 2,
            scratch_shapes=[VMEM((rows, columns), jnp.float32), pltpu.SemaphoreType.DMA(())],
            input_output_aliases={count: 0, count + 1: 1} if kept else {},
            compiler_params=params(),
            cost_estimate=cost(0, 4 * rows * columns * 4),
        )(*args, *kept)

    def cross(step, field):
        return [move(part, functools.partial(across, step)) for part in field]

    first_near, first_far = halo(first, next_door)
    total = inner(0, [first], [first_near])
    fields = [outer(0, total, [first_far], shapes=[half] * STREAMS)]
    first_base = outer(0, total, [first_far], shapes=[half] * STREAMS, late=True)
    arrived = cross(0, fields[0])

    second, *_ = lax.optimization_barrier((second, *fields[0]))
    near, far = halo(second, next_door)
    own_scale, near_scale, far_scale = call(
        functools.partial(scale_kernel, tiles),
        out_shape=[square] * 3,
        in_specs=[spec(VMEM)] * 3,
        out_specs=[spec(VMEM)] * 3,
        compiler_params=params(),
        cost_estimate=cost(10**6, 4 * rows * columns * 4),
    )(first, first_near, first_far)
    total = inner(None, [second], [near])
    second_base = outer(None, total, [far], shapes=[half] * STREAMS)

    middle = sections // 2
    for step in range(1, sections):
        bases = first_base if step < middle else second_base
        halos = [halo(part, next_door) for part in arrived]
        nears, fars = zip(*halos)
        if step == sections - 1:
            total = inner(step, arrived, nears, own_scale, near_scale)
            kept = keep(range(middle - 1)) if middle > 1 else ()
            kept = keep(range(middle - 1, step), kept)
            return tuple(outer(step, total, fars, far_scale, *bases, shapes=result, kept=kept))
        field = []
        for q in range(STREAMS):
            total = inner(step, [arrived[q]], [nears[q]], own_scale, near_scale)
            field += outer(step, total, [fars[q]], far_scale, bases[q], shapes=[half])
        fields.append(field)
        arrived = cross(step, field)


def solution(mesh):
    return jax.shard_map(
        functools.partial(shards, mesh.shape["depth"], mesh.shape["lat"]),
        mesh=mesh,
        in_specs=(
            P("depth", "lat", None, None, None),
            P("depth", "lat"),
            P("depth", "lat"),
            P("depth", "lat", None),
            P("depth", "lat", None),
            P("lat", None),
            P(),
        ),
        out_specs=(P("depth", "lat", None), P("depth", "lat", None)),
        check_vma=False,
    )
```

```python
import functools

import jax
import jax.numpy as jnp
from jax import lax
from jax.experimental import pallas as pl
from jax.experimental.pallas import tpu as pltpu
from jax.sharding import PartitionSpec as P


TILE = 128
HALF = TILE // 2
VMEM = pltpu.VMEM
LIMIT = 16 * 2**20
STREAMS = 2


def spec(space):
    return pl.BlockSpec(memory_space=space)


def f32(*shape):
    return jax.ShapeDtypeStruct(shape, jnp.float32)


def call(kernel, **kwargs):
    return pl.pallas_call(kernel, **kwargs)


def params(limit=LIMIT):
    return pltpu.CompilerParams(vmem_limit_bytes=limit)


def cost(flops, read):
    return pl.CostEstimate(flops=flops, bytes_accessed=read, transcendentals=0)


def in_hbm(x):
    return pltpu.with_memory_space_constraint(x, pltpu.HBM)


def rows_of(t):
    return slice(t * TILE, (t + 1) * TILE)


def down_column(row):
    return jnp.transpose(jnp.broadcast_to(row, (TILE, TILE)))


def split(value):
    high = value.astype(jnp.bfloat16)
    low = (value - high.astype(jnp.float32)).astype(jnp.bfloat16)
    return high, low


def prep_kernel(tiles, shots, sections, assign_at, refl_at, up_at, down_at, src_at, first, second, *refs):
    *streams, assign, refl, up, down, src, pick, sems = refs
    depth = lax.axis_index("depth")
    loads = [
        pltpu.make_async_copy(assign_at, assign, sems.at[0]),
        pltpu.make_async_copy(refl_at, refl, sems.at[1]),
        pltpu.make_async_copy(src_at, src, sems.at[2]),
        pltpu.make_async_copy(up_at, up, sems.at[3]),
        pltpu.make_async_copy(down_at, down, sems.at[4]),
    ]
    for load in loads:
        load.start()
    loads[0].wait()

    @pl.when(depth == 0)
    def _():
        lane = lax.broadcasted_iota(jnp.int32, (8, TILE), 1)
        wanted = jnp.zeros((8, TILE), jnp.int32)
        for b in range(TILE // (2 * shots)):
            for i in range(shots):
                shot = assign[b * shots + i]
                at = b * 2 * shots + i
                wanted = jnp.where(lane == at, shot, wanted)
                wanted = jnp.where(lane == at + shots, shot + TILE // 2, wanted)
        source = lax.broadcasted_iota(jnp.int32, (TILE, TILE), 0)
        found = source == jnp.broadcast_to(wanted[0:1], (TILE, TILE))
        pick[...] = found.astype(jnp.float32).astype(jnp.bfloat16)

    for load in loads[1:]:
        load.wait()
    descends = depth < sections // 2

    def of_up(j):
        return -(down_column(refl[0:1, rows_of(j)]) * up[0, rows_of(j)])

    def of_down(j):
        return down_column(refl[0:1, rows_of(j)]) * down[0, rows_of(j)]

    def put(j, tile, later):
        first[rows_of(j)] = tile
        for stream, part in zip(streams, parted(tile)):
            stream[halves_of(j)] = part
        second[rows_of(j)] = later

    for j in range(tiles):
        row = refl[0:1, rows_of(j)]
        first[tiles * TILE + j : tiles * TILE + j + 1] = row
        streams[0][tiles * HALF + j : tiles * HALF + j + 1] = row

    @pl.when(descends & (depth > 0))
    def _():
        for j in range(tiles):
            put(j, of_up(j), of_down(j))

    @pl.when(jnp.logical_not(descends))
    def _():
        for j in range(tiles):
            put(j, of_down(j), of_up(j))

    @pl.when(depth == 0)
    def _():
        for j in range(tiles):
            x = src[rows_of(j)]
            high = x.astype(jnp.bfloat16)
            mid, low = split(x - high.astype(jnp.float32))
            entering = jnp.dot(low, pick[...], preferred_element_type=jnp.float32)
            entering += jnp.dot(mid, pick[...], preferred_element_type=jnp.float32)
            entering += jnp.dot(high, pick[...], preferred_element_type=jnp.float32)
            r = down_column(refl[0:1, rows_of(j)])
            put(j, (1.0 + r) * entering + of_up(j), of_down(j))


def doubled(tile):
    high, low = split(tile)
    line = jnp.concatenate([high, low], axis=1)
    return jnp.concatenate([line, line], axis=0)


def folded(value):
    return value[:, :TILE] + value[:, TILE:]


def lanes(rows):
    return lax.broadcasted_iota(jnp.int32, (rows, TILE), 1)


def turned(value):
    return pltpu.roll(value, HALF, 1)


def left_half(rows):
    return lanes(rows) < HALF


def halves_of(t):
    return slice(t * HALF, (t + 1) * HALF)


def unpack_tile(chunk, t):
    part = chunk[halves_of(t)]
    return jnp.concatenate([part, turned(part)], axis=0)


def stream_line(tile):
    rest = tile - tile.astype(jnp.bfloat16).astype(jnp.float32)
    line = jnp.where(left_half(TILE), tile, turned(rest)).astype(jnp.bfloat16)
    return jnp.concatenate([line, line], axis=0)


def merged(first, second):
    left = left_half(HALF)
    upper = jnp.where(left, first, turned(second))
    lower = jnp.where(left, turned(first), second)
    return jnp.concatenate([upper, lower], axis=0)


def parted(value):
    upper, lower = value[:HALF], value[HALF:]
    left = left_half(HALF)
    return jnp.where(left, upper, turned(lower)), jnp.where(left, turned(upper), lower)


def full_tile(field, t):
    if len(field) == 1:
        return field[0][rows_of(t)]
    return merged(*[part[halves_of(t)] for part in field])


def spread(field, scale, sign, tiles, narrow, mirrored, held):
    for t in range(tiles):
        tile = unpack_tile(field[0], t) if narrow else full_tile(field, t)
        if scale is not None:
            tile = tile * (1.0 + sign * scale[t])
        at = 2 * t * TILE
        if mirrored is not None:
            at = pl.multiple_of(jnp.where(mirrored, 2 * (tiles - 1 - t) * TILE, at), 2 * TILE)
        held[pl.ds(at, 2 * TILE)] = stream_line(tile) if narrow else doubled(tile)


def product(packed, held, j, slots, narrow):
    value = jnp.dot(
        jnp.concatenate([packed[j, slot] for slot in slots], axis=1),
        held[: 2 * len(slots) * TILE],
        preferred_element_type=jnp.float32,
    )
    return value if narrow else folded(value)


def side_product(packed, held, tiles, jj, low_side, narrow):
    j = jnp.where(low_side, tiles - 1 - jj, jj)
    slots = [jnp.where(low_side, jj - t, 2 * tiles + t - jj) for t in range(jj + 1)]
    return j, product(packed, held, j, slots, narrow)


def when_active(step, sections, body):
    depth = lax.axis_index("depth")
    if step is None:
        body()
    else:
        pl.when((depth == step) | (depth == sections - 1 - step))(body)


def combined(value, shots):
    by_imag = value[TILE:]
    ahead = pltpu.roll(by_imag, TILE - shots, 1)
    behind = pltpu.roll(by_imag, shots, 1)
    return value[:TILE] + jnp.where(lax.rem(lanes(TILE), 2 * shots) < shots, -ahead, behind)


def scale_kernel(tiles, *refs):
    for source, out in zip(refs[:3], refs[3:]):
        for t in range(tiles):
            at = source.shape[0] - 8 + t
            out[t] = down_column(source[at : at + 1])


def pack_kernel(tiles, band, shift_at, tiles_at, own, near, packed, total, shift, raw, held_own, held_near, sems):
    loads = [pltpu.make_async_copy(shift_at, shift, sems.at[tiles])]
    loads += [pltpu.make_async_copy(tiles_at.at[0, j], raw.at[j], sems.at[j]) for j in range(tiles)]
    for load in loads:
        load.start()
    low_side = lax.rem(lax.axis_index("lat"), 2) == 1
    spread([own], None, None, tiles, False, None, held_own)
    spread([near], None, None, tiles, False, low_side, held_near)
    zero = jnp.zeros(packed.shape[2:], jnp.bfloat16)
    loads[0].wait()
    for j in range(tiles):
        loads[1 + j].wait()
        move = shift[0, j]
        for k in range(band):
            high, low = split(raw[j, k])
            slot = k + 1 + move
            packed[j, slot, :, :TILE] = high
            packed[j, slot, :, TILE:] = low
        packed[j, jnp.where(move >= 0, 0, band)] = zero
        packed[j, jnp.where(move <= 0, band + 1, 1)] = zero
        total[j] = product(packed, held_own, j, range(tiles - j, 2 * tiles - j), False)
    for jj in range(tiles):
        j, value = side_product(packed, held_near, tiles, jj, low_side, False)
        total[j] = total[j] + value


def inner_kernel(step, sections, tiles, parts, packed, *refs):
    narrow = bool(step) and parts == 1
    own, near, refs = refs[:parts], refs[parts : 2 * parts], refs[2 * parts :]
    scale, near_scale = refs[:2] if step else (None, None)
    total, held_own, held_near = refs[-3:]

    def body():
        sign = jnp.where(lax.axis_index("depth") == (step or 0), 1.0, -1.0)
        low_side = lax.rem(lax.axis_index("lat"), 2) == 1
        spread(own, scale, sign, tiles, narrow, None, held_own)
        spread(near, near_scale, sign, tiles, narrow, low_side, held_near)
        for j in range(tiles):
            total[j] = product(packed, held_own, j, range(tiles - j, 2 * tiles - j), narrow)
        for jj in range(tiles):
            j, value = side_product(packed, held_near, tiles, jj, low_side, narrow)
            total[j] = total[j] + value

    when_active(step or None, sections, body)


def outer_kernel(step, sections, lats, tiles, shots, parts, stream, ends, late, packed, total, *refs):
    narrow = stream is not None
    far, refs = refs[:parts], refs[parts:]
    scale, base = None, None
    if step:
        scale, base, refs = refs[0], refs[1 : 1 + parts], refs[1 + parts :]
    if ends:
        _, _, result_down, result_up, held, leaving, sems = refs
    else:
        outs, held = refs[:-1], refs[-1]
    lat = lax.axis_index("lat")
    depth = lax.axis_index("depth")
    low_side = lax.rem(lat, 2) == 0
    has_far = (lat > 0) & (lat < lats - 1)

    def body():
        sign = jnp.where(depth == (step or 0), 1.0, -1.0)

        def copy_of(j, result):
            at = pl.ds(pl.multiple_of(j * TILE, TILE), TILE)
            return pltpu.make_async_copy(leaving.at[at], result.at[0, at], sems.at[j])

        def finish(j, value, more):
            at = pl.ds(pl.multiple_of(j * HALF, HALF), HALF)
            if narrow and step == 0:
                mine = left_half(2 * TILE) if stream == 0 else jnp.logical_not(left_half(2 * TILE))
                value = jnp.where(mine, value, turned(value))
                if more is not None:
                    value = value + (more + turned(more))
            else:
                value = value if more is None else value + more
                if narrow:
                    value = value + turned(value)
            value = combined(value, shots)
            if narrow:
                value = jnp.where(left_half(HALF), value[:HALF], value[HALF:])
                outs[0][at] = value if base is None else value + base[0][at]
                return
            if ends:
                value = value + merged(*[part[at] for part in base])
                leaving[pl.ds(pl.multiple_of(j * TILE, TILE), TILE)] = value
                pl.when(depth == step)(lambda: copy_of(j, result_down).start())
                pl.when(depth != step)(lambda: copy_of(j, result_up).start())
                return
            for out, part in zip(outs, parted(value)):
                out[at] = part

        @pl.when(has_far)
        def _():
            spread(far, scale, sign, tiles, narrow, low_side, held)
            for jj in range(tiles):
                j, value = side_product(packed, held, tiles, jj, low_side, narrow)
                finish(j, total[j], value)

        @pl.when(jnp.logical_not(has_far))
        def _():
            for j in range(tiles):
                finish(j, total[j], None)

        if ends:

            def wait_all(result):
                for j in range(tiles):
                    copy_of(j, result).wait()

            pl.when(depth == step)(lambda: wait_all(result_down))
            pl.when(depth != step)(lambda: wait_all(result_up))

    if late:
        pl.when((depth > 0) & (depth < sections - 1))(body)
    else:
        when_active(step, sections, body)


def keep_kernel(sections, tiles, steps, *refs):
    fields, (result_down, result_up, whole, sems) = refs[: 2 * len(steps)], refs[-4:]
    depth = lax.axis_index("depth")

    def put(first, second, result):
        for j in range(tiles):
            whole[rows_of(j)] = merged(first[halves_of(j)], second[halves_of(j)])
        copy = pltpu.make_async_copy(whole, result.at[0], sems)
        copy.start()
        copy.wait()

    for i, step in enumerate(steps):
        first, second = fields[2 * i : 2 * i + 2]
        pl.when(depth == step)(functools.partial(put, first, second, result_down))
        pl.when(depth == sections - 1 - step)(functools.partial(put, first, second, result_up))


def shards(sections, lats, operator, band_shift, reflectivity, up_stored, down_stored, sources, assignment):
    tiles, band = operator.shape[1], operator.shape[2]
    _, columns = sources.shape
    shots = columns // 4
    rows = tiles * TILE
    if sections % 2 or lats % 2 or tiles != band // 2 + 1 or columns != TILE:
        raise ValueError("unsupported sizes")

    def move(x, partner):
        pairs = []
        for d in range(sections):
            for l in range(lats):
                e, m = partner(d, l)
                pairs.append((d * lats + l, e * lats + m))
        return lax.ppermute(x, ("depth", "lat"), pairs)

    def near_of(d, l):
        return d, l ^ 1

    def far_of(spare, d, l):
        m = l + 1 if l % 2 else l - 1
        return (d, m) if 0 <= m < lats else (spare(d), l)

    def across(step, d, l):
        for low in (step, sections - 2 - step):
            if d == low:
                return low + 1, l
            if d == low + 1:
                return low, l
        return near_of(d, l)

    def halo(field, spare):
        near = move(field, near_of)
        return near, move(field, functools.partial(far_of, spare))

    def next_door(d):
        return (d + sections // 2) % sections

    half = f32(rows // STREAMS, columns)
    first, second, *streams = call(
        functools.partial(prep_kernel, tiles, shots, sections),
        out_shape=[f32(rows + 8, columns), f32(rows, columns), f32(rows // STREAMS + 8, columns), half],
        in_specs=[spec(pltpu.HBM)] * 5,
        out_specs=[spec(VMEM)] * 4,
        scratch_shapes=[
            pltpu.SMEM(assignment.shape, jnp.int32),
            VMEM(reflectivity.shape, jnp.float32),
            VMEM(up_stored.shape, jnp.float32),
            VMEM(down_stored.shape, jnp.float32),
            VMEM(sources.shape, jnp.float32),
            VMEM((TILE, TILE), jnp.bfloat16),
            pltpu.SemaphoreType.DMA((5,)),
        ],
        compiler_params=params(),
        cost_estimate=cost(10**7, 5 * rows * columns * 4),
    )(*map(in_hbm, (assignment, reflectivity, up_stored, down_stored, sources)))

    square = f32(tiles, TILE, columns)
    result = [f32(1, rows, columns)] * 2

    def held(narrow):
        return VMEM((tiles * 2 * TILE, TILE if narrow else 2 * TILE), jnp.bfloat16)

    def inner(step, own, near, *scales):
        args = [packed, *own, *near, *scales]
        return call(
            functools.partial(inner_kernel, step, sections, tiles, len(own)),
            out_shape=f32(tiles, 2 * TILE, columns),
            in_specs=[spec(VMEM)] * len(args),
            out_specs=spec(VMEM),
            scratch_shapes=[held(step and len(own) == 1)] * 2,
            compiler_params=params(),
            cost_estimate=cost(2 * 40 * 256**3, 8 * 2**20),
        )(*args)

    def outer(step, total, far, *more, shapes, stream=None, kept=(), late=False):
        ends = bool(kept)
        args = [packed, total, *far, *more]
        count = len(args)
        scratch = [held(stream is not None)]
        if ends:
            scratch += [VMEM((rows, columns), jnp.float32), pltpu.SemaphoreType.DMA((tiles,))]
        return call(
            functools.partial(outer_kernel, step, sections, lats, tiles, shots, len(far), stream, ends, late),
            out_shape=shapes,
            in_specs=[spec(VMEM)] * count + [spec(pl.ANY)] * len(kept),
            out_specs=[spec(pl.ANY if ends else VMEM)] * len(shapes),
            scratch_shapes=scratch,
            input_output_aliases={count: 0, count + 1: 1} if ends else {},
            compiler_params=params(),
            cost_estimate=cost(2 * 15 * 256**3, 4 * 2**20),
        )(*args, *kept)

    def keep(steps, kept=()):
        args = [part for step in steps for part in fields[step]]
        count = len(args)
        return call(
            functools.partial(keep_kernel, sections, tiles, steps),
            out_shape=result,
            in_specs=[spec(VMEM)] * count + [spec(pl.ANY)] * len(kept),
            out_specs=[spec(pl.ANY)] * 2,
            scratch_shapes=[VMEM((rows, columns), jnp.float32), pltpu.SemaphoreType.DMA(())],
            input_output_aliases={count: 0, count + 1: 1} if kept else {},
            compiler_params=params(),
            cost_estimate=cost(0, 4 * rows * columns * 4),
        )(*args, *kept)

    def cross(step, field):
        return [move(part, functools.partial(across, step)) for part in field]

    first_near = move(first, near_of)
    first_fars = [move(part, functools.partial(far_of, next_door)) for part in streams]
    packed, total = call(
        functools.partial(pack_kernel, tiles, band),
        out_shape=[
            jax.ShapeDtypeStruct((tiles, band + 2, 2 * TILE, 2 * TILE), jnp.bfloat16),
            f32(tiles, 2 * TILE, columns),
        ],
        in_specs=[spec(pltpu.HBM)] * 2 + [spec(VMEM)] * 2,
        out_specs=[spec(VMEM)] * 2,
        scratch_shapes=[
            pltpu.SMEM(band_shift.shape, jnp.int32),
            VMEM(operator.shape[1:], jnp.float32),
            held(False),
            held(False),
            pltpu.SemaphoreType.DMA((tiles + 1,)),
        ],
        compiler_params=params(),
        cost_estimate=cost(2 * 40 * 256**3, 2 * operator.size * 4),
    )(in_hbm(band_shift), in_hbm(operator), first, first_near)
    field = []
    for q in range(STREAMS):
        field += outer(0, total, [first_fars[q]], shapes=[half], stream=q)
    fields = [field]
    first_base = outer(0, total, first_fars, shapes=[half] * STREAMS, late=True)
    arrived = cross(0, fields[0])

    second, *_ = lax.optimization_barrier((second, *fields[0]))
    near, far = halo(second, next_door)
    own_scale, near_scale, far_scale = call(
        functools.partial(scale_kernel, tiles),
        out_shape=[square] * 3,
        in_specs=[spec(VMEM)] * 3,
        out_specs=[spec(VMEM)] * 3,
        compiler_params=params(),
        cost_estimate=cost(10**6, 4 * rows * columns * 4),
    )(first, first_near, first_fars[0])
    total = inner(None, [second], [near])
    second_base = outer(None, total, [far], shapes=[half] * STREAMS)

    middle = sections // 2
    for step in range(1, sections):
        bases = first_base if step < middle else second_base
        halos = [halo(part, next_door) for part in arrived]
        nears, fars = zip(*halos)
        if step == sections - 1:
            total = inner(step, arrived, nears, own_scale, near_scale)
            kept = keep(range(middle - 1)) if middle > 1 else ()
            kept = keep(range(middle - 1, step), kept)
            return tuple(outer(step, total, fars, far_scale, *bases, shapes=result, kept=kept))
        field = []
        for q in range(STREAMS):
            total = inner(step, [arrived[q]], [nears[q]], own_scale, near_scale)
            field += outer(step, total, [fars[q]], far_scale, bases[q], shapes=[half], stream=q)
        fields.append(field)
        arrived = cross(step, field)


def solution(mesh):
    return jax.shard_map(
        functools.partial(shards, mesh.shape["depth"], mesh.shape["lat"]),
        mesh=mesh,
        in_specs=(
            P("depth", "lat", None, None, None),
            P("depth", "lat"),
            P("depth", "lat"),
            P("depth", "lat", None),
            P("depth", "lat", None),
            P("lat", None),
            P(),
        ),
        out_specs=(P("depth", "lat", None), P("depth", "lat", None)),
        check_vma=False,
    )
```

```python
import functools

import jax
import jax.numpy as jnp
from jax import lax
from jax.experimental import pallas as pl
from jax.experimental.pallas import tpu as pltpu
from jax.sharding import PartitionSpec as P


TILE = 128
HALF = TILE // 2
VMEM = pltpu.VMEM
LIMIT = 16 * 2**20
STREAMS = 2
CHUNKS = (3, 2)


def spec(space):
    return pl.BlockSpec(memory_space=space)


def f32(*shape):
    return jax.ShapeDtypeStruct(shape, jnp.float32)


def call(kernel, **kwargs):
    return pl.pallas_call(kernel, **kwargs)


def params(limit=LIMIT):
    return pltpu.CompilerParams(vmem_limit_bytes=limit)


def cost(flops, read):
    return pl.CostEstimate(flops=flops, bytes_accessed=read, transcendentals=0)


def in_hbm(x):
    return pltpu.with_memory_space_constraint(x, pltpu.HBM)


def rows_of(t):
    return slice(t * TILE, (t + 1) * TILE)


def down_column(row):
    return jnp.transpose(jnp.broadcast_to(row, (TILE, TILE)))


def split(value):
    high = value.astype(jnp.bfloat16)
    low = (value - high.astype(jnp.float32)).astype(jnp.bfloat16)
    return high, low


def prep_kernel(tiles, shots, sections, assign_at, refl_at, up_at, down_at, src_at, first, second, assign, refl, up, down, src, sems):
    depth = lax.axis_index("depth")
    loads = [
        pltpu.make_async_copy(assign_at, assign, sems.at[0]),
        pltpu.make_async_copy(refl_at, refl, sems.at[1]),
        pltpu.make_async_copy(up_at, up, sems.at[2]),
        pltpu.make_async_copy(down_at, down, sems.at[3]),
        pltpu.make_async_copy(src_at, src, sems.at[4]),
    ]
    for load in loads:
        load.start()
    for load in loads:
        load.wait()
    descends = depth < sections // 2

    def write(of_up, of_down):
        for j in range(tiles):
            row = refl[0:1, rows_of(j)]
            r = down_column(row)
            of_up[rows_of(j)] = -(r * up[0, rows_of(j)])
            of_down[rows_of(j)] = r * down[0, rows_of(j)]
            first[tiles * TILE + j : tiles * TILE + j + 1] = row

    @pl.when(descends)
    def _():
        write(first, second)

    @pl.when(jnp.logical_not(descends))
    def _():
        write(second, first)

    @pl.when(depth == 0)
    def _():
        lane = lax.broadcasted_iota(jnp.int32, (8, TILE), 1)
        wanted = jnp.zeros((8, TILE), jnp.int32)
        for b in range(TILE // (2 * shots)):
            for i in range(shots):
                shot = assign[b * shots + i]
                at = b * 2 * shots + i
                wanted = jnp.where(lane == at, shot, wanted)
                wanted = jnp.where(lane == at + shots, shot + TILE // 2, wanted)
        source = lax.broadcasted_iota(jnp.int32, (TILE, TILE), 0)
        pick = (source == jnp.broadcast_to(wanted[0:1], (TILE, TILE))).astype(jnp.float32).astype(jnp.bfloat16)
        for j in range(tiles):
            x = src[rows_of(j)]
            high = x.astype(jnp.bfloat16)
            mid, low = split(x - high.astype(jnp.float32))
            entering = jnp.dot(low, pick, preferred_element_type=jnp.float32)
            entering += jnp.dot(mid, pick, preferred_element_type=jnp.float32)
            entering += jnp.dot(high, pick, preferred_element_type=jnp.float32)
            r = down_column(refl[0:1, rows_of(j)])
            first[rows_of(j)] = (1.0 + r) * entering + first[rows_of(j)]


def pack_kernel(tiles, band, shift_at, tiles_at, out, shift, held, sems):
    loads = [pltpu.make_async_copy(shift_at, shift, sems.at[tiles])]
    loads += [pltpu.make_async_copy(tiles_at.at[0, j], held.at[j], sems.at[j]) for j in range(tiles)]
    for load in loads:
        load.start()
    loads[0].wait()
    for j in range(tiles):
        loads[1 + j].wait()
        move = shift[0, j]
        for k in range(band):
            high, low = split(held[j, k])
            slot = k + 1 + move
            out[j, slot, :, :TILE] = high
            out[j, slot, :, TILE:] = low
        zero = jnp.zeros(out.shape[2:], jnp.bfloat16)
        out[j, jnp.where(move >= 0, 0, band)] = zero
        out[j, jnp.where(move <= 0, band + 1, 1)] = zero


def doubled(tile):
    high, low = split(tile)
    line = jnp.concatenate([high, low], axis=1)
    return jnp.concatenate([line, line], axis=0)


def folded(value):
    return value[:, :TILE] + value[:, TILE:]


def lanes(rows):
    return lax.broadcasted_iota(jnp.int32, (rows, TILE), 1)


def turned(value):
    return pltpu.roll(value, HALF, 1)


def left_half(rows):
    return lanes(rows) < HALF


def halves_of(t):
    return slice(t * HALF, (t + 1) * HALF)


def part_tile(part, t):
    for chunk in part:
        count = chunk.shape[0] // HALF
        if t < count:
            return chunk[halves_of(t)]
        t -= count


def unpack_tile(part, t):
    tile = part_tile(part, t)
    return jnp.concatenate([tile, turned(tile)], axis=0)


def grouped(refs, layout):
    out = []
    for count in layout:
        out.append(refs[:count])
        refs = refs[count:]
    return out, refs


def stream_line(tile):
    rest = tile - tile.astype(jnp.bfloat16).astype(jnp.float32)
    line = jnp.where(left_half(TILE), tile, turned(rest)).astype(jnp.bfloat16)
    return jnp.concatenate([line, line], axis=0)


def merged(first, second):
    left = left_half(HALF)
    upper = jnp.where(left, first, turned(second))
    lower = jnp.where(left, turned(first), second)
    return jnp.concatenate([upper, lower], axis=0)


def parted(value):
    upper, lower = value[:HALF], value[HALF:]
    left = left_half(HALF)
    return jnp.where(left, upper, turned(lower)), jnp.where(left, turned(upper), lower)


def full_tile(field, t):
    if len(field) == 1:
        return field[0][0][rows_of(t)]
    return merged(*[part_tile(part, t) for part in field])


def spread(field, scale, sign, tiles, narrow, mirrored, held):
    for t in range(tiles):
        tile = unpack_tile(field[0], t) if narrow else full_tile(field, t)
        if scale is not None:
            tile = tile * (1.0 + sign * scale[t])
        at = 2 * t * TILE
        if mirrored is not None:
            at = pl.multiple_of(jnp.where(mirrored, 2 * (tiles - 1 - t) * TILE, at), 2 * TILE)
        held[pl.ds(at, 2 * TILE)] = stream_line(tile) if narrow else doubled(tile)


def product(packed, held, j, slots, narrow):
    value = jnp.dot(
        jnp.concatenate([packed[j, slot] for slot in slots], axis=1),
        held[: 2 * len(slots) * TILE],
        preferred_element_type=jnp.float32,
    )
    return value if narrow else folded(value)


def side_product(packed, held, tiles, jj, low_side, narrow):
    j = jnp.where(low_side, tiles - 1 - jj, jj)
    slots = [jnp.where(low_side, jj - t, 2 * tiles + t - jj) for t in range(jj + 1)]
    return j, product(packed, held, j, slots, narrow)


def when_active(step, sections, body):
    depth = lax.axis_index("depth")
    if step is None:
        body()
    else:
        pl.when((depth == step) | (depth == sections - 1 - step))(body)


def combined(value, shots):
    by_imag = value[TILE:]
    ahead = pltpu.roll(by_imag, TILE - shots, 1)
    behind = pltpu.roll(by_imag, shots, 1)
    return value[:TILE] + jnp.where(lax.rem(lanes(TILE), 2 * shots) < shots, -ahead, behind)


def scale_kernel(tiles, *refs):
    for source, out in zip(refs[:3], refs[3:]):
        for t in range(tiles):
            at = tiles * TILE + t
            out[t] = down_column(source[at : at + 1])


def mark_kernel(out):
    out[...] = jnp.zeros_like(out)


def inner_kernel(step, sections, tiles, layout, packed, *refs):
    narrow = bool(step) and len(layout) == 1
    own, refs = grouped(refs, layout)
    near, refs = grouped(refs, layout)
    scale, near_scale = refs[:2] if step else (None, None)
    total, held_own, held_near = refs[-3:]

    def body():
        sign = jnp.where(lax.axis_index("depth") == (step or 0), 1.0, -1.0)
        low_side = lax.rem(lax.axis_index("lat"), 2) == 1
        spread(own, scale, sign, tiles, narrow, None, held_own)
        spread(near, near_scale, sign, tiles, narrow, low_side, held_near)
        for j in range(tiles):
            total[j] = product(packed, held_own, j, range(tiles - j, 2 * tiles - j), narrow)
        for jj in range(tiles):
            j, value = side_product(packed, held_near, tiles, jj, low_side, narrow)
            total[j] = total[j] + value

    when_active(step or None, sections, body)


def outer_kernel(step, sections, lats, tiles, shots, layout, ends, late, packed, total, *refs):
    narrow = bool(step) and not ends
    parts = len(layout)
    far, refs = grouped(refs, layout)
    scale, base = None, None
    if step:
        scale, base, refs = refs[0], refs[1 : 1 + parts], refs[1 + parts :]
    if ends:
        _, _, result_down, result_up, held, leaving, sems = refs
    else:
        outs, held = refs[:-1], refs[-1]
    lat = lax.axis_index("lat")
    depth = lax.axis_index("depth")
    low_side = lax.rem(lat, 2) == 0
    has_far = (lat > 0) & (lat < lats - 1)

    def body():
        sign = jnp.where(depth == (step or 0), 1.0, -1.0)

        def copy_of(j, result):
            at = pl.ds(pl.multiple_of(j * TILE, TILE), TILE)
            return pltpu.make_async_copy(leaving.at[at], result.at[0, at], sems.at[j])

        def store(j, value):
            first = 0
            for out in outs:
                count = out.shape[0] // HALF

                def put(out=out, first=first):
                    out[pl.ds(pl.multiple_of((j - first) * HALF, HALF), HALF)] = value

                if len(outs) == 1:
                    put()
                else:
                    pl.when((j >= first) & (j < first + count))(put)
                first += count

        def finish(j, value):
            at = pl.ds(pl.multiple_of(j * HALF, HALF), HALF)
            if narrow:
                value = combined(value + turned(value), shots)
                store(j, jnp.where(left_half(HALF), value[:HALF], value[HALF:]) + base[0][at])
                return
            value = combined(value, shots)
            if ends:
                value = value + merged(*[part[at] for part in base])
                leaving[pl.ds(pl.multiple_of(j * TILE, TILE), TILE)] = value
                pl.when(depth == step)(lambda: copy_of(j, result_down).start())
                pl.when(depth != step)(lambda: copy_of(j, result_up).start())
                return
            for out, part in zip(outs, parted(value)):
                out[at] = part

        @pl.when(has_far)
        def _():
            spread(far, scale, sign, tiles, narrow, low_side, held)
            for jj in range(tiles):
                j, value = side_product(packed, held, tiles, jj, low_side, narrow)
                finish(j, total[j] + value)

        @pl.when(jnp.logical_not(has_far))
        def _():
            for j in range(tiles):
                finish(j, total[j])

        if ends:

            def wait_all(result):
                for j in range(tiles):
                    copy_of(j, result).wait()

            pl.when(depth == step)(lambda: wait_all(result_down))
            pl.when(depth != step)(lambda: wait_all(result_up))

    if late:
        pl.when((depth > 0) & (depth < sections - 1))(body)
    else:
        when_active(step, sections, body)


def keep_kernel(sections, tiles, steps, layout, *refs):
    result_down, result_up, whole, sems = refs[-4:]
    fields, _ = grouped(refs, layout)
    depth = lax.axis_index("depth")

    def put(first, second, result):
        for j in range(tiles):
            whole[rows_of(j)] = merged(part_tile(first, j), part_tile(second, j))
        copy = pltpu.make_async_copy(whole, result.at[0], sems)
        copy.start()
        copy.wait()

    for i, step in enumerate(steps):
        first, second = fields[2 * i : 2 * i + 2]
        pl.when(depth == step)(functools.partial(put, first, second, result_down))
        pl.when(depth == sections - 1 - step)(functools.partial(put, first, second, result_up))


def shards(sections, lats, operator, band_shift, reflectivity, up_stored, down_stored, sources, assignment):
    tiles, band = operator.shape[1], operator.shape[2]
    _, columns = sources.shape
    shots = columns // 4
    rows = tiles * TILE
    if sections % 2 or lats % 2 or tiles != band // 2 + 1 or columns != TILE or tiles != sum(CHUNKS):
        raise ValueError("unsupported sizes")

    def move(x, partner):
        pairs = []
        for d in range(sections):
            for l in range(lats):
                e, m = partner(d, l)
                pairs.append((d * lats + l, e * lats + m))
        return lax.ppermute(x, ("depth", "lat"), pairs)

    def near_of(d, l):
        return d, l ^ 1

    def far_of(spare, d, l):
        m = l + 1 if l % 2 else l - 1
        return (d, m) if 0 <= m < lats else (spare(d), l)

    def across(step, d, l):
        for low in (step, sections - 2 - step):
            if d == low:
                return low + 1, l
            if d == low + 1:
                return low, l
        return near_of(d, l)

    def halo(field, spare):
        near = move(field, near_of)
        return near, move(field, functools.partial(far_of, spare))

    def next_door(d):
        return (d + sections // 2) % sections

    first, second = call(
        functools.partial(prep_kernel, tiles, shots, sections),
        out_shape=[f32(rows + 8, columns), f32(rows, columns)],
        in_specs=[spec(pltpu.HBM)] * 5,
        out_specs=[spec(VMEM)] * 2,
        scratch_shapes=[
            pltpu.SMEM(assignment.shape, jnp.int32),
            VMEM(reflectivity.shape, jnp.float32),
            VMEM(up_stored.shape, jnp.float32),
            VMEM(down_stored.shape, jnp.float32),
            VMEM(sources.shape, jnp.float32),
            pltpu.SemaphoreType.DMA((5,)),
        ],
        compiler_params=params(),
        cost_estimate=cost(10**7, 5 * rows * columns * 4),
    )(*map(in_hbm, (assignment, reflectivity, up_stored, down_stored, sources)))

    packed = call(
        functools.partial(pack_kernel, tiles, band),
        out_shape=jax.ShapeDtypeStruct((tiles, band + 2, 2 * TILE, 2 * TILE), jnp.bfloat16),
        in_specs=[spec(pltpu.HBM)] * 2,
        out_specs=spec(VMEM),
        scratch_shapes=[
            pltpu.SMEM(band_shift.shape, jnp.int32),
            VMEM(operator.shape[1:], jnp.float32),
            pltpu.SemaphoreType.DMA((tiles + 1,)),
        ],
        compiler_params=params(),
        cost_estimate=cost(10**7, 2 * operator.size * 4),
    )(in_hbm(band_shift), in_hbm(operator))

    square = f32(tiles, TILE, columns)
    half = f32(rows // STREAMS, columns)
    result = [f32(1, rows, columns)] * 2

    def held(narrow):
        return VMEM((tiles * 2 * TILE, TILE if narrow else 2 * TILE), jnp.bfloat16)

    def inner(step, own, near, *scales):
        args = [packed, *flat(own), *flat(near), *scales]
        return call(
            functools.partial(inner_kernel, step, sections, tiles, [len(part) for part in own]),
            out_shape=f32(tiles, 2 * TILE, columns),
            in_specs=[spec(VMEM)] * len(args),
            out_specs=spec(VMEM),
            scratch_shapes=[held(step and len(own) == 1)] * 2,
            compiler_params=params(),
            cost_estimate=cost(2 * 40 * 256**3, 8 * 2**20),
        )(*args)

    def outer(step, total, far, *more, shapes, kept=(), late=False):
        ends = bool(kept)
        args = [packed, total, *flat(far), *more]
        count = len(args)
        scratch = [held(step and not ends)]
        if ends:
            scratch += [VMEM((rows, columns), jnp.float32), pltpu.SemaphoreType.DMA((tiles,))]
        return call(
            functools.partial(
                outer_kernel, step, sections, lats, tiles, shots, [len(part) for part in far], ends, late
            ),
            out_shape=shapes,
            in_specs=[spec(VMEM)] * count + [spec(pl.ANY)] * len(kept),
            out_specs=[spec(pl.ANY if ends else VMEM)] * len(shapes),
            scratch_shapes=scratch,
            input_output_aliases={count: 0, count + 1: 1} if ends else {},
            compiler_params=params(),
            cost_estimate=cost(2 * 15 * 256**3, 4 * 2**20),
        )(*args, *kept)

    def keep(steps, kept=()):
        parts = [part for step in steps for part in fields[step]]
        args = flat(parts)
        count = len(args)
        return call(
            functools.partial(keep_kernel, sections, tiles, steps, [len(part) for part in parts]),
            out_shape=result,
            in_specs=[spec(VMEM)] * count + [spec(pl.ANY)] * len(kept),
            out_specs=[spec(pl.ANY)] * 2,
            scratch_shapes=[VMEM((rows, columns), jnp.float32), pltpu.SemaphoreType.DMA(())],
            input_output_aliases={count: 0, count + 1: 1} if kept else {},
            compiler_params=params(),
            cost_estimate=cost(0, 4 * rows * columns * 4),
        )(*args, *kept)

    def flat(parts):
        return [chunk for part in parts for chunk in part]

    def cross(step, field):
        def one(chunk):
            return move(chunk, functools.partial(across, step))

        return [[one(chunk) for chunk in part] for part in field]

    first_near, first_far = halo(first, next_door)
    total = inner(0, [[first]], [[first_near]])
    field = outer(0, total, [[first_far]], shapes=[half] * STREAMS)
    fields = [[[part] for part in field]]
    first_base = outer(0, total, [[first_far]], shapes=[half] * STREAMS, late=True)
    arrived = cross(0, fields[0])

    second, *_ = lax.optimization_barrier((second, *field))
    near, far = halo(second, next_door)
    own_scale, near_scale, far_scale = call(
        functools.partial(scale_kernel, tiles),
        out_shape=[square] * 3,
        in_specs=[spec(VMEM)] * 3,
        out_specs=[spec(VMEM)] * 3,
        compiler_params=params(),
        cost_estimate=cost(10**6, 4 * rows * columns * 4),
    )(first, first_near, first_far)
    total = inner(None, [[second]], [[near]])
    second_base = outer(None, total, [[far]], shapes=[half] * STREAMS)

    middle = sections // 2
    for step in range(1, sections):
        bases = first_base if step < middle else second_base
        nears, fars = [], []
        for part in arrived:
            halos = [halo(chunk, next_door) for chunk in part]
            nears.append([near for near, _ in halos])
            fars.append([far for _, far in halos])
        if step == sections - 1:
            mark = call(
                mark_kernel,
                out_shape=f32(8, columns),
                in_specs=[],
                out_specs=spec(VMEM),
                compiler_params=params(),
                cost_estimate=cost(0, 1),
            )()
            total = inner(step, arrived, nears, own_scale, near_scale, mark)
            kept = keep(range(middle - 1)) if middle > 1 else ()
            kept = keep(range(middle - 1, step), kept)
            return tuple(outer(step, total, fars, far_scale, *bases, shapes=result, kept=kept))
        field = []
        for q in range(STREAMS):
            total = inner(step, [arrived[q]], [nears[q]], own_scale, near_scale)
            shapes = [half]
            if step == sections - 2 and q == STREAMS - 1:
                shapes = [f32(count * HALF, columns) for count in CHUNKS]
            field.append(outer(step, total, [fars[q]], far_scale, bases[q], shapes=shapes))
        fields.append(field)
        arrived = cross(step, field)


def solution(mesh):
    return jax.shard_map(
        functools.partial(shards, mesh.shape["depth"], mesh.shape["lat"]),
        mesh=mesh,
        in_specs=(
            P("depth", "lat", None, None, None),
            P("depth", "lat"),
            P("depth", "lat"),
            P("depth", "lat", None),
            P("depth", "lat", None),
            P("lat", None),
            P(),
        ),
        out_specs=(P("depth", "lat", None), P("depth", "lat", None)),
        check_vma=False,
    )
```

```python
import functools

import jax
import jax.numpy as jnp
from jax import lax
from jax.experimental import pallas as pl
from jax.experimental.pallas import tpu as pltpu
from jax.sharding import PartitionSpec as P


TILE = 128
HALF = TILE // 2
VMEM = pltpu.VMEM
LIMIT = 16 * 2**20
STREAMS = 2
CHUNKS = (3, 2)


def spec(space):
    return pl.BlockSpec(memory_space=space)


def f32(*shape):
    return jax.ShapeDtypeStruct(shape, jnp.float32)


def call(kernel, **kwargs):
    return pl.pallas_call(kernel, **kwargs)


def params(limit=LIMIT):
    return pltpu.CompilerParams(vmem_limit_bytes=limit)


def cost(flops, read):
    return pl.CostEstimate(flops=flops, bytes_accessed=read, transcendentals=0)


def in_hbm(x):
    return pltpu.with_memory_space_constraint(x, pltpu.HBM)


def rows_of(t):
    return slice(t * TILE, (t + 1) * TILE)


def down_column(row):
    return jnp.transpose(jnp.broadcast_to(row, (TILE, TILE)))


def split(value):
    high = value.astype(jnp.bfloat16)
    low = (value - high.astype(jnp.float32)).astype(jnp.bfloat16)
    return high, low


def prep_kernel(tiles, shots, sections, assign_at, refl_at, up_at, down_at, src_at, first, second, assign, refl, up, down, src, sems):
    depth = lax.axis_index("depth")
    loads = [
        pltpu.make_async_copy(assign_at, assign, sems.at[0]),
        pltpu.make_async_copy(refl_at, refl, sems.at[1]),
        pltpu.make_async_copy(up_at, up, sems.at[2]),
        pltpu.make_async_copy(down_at, down, sems.at[3]),
        pltpu.make_async_copy(src_at, src, sems.at[4]),
    ]
    for load in loads:
        load.start()
    for load in loads:
        load.wait()
    descends = depth < sections // 2

    def write(of_up, of_down):
        for j in range(tiles):
            row = refl[0:1, rows_of(j)]
            r = down_column(row)
            of_up[rows_of(j)] = -(r * up[0, rows_of(j)])
            of_down[rows_of(j)] = r * down[0, rows_of(j)]
            first[tiles * TILE + j : tiles * TILE + j + 1] = row

    @pl.when(descends)
    def _():
        write(first, second)

    @pl.when(jnp.logical_not(descends))
    def _():
        write(second, first)

    @pl.when(depth == 0)
    def _():
        lane = lax.broadcasted_iota(jnp.int32, (8, TILE), 1)
        wanted = jnp.zeros((8, TILE), jnp.int32)
        for b in range(TILE // (2 * shots)):
            for i in range(shots):
                shot = assign[b * shots + i]
                at = b * 2 * shots + i
                wanted = jnp.where(lane == at, shot, wanted)
                wanted = jnp.where(lane == at + shots, shot + TILE // 2, wanted)
        source = lax.broadcasted_iota(jnp.int32, (TILE, TILE), 0)
        pick = (source == jnp.broadcast_to(wanted[0:1], (TILE, TILE))).astype(jnp.float32).astype(jnp.bfloat16)
        for j in range(tiles):
            x = src[rows_of(j)]
            high = x.astype(jnp.bfloat16)
            mid, low = split(x - high.astype(jnp.float32))
            entering = jnp.dot(low, pick, preferred_element_type=jnp.float32)
            entering += jnp.dot(mid, pick, preferred_element_type=jnp.float32)
            entering += jnp.dot(high, pick, preferred_element_type=jnp.float32)
            r = down_column(refl[0:1, rows_of(j)])
            first[rows_of(j)] = (1.0 + r) * entering + first[rows_of(j)]


def pack_kernel(tiles, band, shift_at, tiles_at, out, shift, held, sems):
    loads = [pltpu.make_async_copy(shift_at, shift, sems.at[tiles])]
    loads += [pltpu.make_async_copy(tiles_at.at[0, j], held.at[j], sems.at[j]) for j in range(tiles)]
    for load in loads:
        load.start()
    loads[0].wait()
    for j in range(tiles):
        loads[1 + j].wait()
        move = shift[0, j]
        for k in range(band):
            high, low = split(held[j, k])
            slot = k + 1 + move
            out[j, slot, :, :TILE] = high
            out[j, slot, :, TILE:] = low
        zero = jnp.zeros(out.shape[2:], jnp.bfloat16)
        out[j, jnp.where(move >= 0, 0, band)] = zero
        out[j, jnp.where(move <= 0, band + 1, 1)] = zero


def doubled(tile):
    high, low = split(tile)
    line = jnp.concatenate([high, low], axis=1)
    return jnp.concatenate([line, line], axis=0)


def folded(value):
    return value[:, :TILE] + value[:, TILE:]


def lanes(rows):
    return lax.broadcasted_iota(jnp.int32, (rows, TILE), 1)


def turned(value):
    return pltpu.roll(value, HALF, 1)


def left_half(rows):
    return lanes(rows) < HALF


def halves_of(t):
    return slice(t * HALF, (t + 1) * HALF)


def part_tile(part, t):
    for chunk in part:
        count = chunk.shape[0] // HALF
        if t < count:
            return chunk[halves_of(t)]
        t -= count


def unpack_tile(part, t):
    tile = part_tile(part, t)
    return jnp.concatenate([tile, turned(tile)], axis=0)


def grouped(refs, layout):
    out = []
    for count in layout:
        out.append(refs[:count])
        refs = refs[count:]
    return out, refs


def stream_line(tile):
    rest = tile - tile.astype(jnp.bfloat16).astype(jnp.float32)
    line = jnp.where(left_half(TILE), tile, turned(rest)).astype(jnp.bfloat16)
    return jnp.concatenate([line, line], axis=0)


def merged(first, second):
    left = left_half(HALF)
    upper = jnp.where(left, first, turned(second))
    lower = jnp.where(left, turned(first), second)
    return jnp.concatenate([upper, lower], axis=0)


def parted(value):
    upper, lower = value[:HALF], value[HALF:]
    left = left_half(HALF)
    return jnp.where(left, upper, turned(lower)), jnp.where(left, turned(upper), lower)


def full_tile(field, t):
    if len(field) == 1:
        return field[0][0][rows_of(t)]
    return merged(*[part_tile(part, t) for part in field])


def aligned(j, size):
    return j * size if isinstance(j, int) else pl.multiple_of(j * size, size)


def choose(condition, this, that):
    if isinstance(condition, bool):
        return this if condition else that
    return jnp.where(condition, this, that)


def spread(field, scale, sign, tiles, narrow, mirrored, held):
    for t in range(tiles):
        tile = unpack_tile(field[0], t) if narrow else full_tile(field, t)
        if scale is not None:
            tile = tile * (1.0 + sign * scale[t])
        at = 2 * t * TILE
        if mirrored is not None:
            at = choose(mirrored, 2 * (tiles - 1 - t) * TILE, at)
            at = at if isinstance(at, int) else pl.multiple_of(at, 2 * TILE)
        held[pl.ds(at, 2 * TILE)] = stream_line(tile) if narrow else doubled(tile)


def product(packed, held, j, slots, narrow):
    value = jnp.dot(
        jnp.concatenate([packed[j, slot] for slot in slots], axis=1),
        held[: 2 * len(slots) * TILE],
        preferred_element_type=jnp.float32,
    )
    return value if narrow else folded(value)


def side_product(packed, held, tiles, jj, low_side, narrow):
    j = choose(low_side, tiles - 1 - jj, jj)
    slots = [choose(low_side, jj - t, 2 * tiles + t - jj) for t in range(jj + 1)]
    return j, product(packed, held, j, slots, narrow)


def when_active(step, sections, body):
    depth = lax.axis_index("depth")
    if step is None:
        body()
    else:
        pl.when((depth == step) | (depth == sections - 1 - step))(body)


def combined(value, shots):
    by_imag = value[TILE:]
    ahead = pltpu.roll(by_imag, TILE - shots, 1)
    behind = pltpu.roll(by_imag, shots, 1)
    return value[:TILE] + jnp.where(lax.rem(lanes(TILE), 2 * shots) < shots, -ahead, behind)


def scale_kernel(tiles, *refs):
    for source, out in zip(refs[:3], refs[3:]):
        for t in range(tiles):
            at = tiles * TILE + t
            out[t] = down_column(source[at : at + 1])


def mark_kernel(out):
    out[...] = jnp.zeros_like(out)


def inner_kernel(step, sections, tiles, layout, packed, *refs):
    narrow = bool(step) and len(layout) == 1
    own, refs = grouped(refs, layout)
    near, refs = grouped(refs, layout)
    scale, near_scale = refs[:2] if step else (None, None)
    total, held_own, held_near = refs[-3:]

    def body():
        sign = jnp.where(lax.axis_index("depth") == (step or 0), 1.0, -1.0)
        low_side = lax.rem(lax.axis_index("lat"), 2) == 1
        spread(own, scale, sign, tiles, narrow, None, held_own)
        spread(near, near_scale, sign, tiles, narrow, low_side, held_near)
        for j in range(tiles):
            total[j] = product(packed, held_own, j, range(tiles - j, 2 * tiles - j), narrow)
        for jj in range(tiles):
            j, value = side_product(packed, held_near, tiles, jj, low_side, narrow)
            total[j] = total[j] + value

    when_active(step or None, sections, body)


def outer_kernel(step, sections, lats, tiles, shots, layout, ends, late, packed, total, *refs):
    narrow = bool(step) and not ends
    parts = len(layout)
    far, refs = grouped(refs, layout)
    scale, base = None, None
    if step:
        scale, base, refs = refs[0], refs[1 : 1 + parts], refs[1 + parts :]
    if ends:
        _, _, result_down, result_up, held, leaving, sems = refs
    else:
        outs, held = refs[:-1], refs[-1]
    lat = lax.axis_index("lat")
    depth = lax.axis_index("depth")
    low_side = lax.rem(lat, 2) == 0
    has_far = (lat > 0) & (lat < lats - 1)

    def body():
        sign = jnp.where(depth == (step or 0), 1.0, -1.0)

        def copy_of(j, result):
            at = pl.ds(pl.multiple_of(j * TILE, TILE), TILE)
            return pltpu.make_async_copy(leaving.at[at], result.at[0, at], sems.at[j])

        def store(j, value):
            if len(outs) == 1:
                outs[0][pl.ds(aligned(j, HALF), HALF)] = value
                return
            for out in outs:
                count = out.shape[0] // HALF
                if 0 <= j < count:
                    out[halves_of(j)] = value
                j -= count

        def finish(j, value):
            at = pl.ds(aligned(j, HALF), HALF)
            if narrow:
                value = combined(value + turned(value), shots)
                store(j, jnp.where(left_half(HALF), value[:HALF], value[HALF:]) + base[0][at])
                return
            value = combined(value, shots)
            if ends:
                value = value + merged(*[part[at] for part in base])
                leaving[pl.ds(pl.multiple_of(j * TILE, TILE), TILE)] = value
                pl.when(depth == step)(lambda: copy_of(j, result_down).start())
                pl.when(depth != step)(lambda: copy_of(j, result_up).start())
                return
            for out, part in zip(outs, parted(value)):
                out[at] = part

        def with_far(low):
            spread(far, scale, sign, tiles, narrow, low, held)
            for jj in range(tiles):
                j, value = side_product(packed, held, tiles, jj, low, narrow)
                finish(j, total[j] + value)

        if narrow and len(outs) > 1:
            pl.when(has_far & low_side)(lambda: with_far(True))
            pl.when(has_far & jnp.logical_not(low_side))(lambda: with_far(False))
        else:
            pl.when(has_far)(lambda: with_far(low_side))

        @pl.when(jnp.logical_not(has_far))
        def _():
            for j in range(tiles):
                finish(j, total[j])

        if ends:

            def wait_all(result):
                for j in range(tiles):
                    copy_of(j, result).wait()

            pl.when(depth == step)(lambda: wait_all(result_down))
            pl.when(depth != step)(lambda: wait_all(result_up))

    if late:
        pl.when((depth > 0) & (depth < sections - 1))(body)
    else:
        when_active(step, sections, body)


def keep_kernel(sections, tiles, steps, layout, *refs):
    result_down, result_up, whole, sems = refs[-4:]
    fields, _ = grouped(refs, layout)
    depth = lax.axis_index("depth")

    def put(first, second, result):
        for j in range(tiles):
            whole[rows_of(j)] = merged(part_tile(first, j), part_tile(second, j))
        copy = pltpu.make_async_copy(whole, result.at[0], sems)
        copy.start()
        copy.wait()

    for i, step in enumerate(steps):
        first, second = fields[2 * i : 2 * i + 2]
        pl.when(depth == step)(functools.partial(put, first, second, result_down))
        pl.when(depth == sections - 1 - step)(functools.partial(put, first, second, result_up))


def shards(sections, lats, operator, band_shift, reflectivity, up_stored, down_stored, sources, assignment):
    tiles, band = operator.shape[1], operator.shape[2]
    _, columns = sources.shape
    shots = columns // 4
    rows = tiles * TILE
    if sections % 2 or lats % 2 or tiles != band // 2 + 1 or columns != TILE or tiles != sum(CHUNKS):
        raise ValueError("unsupported sizes")

    def move(x, partner):
        pairs = []
        for d in range(sections):
            for l in range(lats):
                e, m = partner(d, l)
                pairs.append((d * lats + l, e * lats + m))
        return lax.ppermute(x, ("depth", "lat"), pairs)

    def near_of(d, l):
        return d, l ^ 1

    def far_of(spare, d, l):
        m = l + 1 if l % 2 else l - 1
        return (d, m) if 0 <= m < lats else (spare(d), l)

    def across(step, d, l):
        for low in (step, sections - 2 - step):
            if d == low:
                return low + 1, l
            if d == low + 1:
                return low, l
        return near_of(d, l)

    def halo(field, spare):
        near = move(field, near_of)
        return near, move(field, functools.partial(far_of, spare))

    def next_door(d):
        return (d + sections // 2) % sections

    first, second = call(
        functools.partial(prep_kernel, tiles, shots, sections),
        out_shape=[f32(rows + 8, columns), f32(rows, columns)],
        in_specs=[spec(pltpu.HBM)] * 5,
        out_specs=[spec(VMEM)] * 2,
        scratch_shapes=[
            pltpu.SMEM(assignment.shape, jnp.int32),
            VMEM(reflectivity.shape, jnp.float32),
            VMEM(up_stored.shape, jnp.float32),
            VMEM(down_stored.shape, jnp.float32),
            VMEM(sources.shape, jnp.float32),
            pltpu.SemaphoreType.DMA((5,)),
        ],
        compiler_params=params(),
        cost_estimate=cost(10**7, 5 * rows * columns * 4),
    )(*map(in_hbm, (assignment, reflectivity, up_stored, down_stored, sources)))

    packed = call(
        functools.partial(pack_kernel, tiles, band),
        out_shape=jax.ShapeDtypeStruct((tiles, band + 2, 2 * TILE, 2 * TILE), jnp.bfloat16),
        in_specs=[spec(pltpu.HBM)] * 2,
        out_specs=spec(VMEM),
        scratch_shapes=[
            pltpu.SMEM(band_shift.shape, jnp.int32),
            VMEM(operator.shape[1:], jnp.float32),
            pltpu.SemaphoreType.DMA((tiles + 1,)),
        ],
        compiler_params=params(),
        cost_estimate=cost(10**7, 2 * operator.size * 4),
    )(in_hbm(band_shift), in_hbm(operator))

    square = f32(tiles, TILE, columns)
    half = f32(rows // STREAMS, columns)
    result = [f32(1, rows, columns)] * 2

    def held(narrow):
        return VMEM((tiles * 2 * TILE, TILE if narrow else 2 * TILE), jnp.bfloat16)

    def inner(step, own, near, *scales):
        args = [packed, *flat(own), *flat(near), *scales]
        return call(
            functools.partial(inner_kernel, step, sections, tiles, [len(part) for part in own]),
            out_shape=f32(tiles, 2 * TILE, columns),
            in_specs=[spec(VMEM)] * len(args),
            out_specs=spec(VMEM),
            scratch_shapes=[held(step and len(own) == 1)] * 2,
            compiler_params=params(),
            cost_estimate=cost(2 * 40 * 256**3, 8 * 2**20),
        )(*args)

    def outer(step, total, far, *more, shapes, kept=(), late=False):
        ends = bool(kept)
        args = [packed, total, *flat(far), *more]
        count = len(args)
        scratch = [held(step and not ends)]
        if ends:
            scratch += [VMEM((rows, columns), jnp.float32), pltpu.SemaphoreType.DMA((tiles,))]
        return call(
            functools.partial(
                outer_kernel, step, sections, lats, tiles, shots, [len(part) for part in far], ends, late
            ),
            out_shape=shapes,
            in_specs=[spec(VMEM)] * count + [spec(pl.ANY)] * len(kept),
            out_specs=[spec(pl.ANY if ends else VMEM)] * len(shapes),
            scratch_shapes=scratch,
            input_output_aliases={count: 0, count + 1: 1} if ends else {},
            compiler_params=params(),
            cost_estimate=cost(2 * 15 * 256**3, 4 * 2**20),
        )(*args, *kept)

    def keep(steps, kept=()):
        parts = [part for step in steps for part in fields[step]]
        args = flat(parts)
        count = len(args)
        return call(
            functools.partial(keep_kernel, sections, tiles, steps, [len(part) for part in parts]),
            out_shape=result,
            in_specs=[spec(VMEM)] * count + [spec(pl.ANY)] * len(kept),
            out_specs=[spec(pl.ANY)] * 2,
            scratch_shapes=[VMEM((rows, columns), jnp.float32), pltpu.SemaphoreType.DMA(())],
            input_output_aliases={count: 0, count + 1: 1} if kept else {},
            compiler_params=params(),
            cost_estimate=cost(0, 4 * rows * columns * 4),
        )(*args, *kept)

    def flat(parts):
        return [chunk for part in parts for chunk in part]

    def cross(step, field):
        def one(chunk):
            return move(chunk, functools.partial(across, step))

        return [[one(chunk) for chunk in part] for part in field]

    first_near, first_far = halo(first, next_door)
    total = inner(0, [[first]], [[first_near]])
    field = outer(0, total, [[first_far]], shapes=[half] * STREAMS)
    fields = [[[part] for part in field]]
    first_base = outer(0, total, [[first_far]], shapes=[half] * STREAMS, late=True)
    arrived = cross(0, fields[0])

    second, *_ = lax.optimization_barrier((second, *field))
    near, far = halo(second, next_door)
    own_scale, near_scale, far_scale = call(
        functools.partial(scale_kernel, tiles),
        out_shape=[square] * 3,
        in_specs=[spec(VMEM)] * 3,
        out_specs=[spec(VMEM)] * 3,
        compiler_params=params(),
        cost_estimate=cost(10**6, 4 * rows * columns * 4),
    )(first, first_near, first_far)
    total = inner(None, [[second]], [[near]])
    second_base = outer(None, total, [[far]], shapes=[half] * STREAMS)

    middle = sections // 2
    for step in range(1, sections):
        bases = first_base if step < middle else second_base
        nears, fars = [], []
        for part in arrived:
            halos = [halo(chunk, next_door) for chunk in part]
            nears.append([near for near, _ in halos])
            fars.append([far for _, far in halos])
        if step == sections - 1:
            marks = [
                call(
                    mark_kernel,
                    out_shape=f32(8, columns),
                    in_specs=[],
                    out_specs=spec(VMEM),
                    compiler_params=pltpu.CompilerParams(vmem_limit_bytes=LIMIT, has_side_effects=True),
                    cost_estimate=cost(0, 1),
                )()
                for _ in range(STREAMS)
            ]
            total = inner(step, arrived, nears, own_scale, near_scale, *marks)
            kept = keep(range(middle - 1)) if middle > 1 else ()
            kept = keep(range(middle - 1, step), kept)
            return tuple(outer(step, total, fars, far_scale, *bases, shapes=result, kept=kept))
        field = []
        for q in range(STREAMS):
            total = inner(step, [arrived[q]], [nears[q]], own_scale, near_scale)
            shapes = [half]
            if step == sections - 2 and q == STREAMS - 1:
                shapes = [f32(count * HALF, columns) for count in CHUNKS]
            field.append(outer(step, total, [fars[q]], far_scale, bases[q], shapes=shapes))
        fields.append(field)
        arrived = cross(step, field)


def solution(mesh):
    return jax.shard_map(
        functools.partial(shards, mesh.shape["depth"], mesh.shape["lat"]),
        mesh=mesh,
        in_specs=(
            P("depth", "lat", None, None, None),
            P("depth", "lat"),
            P("depth", "lat"),
            P("depth", "lat", None),
            P("depth", "lat", None),
            P("lat", None),
            P(),
        ),
        out_specs=(P("depth", "lat", None), P("depth", "lat", None)),
        check_vma=False,
    )
```

```python
import functools

import jax
import jax.numpy as jnp
from jax import lax
from jax.experimental import pallas as pl
from jax.experimental.pallas import tpu as pltpu
from jax.sharding import PartitionSpec as P


TILE = 128
HALF = TILE // 2
VMEM = pltpu.VMEM
LIMIT = 16 * 2**20
STREAMS = 2
CHUNKS = (2, 3)


def spec(space):
    return pl.BlockSpec(memory_space=space)


def f32(*shape):
    return jax.ShapeDtypeStruct(shape, jnp.float32)


def call(kernel, **kwargs):
    return pl.pallas_call(kernel, **kwargs)


def params(limit=LIMIT):
    return pltpu.CompilerParams(vmem_limit_bytes=limit)


def cost(flops, read):
    return pl.CostEstimate(flops=flops, bytes_accessed=read, transcendentals=0)


def in_hbm(x):
    return pltpu.with_memory_space_constraint(x, pltpu.HBM)


def rows_of(t):
    return slice(t * TILE, (t + 1) * TILE)


def down_column(row):
    return jnp.transpose(jnp.broadcast_to(row, (TILE, TILE)))


def split(value):
    high = value.astype(jnp.bfloat16)
    low = (value - high.astype(jnp.float32)).astype(jnp.bfloat16)
    return high, low


def prep_kernel(tiles, shots, sections, assign_at, refl_at, up_at, down_at, src_at, first, second, *refs):
    assign, refl, up, down, src, pick, sems = refs
    depth = lax.axis_index("depth")
    loads = [
        pltpu.make_async_copy(assign_at, assign, sems.at[0]),
        pltpu.make_async_copy(refl_at, refl, sems.at[1]),
        pltpu.make_async_copy(src_at, src, sems.at[2]),
        pltpu.make_async_copy(up_at, up, sems.at[3]),
        pltpu.make_async_copy(down_at, down, sems.at[4]),
    ]
    for load in loads:
        load.start()
    loads[0].wait()

    @pl.when(depth == 0)
    def _():
        lane = lax.broadcasted_iota(jnp.int32, (8, TILE), 1)
        wanted = jnp.zeros((8, TILE), jnp.int32)
        for b in range(TILE // (2 * shots)):
            for i in range(shots):
                shot = assign[b * shots + i]
                at = b * 2 * shots + i
                wanted = jnp.where(lane == at, shot, wanted)
                wanted = jnp.where(lane == at + shots, shot + TILE // 2, wanted)
        source = lax.broadcasted_iota(jnp.int32, (TILE, TILE), 0)
        found = source == jnp.broadcast_to(wanted[0:1], (TILE, TILE))
        pick[...] = found.astype(jnp.float32).astype(jnp.bfloat16)

    for load in loads[1:]:
        load.wait()
    descends = depth < sections // 2

    def of_up(j):
        return -(down_column(refl[0:1, rows_of(j)]) * up[0, rows_of(j)])

    def of_down(j):
        return down_column(refl[0:1, rows_of(j)]) * down[0, rows_of(j)]

    for j in range(tiles):
        first[tiles * TILE + j : tiles * TILE + j + 1] = refl[0:1, rows_of(j)]

    @pl.when(descends & (depth > 0))
    def _():
        for j in range(tiles):
            first[rows_of(j)] = of_up(j)
            second[rows_of(j)] = of_down(j)

    @pl.when(jnp.logical_not(descends))
    def _():
        for j in range(tiles):
            first[rows_of(j)] = of_down(j)
            second[rows_of(j)] = of_up(j)

    @pl.when(depth == 0)
    def _():
        for j in range(tiles):
            x = src[rows_of(j)]
            high = x.astype(jnp.bfloat16)
            mid, low = split(x - high.astype(jnp.float32))
            entering = jnp.dot(low, pick[...], preferred_element_type=jnp.float32)
            entering += jnp.dot(mid, pick[...], preferred_element_type=jnp.float32)
            entering += jnp.dot(high, pick[...], preferred_element_type=jnp.float32)
            r = down_column(refl[0:1, rows_of(j)])
            first[rows_of(j)] = (1.0 + r) * entering + of_up(j)
            second[rows_of(j)] = of_down(j)


def pack_kernel(tiles, band, shift_at, tiles_at, out, shift, held, sems):
    loads = [pltpu.make_async_copy(shift_at, shift, sems.at[tiles])]
    loads += [pltpu.make_async_copy(tiles_at.at[0, j], held.at[j], sems.at[j]) for j in range(tiles)]
    for load in loads:
        load.start()
    loads[0].wait()
    for j in range(tiles):
        loads[1 + j].wait()
        move = shift[0, j]
        for k in range(band):
            high, low = split(held[j, k])
            slot = k + 1 + move
            out[j, slot, :, :TILE] = high
            out[j, slot, :, TILE:] = low
        zero = jnp.zeros(out.shape[2:], jnp.bfloat16)
        out[j, jnp.where(move >= 0, 0, band)] = zero
        out[j, jnp.where(move <= 0, band + 1, 1)] = zero


def doubled(tile):
    high, low = split(tile)
    line = jnp.concatenate([high, low], axis=1)
    return jnp.concatenate([line, line], axis=0)


def folded(value):
    return value[:, :TILE] + value[:, TILE:]


def lanes(rows):
    return lax.broadcasted_iota(jnp.int32, (rows, TILE), 1)


def turned(value):
    return pltpu.roll(value, HALF, 1)


def left_half(rows):
    return lanes(rows) < HALF


def halves_of(t):
    return slice(t * HALF, (t + 1) * HALF)


def part_tile(part, t):
    for chunk in part:
        count = chunk.shape[0] // HALF
        if t < count:
            return chunk[halves_of(t)]
        t -= count


def unpack_tile(part, t):
    tile = part_tile(part, t)
    return jnp.concatenate([tile, turned(tile)], axis=0)


def grouped(refs, layout):
    out = []
    for count in layout:
        out.append(refs[:count])
        refs = refs[count:]
    return out, refs


def stream_line(tile):
    rest = tile - tile.astype(jnp.bfloat16).astype(jnp.float32)
    line = jnp.where(left_half(TILE), tile, turned(rest)).astype(jnp.bfloat16)
    return jnp.concatenate([line, line], axis=0)


def merged(first, second):
    left = left_half(HALF)
    upper = jnp.where(left, first, turned(second))
    lower = jnp.where(left, turned(first), second)
    return jnp.concatenate([upper, lower], axis=0)


def parted(value):
    upper, lower = value[:HALF], value[HALF:]
    left = left_half(HALF)
    return jnp.where(left, upper, turned(lower)), jnp.where(left, turned(upper), lower)


def full_tile(field, t):
    if len(field) == 1:
        return field[0][0][rows_of(t)]
    return merged(*[part_tile(part, t) for part in field])


def aligned(j, size):
    return j * size if isinstance(j, int) else pl.multiple_of(j * size, size)


def choose(condition, this, that):
    if isinstance(condition, bool):
        return this if condition else that
    return jnp.where(condition, this, that)


def spread(field, scale, sign, tiles, narrow, mirrored, held):
    for t in range(tiles):
        tile = unpack_tile(field[0], t) if narrow else full_tile(field, t)
        if scale is not None:
            tile = tile * (1.0 + sign * scale[t])
        at = 2 * t * TILE
        if mirrored is not None:
            at = choose(mirrored, 2 * (tiles - 1 - t) * TILE, at)
            at = at if isinstance(at, int) else pl.multiple_of(at, 2 * TILE)
        held[pl.ds(at, 2 * TILE)] = stream_line(tile) if narrow else doubled(tile)


def product(packed, held, j, slots, narrow):
    value = jnp.dot(
        jnp.concatenate([packed[j, slot] for slot in slots], axis=1),
        held[: 2 * len(slots) * TILE],
        preferred_element_type=jnp.float32,
    )
    return value if narrow else folded(value)


def side_product(packed, held, tiles, jj, low_side, narrow):
    j = choose(low_side, tiles - 1 - jj, jj)
    slots = [choose(low_side, jj - t, 2 * tiles + t - jj) for t in range(jj + 1)]
    return j, product(packed, held, j, slots, narrow)


def when_active(step, sections, body):
    depth = lax.axis_index("depth")
    if step is None:
        body()
    else:
        pl.when((depth == step) | (depth == sections - 1 - step))(body)


def combined(value, shots):
    by_imag = value[TILE:]
    ahead = pltpu.roll(by_imag, TILE - shots, 1)
    behind = pltpu.roll(by_imag, shots, 1)
    return value[:TILE] + jnp.where(lax.rem(lanes(TILE), 2 * shots) < shots, -ahead, behind)


def scale_kernel(tiles, *refs):
    for source, out in zip(refs[:3], refs[3:]):
        for t in range(tiles):
            at = tiles * TILE + t
            out[t] = down_column(source[at : at + 1])


def mark_kernel(out):
    out[...] = jnp.zeros_like(out)


def inner_kernel(step, sections, tiles, layout, packed, *refs):
    narrow = bool(step) and len(layout) == 1
    own, refs = grouped(refs, layout)
    near, refs = grouped(refs, layout)
    scale, near_scale = refs[:2] if step else (None, None)
    total, held_own, held_near = refs[-3:]

    def body():
        sign = jnp.where(lax.axis_index("depth") == (step or 0), 1.0, -1.0)
        low_side = lax.rem(lax.axis_index("lat"), 2) == 1
        spread(own, scale, sign, tiles, narrow, None, held_own)
        spread(near, near_scale, sign, tiles, narrow, low_side, held_near)
        for j in range(tiles):
            total[j] = product(packed, held_own, j, range(tiles - j, 2 * tiles - j), narrow)
        for jj in range(tiles):
            j, value = side_product(packed, held_near, tiles, jj, low_side, narrow)
            total[j] = total[j] + value

    when_active(step or None, sections, body)


def outer_kernel(step, sections, lats, tiles, shots, layout, ends, late, packed, total, *refs):
    narrow = bool(step) and not ends
    parts = len(layout)
    far, refs = grouped(refs, layout)
    scale, base = None, None
    if step:
        scale, base, refs = refs[0], refs[1 : 1 + parts], refs[1 + parts :]
    if ends:
        _, _, result_down, result_up, held, leaving, sems = refs
    else:
        outs, held = refs[:-1], refs[-1]
    lat = lax.axis_index("lat")
    depth = lax.axis_index("depth")
    low_side = lax.rem(lat, 2) == 0
    has_far = (lat > 0) & (lat < lats - 1)

    def body():
        sign = jnp.where(depth == (step or 0), 1.0, -1.0)

        def copy_of(j, result):
            at = pl.ds(pl.multiple_of(j * TILE, TILE), TILE)
            return pltpu.make_async_copy(leaving.at[at], result.at[0, at], sems.at[j])

        def store(j, value):
            if len(outs) == 1:
                outs[0][pl.ds(aligned(j, HALF), HALF)] = value
                return
            for out in outs:
                count = out.shape[0] // HALF
                if 0 <= j < count:
                    out[halves_of(j)] = value
                j -= count

        def finish(j, value):
            at = pl.ds(aligned(j, HALF), HALF)
            if narrow:
                value = combined(value + turned(value), shots)
                store(j, jnp.where(left_half(HALF), value[:HALF], value[HALF:]) + base[0][at])
                return
            value = combined(value, shots)
            if ends:
                value = value + merged(*[part[at] for part in base])
                leaving[pl.ds(pl.multiple_of(j * TILE, TILE), TILE)] = value
                pl.when(depth == step)(lambda: copy_of(j, result_down).start())
                pl.when(depth != step)(lambda: copy_of(j, result_up).start())
                return
            for out, part in zip(outs, parted(value)):
                out[at] = part

        def with_far(low):
            spread(far, scale, sign, tiles, narrow, low, held)
            for jj in range(tiles):
                j, value = side_product(packed, held, tiles, jj, low, narrow)
                finish(j, total[j] + value)

        if narrow and len(outs) > 1:
            pl.when(has_far & low_side)(lambda: with_far(True))
            pl.when(has_far & jnp.logical_not(low_side))(lambda: with_far(False))
        else:
            pl.when(has_far)(lambda: with_far(low_side))

        @pl.when(jnp.logical_not(has_far))
        def _():
            for j in range(tiles):
                finish(j, total[j])

        if ends:

            def wait_all(result):
                for j in range(tiles):
                    copy_of(j, result).wait()

            pl.when(depth == step)(lambda: wait_all(result_down))
            pl.when(depth != step)(lambda: wait_all(result_up))

    if late:
        pl.when((depth > 0) & (depth < sections - 1))(body)
    else:
        when_active(step, sections, body)


def keep_kernel(sections, tiles, steps, layout, *refs):
    result_down, result_up, whole, sems = refs[-4:]
    fields, _ = grouped(refs, layout)
    depth = lax.axis_index("depth")

    def put(first, second, result):
        for j in range(tiles):
            whole[rows_of(j)] = merged(part_tile(first, j), part_tile(second, j))
        copy = pltpu.make_async_copy(whole, result.at[0], sems)
        copy.start()
        copy.wait()

    for i, step in enumerate(steps):
        first, second = fields[2 * i : 2 * i + 2]
        pl.when(depth == step)(functools.partial(put, first, second, result_down))
        pl.when(depth == sections - 1 - step)(functools.partial(put, first, second, result_up))


def shards(sections, lats, operator, band_shift, reflectivity, up_stored, down_stored, sources, assignment):
    tiles, band = operator.shape[1], operator.shape[2]
    _, columns = sources.shape
    shots = columns // 4
    rows = tiles * TILE
    if sections % 2 or lats % 2 or tiles != band // 2 + 1 or columns != TILE or tiles != sum(CHUNKS):
        raise ValueError("unsupported sizes")

    def move(x, partner):
        pairs = []
        for d in range(sections):
            for l in range(lats):
                e, m = partner(d, l)
                pairs.append((d * lats + l, e * lats + m))
        return lax.ppermute(x, ("depth", "lat"), pairs)

    def near_of(d, l):
        return d, l ^ 1

    def far_of(spare, d, l):
        m = l + 1 if l % 2 else l - 1
        return (d, m) if 0 <= m < lats else (spare(d), l)

    def across(step, d, l):
        for low in (step, sections - 2 - step):
            if d == low:
                return low + 1, l
            if d == low + 1:
                return low, l
        return near_of(d, l)

    def halo(field, spare):
        near = move(field, near_of)
        return near, move(field, functools.partial(far_of, spare))

    def next_door(d):
        return (d + sections // 2) % sections

    first, second = call(
        functools.partial(prep_kernel, tiles, shots, sections),
        out_shape=[f32(rows + 8, columns), f32(rows, columns)],
        in_specs=[spec(pltpu.HBM)] * 5,
        out_specs=[spec(VMEM)] * 2,
        scratch_shapes=[
            pltpu.SMEM(assignment.shape, jnp.int32),
            VMEM(reflectivity.shape, jnp.float32),
            VMEM(up_stored.shape, jnp.float32),
            VMEM(down_stored.shape, jnp.float32),
            VMEM(sources.shape, jnp.float32),
            VMEM((TILE, TILE), jnp.bfloat16),
            pltpu.SemaphoreType.DMA((5,)),
        ],
        compiler_params=params(),
        cost_estimate=cost(10**7, 5 * rows * columns * 4),
    )(*map(in_hbm, (assignment, reflectivity, up_stored, down_stored, sources)))

    packed = call(
        functools.partial(pack_kernel, tiles, band),
        out_shape=jax.ShapeDtypeStruct((tiles, band + 2, 2 * TILE, 2 * TILE), jnp.bfloat16),
        in_specs=[spec(pltpu.HBM)] * 2,
        out_specs=spec(VMEM),
        scratch_shapes=[
            pltpu.SMEM(band_shift.shape, jnp.int32),
            VMEM(operator.shape[1:], jnp.float32),
            pltpu.SemaphoreType.DMA((tiles + 1,)),
        ],
        compiler_params=params(),
        cost_estimate=cost(10**7, 2 * operator.size * 4),
    )(in_hbm(band_shift), in_hbm(operator))

    square = f32(tiles, TILE, columns)
    half = f32(rows // STREAMS, columns)
    result = [f32(1, rows, columns)] * 2

    def held(narrow):
        return VMEM((tiles * 2 * TILE, TILE if narrow else 2 * TILE), jnp.bfloat16)

    def inner(step, own, near, *scales):
        args = [packed, *flat(own), *flat(near), *scales]
        return call(
            functools.partial(inner_kernel, step, sections, tiles, [len(part) for part in own]),
            out_shape=f32(tiles, 2 * TILE, columns),
            in_specs=[spec(VMEM)] * len(args),
            out_specs=spec(VMEM),
            scratch_shapes=[held(step and len(own) == 1)] * 2,
            compiler_params=params(),
            cost_estimate=cost(2 * 40 * 256**3, 8 * 2**20),
        )(*args)

    def outer(step, total, far, *more, shapes, kept=(), late=False):
        ends = bool(kept)
        args = [packed, total, *flat(far), *more]
        count = len(args)
        scratch = [held(step and not ends)]
        if ends:
            scratch += [VMEM((rows, columns), jnp.float32), pltpu.SemaphoreType.DMA((tiles,))]
        return call(
            functools.partial(
                outer_kernel, step, sections, lats, tiles, shots, [len(part) for part in far], ends, late
            ),
            out_shape=shapes,
            in_specs=[spec(VMEM)] * count + [spec(pl.ANY)] * len(kept),
            out_specs=[spec(pl.ANY if ends else VMEM)] * len(shapes),
            scratch_shapes=scratch,
            input_output_aliases={count: 0, count + 1: 1} if ends else {},
            compiler_params=params(),
            cost_estimate=cost(2 * 15 * 256**3, 4 * 2**20),
        )(*args, *kept)

    def keep(steps, kept=()):
        parts = [part for step in steps for part in fields[step]]
        args = flat(parts)
        count = len(args)
        return call(
            functools.partial(keep_kernel, sections, tiles, steps, [len(part) for part in parts]),
            out_shape=result,
            in_specs=[spec(VMEM)] * count + [spec(pl.ANY)] * len(kept),
            out_specs=[spec(pl.ANY)] * 2,
            scratch_shapes=[VMEM((rows, columns), jnp.float32), pltpu.SemaphoreType.DMA(())],
            input_output_aliases={count: 0, count + 1: 1} if kept else {},
            compiler_params=params(),
            cost_estimate=cost(0, 4 * rows * columns * 4),
        )(*args, *kept)

    def flat(parts):
        return [chunk for part in parts for chunk in part]

    def cross(step, field):
        def one(chunk):
            return move(chunk, functools.partial(across, step))

        return [[one(chunk) for chunk in part] for part in field]

    first_near, first_far = halo(first, next_door)
    total = inner(0, [[first]], [[first_near]])
    field = outer(0, total, [[first_far]], shapes=[half] * STREAMS)
    fields = [[[part] for part in field]]
    first_base = outer(0, total, [[first_far]], shapes=[half] * STREAMS, late=True)
    arrived = cross(0, fields[0])

    second, *_ = lax.optimization_barrier((second, *field))
    near, far = halo(second, next_door)
    own_scale, near_scale, far_scale = call(
        functools.partial(scale_kernel, tiles),
        out_shape=[square] * 3,
        in_specs=[spec(VMEM)] * 3,
        out_specs=[spec(VMEM)] * 3,
        compiler_params=params(),
        cost_estimate=cost(10**6, 4 * rows * columns * 4),
    )(first, first_near, first_far)
    total = inner(None, [[second]], [[near]])
    second_base = outer(None, total, [[far]], shapes=[half] * STREAMS)

    middle = sections // 2
    for step in range(1, sections):
        bases = first_base if step < middle else second_base
        nears, fars = [], []
        for part in arrived:
            halos = [halo(chunk, next_door) for chunk in part]
            nears.append([near for near, _ in halos])
            fars.append([far for _, far in halos])
        if step == sections - 1:
            marks = [
                call(
                    mark_kernel,
                    out_shape=f32(8, columns),
                    in_specs=[],
                    out_specs=spec(VMEM),
                    compiler_params=pltpu.CompilerParams(vmem_limit_bytes=LIMIT, has_side_effects=True),
                    cost_estimate=cost(0, 1),
                )()
                for _ in range(STREAMS)
            ]
            total = inner(step, arrived, nears, own_scale, near_scale, *marks)
            kept = keep(range(middle - 1)) if middle > 1 else ()
            kept = keep(range(middle - 1, step), kept)
            return tuple(outer(step, total, fars, far_scale, *bases, shapes=result, kept=kept))
        field = []
        for q in range(STREAMS):
            total = inner(step, [arrived[q]], [nears[q]], own_scale, near_scale)
            shapes = [half]
            if step == sections - 2 and q == STREAMS - 1:
                shapes = [f32(count * HALF, columns) for count in CHUNKS]
            field.append(outer(step, total, [fars[q]], far_scale, bases[q], shapes=shapes))
        fields.append(field)
        arrived = cross(step, field)


def solution(mesh):
    return jax.shard_map(
        functools.partial(shards, mesh.shape["depth"], mesh.shape["lat"]),
        mesh=mesh,
        in_specs=(
            P("depth", "lat", None, None, None),
            P("depth", "lat"),
            P("depth", "lat"),
            P("depth", "lat", None),
            P("depth", "lat", None),
            P("lat", None),
            P(),
        ),
        out_specs=(P("depth", "lat", None), P("depth", "lat", None)),
        check_vma=False,
    )
```

```python
import functools

import jax
import jax.numpy as jnp
from jax import lax
from jax.experimental import pallas as pl
from jax.experimental.pallas import tpu as pltpu
from jax.sharding import PartitionSpec as P


TILE = 128
HALF = TILE // 2
VMEM = pltpu.VMEM
LIMIT = 16 * 2**20
STREAMS = 2
CHUNKS = (2, 3)


def spec(space):
    return pl.BlockSpec(memory_space=space)


def f32(*shape):
    return jax.ShapeDtypeStruct(shape, jnp.float32)


def call(kernel, **kwargs):
    return pl.pallas_call(kernel, **kwargs)


def params(limit=LIMIT):
    return pltpu.CompilerParams(vmem_limit_bytes=limit)


def cost(flops, read):
    return pl.CostEstimate(flops=flops, bytes_accessed=read, transcendentals=0)


def in_hbm(x):
    return pltpu.with_memory_space_constraint(x, pltpu.HBM)


def rows_of(t):
    return slice(t * TILE, (t + 1) * TILE)


def down_column(row):
    return jnp.transpose(jnp.broadcast_to(row, (TILE, TILE)))


def split(value):
    high = value.astype(jnp.bfloat16)
    low = (value - high.astype(jnp.float32)).astype(jnp.bfloat16)
    return high, low


def prep_kernel(tiles, shots, sections, assign_at, refl_at, up_at, down_at, src_at, first, second, *refs):
    assign, refl, up, down, src, pick, sems = refs
    depth = lax.axis_index("depth")
    loads = [
        pltpu.make_async_copy(assign_at, assign, sems.at[0]),
        pltpu.make_async_copy(refl_at, refl, sems.at[1]),
        pltpu.make_async_copy(src_at, src, sems.at[2]),
        pltpu.make_async_copy(up_at, up, sems.at[3]),
        pltpu.make_async_copy(down_at, down, sems.at[4]),
    ]
    for load in loads:
        load.start()
    loads[0].wait()

    @pl.when(depth == 0)
    def _():
        lane = lax.broadcasted_iota(jnp.int32, (8, TILE), 1)
        wanted = jnp.zeros((8, TILE), jnp.int32)
        for b in range(TILE // (2 * shots)):
            for i in range(shots):
                shot = assign[b * shots + i]
                at = b * 2 * shots + i
                wanted = jnp.where(lane == at, shot, wanted)
                wanted = jnp.where(lane == at + shots, shot + TILE // 2, wanted)
        source = lax.broadcasted_iota(jnp.int32, (TILE, TILE), 0)
        found = source == jnp.broadcast_to(wanted[0:1], (TILE, TILE))
        pick[...] = found.astype(jnp.float32).astype(jnp.bfloat16)

    for load in loads[1:]:
        load.wait()
    descends = depth < sections // 2

    def of_up(j):
        return -(down_column(refl[0:1, rows_of(j)]) * up[0, rows_of(j)])

    def of_down(j):
        return down_column(refl[0:1, rows_of(j)]) * down[0, rows_of(j)]

    for j in range(tiles):
        first[tiles * TILE + j : tiles * TILE + j + 1] = refl[0:1, rows_of(j)]

    @pl.when(descends & (depth > 0))
    def _():
        for j in range(tiles):
            first[rows_of(j)] = of_up(j)
            second[rows_of(j)] = of_down(j)

    @pl.when(jnp.logical_not(descends))
    def _():
        for j in range(tiles):
            first[rows_of(j)] = of_down(j)
            second[rows_of(j)] = of_up(j)

    @pl.when(depth == 0)
    def _():
        for j in range(tiles):
            x = src[rows_of(j)]
            high = x.astype(jnp.bfloat16)
            mid, low = split(x - high.astype(jnp.float32))
            entering = jnp.dot(low, pick[...], preferred_element_type=jnp.float32)
            entering += jnp.dot(mid, pick[...], preferred_element_type=jnp.float32)
            entering += jnp.dot(high, pick[...], preferred_element_type=jnp.float32)
            r = down_column(refl[0:1, rows_of(j)])
            first[rows_of(j)] = (1.0 + r) * entering + of_up(j)
            second[rows_of(j)] = of_down(j)


def pack_kernel(tiles, band, shift_at, tiles_at, out, shift, held, sems):
    loads = [pltpu.make_async_copy(shift_at, shift, sems.at[tiles * (band // 3)])]
    loads += [
        pltpu.make_async_copy(tiles_at.at[0, j, pl.ds(3 * k, 3)], held.at[j, pl.ds(3 * k, 3)], sems.at[j * (band // 3) + k])
        for j in range(tiles)
        for k in range(band // 3)
    ]
    for load in loads:
        load.start()
    loads[0].wait()
    for j in range(tiles):
        move = shift[0, j]
        for k in range(band):
            if k % 3 == 0:
                loads[1 + j * (band // 3) + k // 3].wait()
            high, low = split(held[j, k])
            slot = k + 1 + move
            out[j, slot, :, :TILE] = high
            out[j, slot, :, TILE:] = low
        zero = jnp.zeros(out.shape[2:], jnp.bfloat16)
        out[j, jnp.where(move >= 0, 0, band)] = zero
        out[j, jnp.where(move <= 0, band + 1, 1)] = zero


def doubled(tile):
    high, low = split(tile)
    line = jnp.concatenate([high, low], axis=1)
    return jnp.concatenate([line, line], axis=0)


def folded(value):
    return value[:, :TILE] + value[:, TILE:]


def lanes(rows):
    return lax.broadcasted_iota(jnp.int32, (rows, TILE), 1)


def turned(value):
    return pltpu.roll(value, HALF, 1)


def left_half(rows):
    return lanes(rows) < HALF


def halves_of(t):
    return slice(t * HALF, (t + 1) * HALF)


def part_tile(part, t):
    for chunk in part:
        count = chunk.shape[0] // HALF
        if t < count:
            return chunk[halves_of(t)]
        t -= count


def unpack_tile(part, t):
    tile = part_tile(part, t)
    return jnp.concatenate([tile, turned(tile)], axis=0)


def grouped(refs, layout):
    out = []
    for count in layout:
        out.append(refs[:count])
        refs = refs[count:]
    return out, refs


def stream_line(tile):
    rest = tile - tile.astype(jnp.bfloat16).astype(jnp.float32)
    line = jnp.where(left_half(TILE), tile, turned(rest)).astype(jnp.bfloat16)
    return jnp.concatenate([line, line], axis=0)


def merged(first, second):
    left = left_half(HALF)
    upper = jnp.where(left, first, turned(second))
    lower = jnp.where(left, turned(first), second)
    return jnp.concatenate([upper, lower], axis=0)


def parted(value):
    upper, lower = value[:HALF], value[HALF:]
    left = left_half(HALF)
    return jnp.where(left, upper, turned(lower)), jnp.where(left, turned(upper), lower)


def full_tile(field, t):
    if len(field) == 1:
        return field[0][0][rows_of(t)]
    return merged(*[part_tile(part, t) for part in field])


def aligned(j, size):
    return j * size if isinstance(j, int) else pl.multiple_of(j * size, size)


def choose(condition, this, that):
    if isinstance(condition, bool):
        return this if condition else that
    return jnp.where(condition, this, that)


def spread(field, scale, sign, tiles, narrow, mirrored, held):
    for t in range(tiles):
        tile = unpack_tile(field[0], t) if narrow else full_tile(field, t)
        if scale is not None:
            tile = tile * (1.0 + sign * scale[t])
        at = 2 * t * TILE
        if mirrored is not None:
            at = choose(mirrored, 2 * (tiles - 1 - t) * TILE, at)
            at = at if isinstance(at, int) else pl.multiple_of(at, 2 * TILE)
        held[pl.ds(at, 2 * TILE)] = stream_line(tile) if narrow else doubled(tile)


def product(packed, held, j, slots, narrow):
    value = jnp.dot(
        jnp.concatenate([packed[j, slot] for slot in slots], axis=1),
        held[: 2 * len(slots) * TILE],
        preferred_element_type=jnp.float32,
    )
    return value if narrow else folded(value)


def side_product(packed, held, tiles, jj, low_side, narrow):
    j = choose(low_side, tiles - 1 - jj, jj)
    slots = [choose(low_side, jj - t, 2 * tiles + t - jj) for t in range(jj + 1)]
    return j, product(packed, held, j, slots, narrow)


def when_active(step, sections, body):
    depth = lax.axis_index("depth")
    if step is None:
        body()
    else:
        pl.when((depth == step) | (depth == sections - 1 - step))(body)


def combined(value, shots):
    by_imag = value[TILE:]
    ahead = pltpu.roll(by_imag, TILE - shots, 1)
    behind = pltpu.roll(by_imag, shots, 1)
    return value[:TILE] + jnp.where(lax.rem(lanes(TILE), 2 * shots) < shots, -ahead, behind)


def scale_kernel(tiles, *refs):
    for source, out in zip(refs[:3], refs[3:]):
        for t in range(tiles):
            at = tiles * TILE + t
            out[t] = down_column(source[at : at + 1])


def mark_kernel(out):
    out[...] = jnp.zeros_like(out)


def inner_kernel(step, sections, tiles, layout, packed, *refs):
    narrow = bool(step) and len(layout) == 1
    own, refs = grouped(refs, layout)
    near, refs = grouped(refs, layout)
    scale, near_scale = refs[:2] if step else (None, None)
    total, held_own, held_near = refs[-3:]

    def body():
        sign = jnp.where(lax.axis_index("depth") == (step or 0), 1.0, -1.0)
        low_side = lax.rem(lax.axis_index("lat"), 2) == 1
        spread(own, scale, sign, tiles, narrow, None, held_own)
        spread(near, near_scale, sign, tiles, narrow, low_side, held_near)
        for j in range(tiles):
            total[j] = product(packed, held_own, j, range(tiles - j, 2 * tiles - j), narrow)
        for jj in range(tiles):
            j, value = side_product(packed, held_near, tiles, jj, low_side, narrow)
            total[j] = total[j] + value

    when_active(step or None, sections, body)


def outer_kernel(step, sections, lats, tiles, shots, layout, ends, late, packed, total, *refs):
    narrow = bool(step) and not ends
    parts = len(layout)
    far, refs = grouped(refs, layout)
    scale, base = None, None
    if step:
        scale, base, refs = refs[0], refs[1 : 1 + parts], refs[1 + parts :]
    if ends:
        _, _, result_down, result_up, held, leaving, sems = refs
    else:
        outs, held = refs[:-1], refs[-1]
    lat = lax.axis_index("lat")
    depth = lax.axis_index("depth")
    low_side = lax.rem(lat, 2) == 0
    has_far = (lat > 0) & (lat < lats - 1)

    def body():
        sign = jnp.where(depth == (step or 0), 1.0, -1.0)

        def copy_of(j, result):
            at = pl.ds(pl.multiple_of(j * TILE, TILE), TILE)
            return pltpu.make_async_copy(leaving.at[at], result.at[0, at], sems.at[j])

        def store(j, value):
            if len(outs) == 1:
                outs[0][pl.ds(aligned(j, HALF), HALF)] = value
                return
            for out in outs:
                count = out.shape[0] // HALF
                if 0 <= j < count:
                    out[halves_of(j)] = value
                j -= count

        def finish(j, value):
            at = pl.ds(aligned(j, HALF), HALF)
            if narrow:
                value = combined(value + turned(value), shots)
                store(j, jnp.where(left_half(HALF), value[:HALF], value[HALF:]) + base[0][at])
                return
            value = combined(value, shots)
            if ends:
                value = value + merged(*[part[at] for part in base])
                leaving[pl.ds(pl.multiple_of(j * TILE, TILE), TILE)] = value
                pl.when(depth == step)(lambda: copy_of(j, result_down).start())
                pl.when(depth != step)(lambda: copy_of(j, result_up).start())
                return
            for out, part in zip(outs, parted(value)):
                out[at] = part

        def with_far(low):
            spread(far, scale, sign, tiles, narrow, low, held)
            for jj in range(tiles):
                j, value = side_product(packed, held, tiles, jj, low, narrow)
                finish(j, total[j] + value)

        if narrow and len(outs) > 1:
            pl.when(has_far & low_side)(lambda: with_far(True))
            pl.when(has_far & jnp.logical_not(low_side))(lambda: with_far(False))
        else:
            pl.when(has_far)(lambda: with_far(low_side))

        @pl.when(jnp.logical_not(has_far))
        def _():
            for j in range(tiles):
                finish(j, total[j])

        if ends:

            def wait_all(result):
                for j in range(tiles):
                    copy_of(j, result).wait()

            pl.when(depth == step)(lambda: wait_all(result_down))
            pl.when(depth != step)(lambda: wait_all(result_up))

    if late:
        pl.when((depth > 0) & (depth < sections - 1))(body)
    else:
        when_active(step, sections, body)


def keep_kernel(sections, tiles, steps, layout, *refs):
    result_down, result_up, whole, sems = refs[-4:]
    fields, _ = grouped(refs, layout)
    depth = lax.axis_index("depth")

    def put(first, second, result):
        for j in range(tiles):
            whole[rows_of(j)] = merged(part_tile(first, j), part_tile(second, j))
        copy = pltpu.make_async_copy(whole, result.at[0], sems)
        copy.start()
        copy.wait()

    for i, step in enumerate(steps):
        first, second = fields[2 * i : 2 * i + 2]
        pl.when(depth == step)(functools.partial(put, first, second, result_down))
        pl.when(depth == sections - 1 - step)(functools.partial(put, first, second, result_up))


def shards(sections, lats, operator, band_shift, reflectivity, up_stored, down_stored, sources, assignment):
    tiles, band = operator.shape[1], operator.shape[2]
    _, columns = sources.shape
    shots = columns // 4
    rows = tiles * TILE
    if sections % 2 or lats % 2 or tiles != band // 2 + 1 or columns != TILE or tiles != sum(CHUNKS):
        raise ValueError("unsupported sizes")

    def move(x, partner):
        pairs = []
        for d in range(sections):
            for l in range(lats):
                e, m = partner(d, l)
                pairs.append((d * lats + l, e * lats + m))
        return lax.ppermute(x, ("depth", "lat"), pairs)

    def near_of(d, l):
        return d, l ^ 1

    def far_of(spare, d, l):
        m = l + 1 if l % 2 else l - 1
        return (d, m) if 0 <= m < lats else (spare(d), l)

    def across(step, d, l):
        for low in (step, sections - 2 - step):
            if d == low:
                return low + 1, l
            if d == low + 1:
                return low, l
        return near_of(d, l)

    def halo(field, spare):
        near = move(field, near_of)
        return near, move(field, functools.partial(far_of, spare))

    def next_door(d):
        return (d + sections // 2) % sections

    first, second = call(
        functools.partial(prep_kernel, tiles, shots, sections),
        out_shape=[f32(rows + 8, columns), f32(rows, columns)],
        in_specs=[spec(pltpu.HBM)] * 5,
        out_specs=[spec(VMEM)] * 2,
        scratch_shapes=[
            pltpu.SMEM(assignment.shape, jnp.int32),
            VMEM(reflectivity.shape, jnp.float32),
            VMEM(up_stored.shape, jnp.float32),
            VMEM(down_stored.shape, jnp.float32),
            VMEM(sources.shape, jnp.float32),
            VMEM((TILE, TILE), jnp.bfloat16),
            pltpu.SemaphoreType.DMA((5,)),
        ],
        compiler_params=params(),
        cost_estimate=cost(10**7, 5 * rows * columns * 4),
    )(*map(in_hbm, (assignment, reflectivity, up_stored, down_stored, sources)))

    packed = call(
        functools.partial(pack_kernel, tiles, band),
        out_shape=jax.ShapeDtypeStruct((tiles, band + 2, 2 * TILE, 2 * TILE), jnp.bfloat16),
        in_specs=[spec(pltpu.HBM)] * 2,
        out_specs=spec(VMEM),
        scratch_shapes=[
            pltpu.SMEM(band_shift.shape, jnp.int32),
            VMEM(operator.shape[1:], jnp.float32),
            pltpu.SemaphoreType.DMA((tiles * (band // 3) + 1,)),
        ],
        compiler_params=params(),
        cost_estimate=cost(10**7, 2 * operator.size * 4),
    )(in_hbm(band_shift), in_hbm(operator))

    square = f32(tiles, TILE, columns)
    half = f32(rows // STREAMS, columns)
    result = [f32(1, rows, columns)] * 2

    def held(narrow):
        return VMEM((tiles * 2 * TILE, TILE if narrow else 2 * TILE), jnp.bfloat16)

    def inner(step, own, near, *scales):
        args = [packed, *flat(own), *flat(near), *scales]
        return call(
            functools.partial(inner_kernel, step, sections, tiles, [len(part) for part in own]),
            out_shape=f32(tiles, 2 * TILE, columns),
            in_specs=[spec(VMEM)] * len(args),
            out_specs=spec(VMEM),
            scratch_shapes=[held(step and len(own) == 1)] * 2,
            compiler_params=params(),
            cost_estimate=cost(2 * 40 * 256**3, 8 * 2**20),
        )(*args)

    def outer(step, total, far, *more, shapes, kept=(), late=False):
        ends = bool(kept)
        args = [packed, total, *flat(far), *more]
        count = len(args)
        scratch = [held(step and not ends)]
        if ends:
            scratch += [VMEM((rows, columns), jnp.float32), pltpu.SemaphoreType.DMA((tiles,))]
        return call(
            functools.partial(
                outer_kernel, step, sections, lats, tiles, shots, [len(part) for part in far], ends, late
            ),
            out_shape=shapes,
            in_specs=[spec(VMEM)] * count + [spec(pl.ANY)] * len(kept),
            out_specs=[spec(pl.ANY if ends else VMEM)] * len(shapes),
            scratch_shapes=scratch,
            input_output_aliases={count: 0, count + 1: 1} if ends else {},
            compiler_params=params(),
            cost_estimate=cost(2 * 15 * 256**3, 4 * 2**20),
        )(*args, *kept)

    def keep(steps, kept=()):
        parts = [part for step in steps for part in fields[step]]
        args = flat(parts)
        count = len(args)
        return call(
            functools.partial(keep_kernel, sections, tiles, steps, [len(part) for part in parts]),
            out_shape=result,
            in_specs=[spec(VMEM)] * count + [spec(pl.ANY)] * len(kept),
            out_specs=[spec(pl.ANY)] * 2,
            scratch_shapes=[VMEM((rows, columns), jnp.float32), pltpu.SemaphoreType.DMA(())],
            input_output_aliases={count: 0, count + 1: 1} if kept else {},
            compiler_params=params(),
            cost_estimate=cost(0, 4 * rows * columns * 4),
        )(*args, *kept)

    def flat(parts):
        return [chunk for part in parts for chunk in part]

    def cross(step, field):
        def one(chunk):
            return move(chunk, functools.partial(across, step))

        return [[one(chunk) for chunk in part] for part in field]

    first_near, first_far = halo(first, next_door)
    total = inner(0, [[first]], [[first_near]])
    field = outer(0, total, [[first_far]], shapes=[half] * STREAMS)
    fields = [[[part] for part in field]]
    first_base = outer(0, total, [[first_far]], shapes=[half] * STREAMS, late=True)
    arrived = cross(0, fields[0])

    second, *_ = lax.optimization_barrier((second, *field))
    near, far = halo(second, next_door)
    own_scale, near_scale, far_scale = call(
        functools.partial(scale_kernel, tiles),
        out_shape=[square] * 3,
        in_specs=[spec(VMEM)] * 3,
        out_specs=[spec(VMEM)] * 3,
        compiler_params=params(),
        cost_estimate=cost(10**6, 4 * rows * columns * 4),
    )(first, first_near, first_far)
    total = inner(None, [[second]], [[near]])
    second_base = outer(None, total, [[far]], shapes=[half] * STREAMS)

    middle = sections // 2
    for step in range(1, sections):
        bases = first_base if step < middle else second_base
        nears, fars = [], []
        for part in arrived:
            halos = [halo(chunk, next_door) for chunk in part]
            nears.append([near for near, _ in halos])
            fars.append([far for _, far in halos])
        if step == sections - 1:
            marks = [
                call(
                    mark_kernel,
                    out_shape=f32(8, columns),
                    in_specs=[],
                    out_specs=spec(VMEM),
                    compiler_params=pltpu.CompilerParams(vmem_limit_bytes=LIMIT, has_side_effects=True),
                    cost_estimate=cost(0, 1),
                )()
                for _ in range(STREAMS)
            ]
            total = inner(step, arrived, nears, own_scale, near_scale, *marks)
            kept = keep(range(middle - 1)) if middle > 1 else ()
            kept = keep(range(middle - 1, step), kept)
            return tuple(outer(step, total, fars, far_scale, *bases, shapes=result, kept=kept))
        field = []
        for q in range(STREAMS):
            total = inner(step, [arrived[q]], [nears[q]], own_scale, near_scale)
            shapes = [half]
            if step == sections - 2 and q == STREAMS - 1:
                shapes = [f32(count * HALF, columns) for count in CHUNKS]
            field.append(outer(step, total, [fars[q]], far_scale, bases[q], shapes=shapes))
        fields.append(field)
        arrived = cross(step, field)


def solution(mesh):
    return jax.shard_map(
        functools.partial(shards, mesh.shape["depth"], mesh.shape["lat"]),
        mesh=mesh,
        in_specs=(
            P("depth", "lat", None, None, None),
            P("depth", "lat"),
            P("depth", "lat"),
            P("depth", "lat", None),
            P("depth", "lat", None),
            P("lat", None),
            P(),
        ),
        out_specs=(P("depth", "lat", None), P("depth", "lat", None)),
        check_vma=False,
    )
```
